32 devices in a mesh: row: 8 (over z, y), col: 4 (over x, core).
Axes of the slice: x: 2, y: 2, z: 4, core: 2. Of those that a mesh axis runs over, the one named last changes fastest.
Arguments:
- factor: float32 [2, 1024, 1024], P(None, 'row', 'col'), may hold values from -0.125 to 0.125
- lower_inverse: float32 [2, 512, 1024], P(None, None, 'row'), may hold values from -1 to 2
- upper_inverse: float32 [2, 512, 1024], P(None, None, 'row'), may hold values from -1 to 2
- krylov_block: float32 [2, 16, 1024], P(None, None, 'row'), may hold values from -6 to 6
- basis: float32 [2, 64, 1024], P(None, None, 'row'), may hold values from -0.125 to 0.125
Outputs:
- projected: float32 [2, 16, 1024], P(None, None, 'row')
- coefficients: float32 [2, 64, 16], replicated
The draws below stay inside these ranges and needn't reach their ends.
All inputs are finite; a program needn't handle non-finite values.
Results may differ from the reference program's by a relative error of at most 0.00012.
Values sent between devices are 32-bit elements; how exact they have to be, the bound alone decides.
A program may use at most 64 MiB of HBM per device.

```python
import jax
import jax.numpy as jnp
from jax import lax

TILE = 512
NRHS = 16
NB = 64
KT = 2
N = 1024


def tile_inverse(key):
    cols = jnp.arange(N) % TILE
    ident = (jnp.arange(TILE)[:, None] == cols[None, :]).astype(jnp.float32)
    noise = jax.random.normal(key, (2, TILE, N), jnp.float32) * (0.3 / jnp.sqrt(jnp.float32(TILE)))
    noise = jnp.clip(noise, -0.2, 0.2)
    return jnp.stack([ident + noise[0], noise[1]])


def draw_lower_inverse(key, part):
    return tile_inverse(jax.random.fold_in(key, 101))


def draw_upper_inverse(key, part):
    return tile_inverse(jax.random.fold_in(key, 202))


def steps_of(rng, shape, split, least, top_value):
    def one(dim, shards_of):
        heights = jax.random.uniform(jax.random.fold_in(jax.random.fold_in(rng, 6), dim), (shards_of,), jnp.float32, least / len(split), top_value / len(split))
        return jnp.repeat(jnp.exp(heights), shape[dim] // shards_of).reshape((-1,) + (1,) * (len(shape) - dim - 1))

    factor_of = one(*split[0])
    for cut in split[1:]:
        factor_of = factor_of * one(*cut)
    return factor_of


def gaussian(stream_key, dims, scale, bound, cuts=(), kind=jnp.bfloat16):
    loudness = steps_of(stream_key, dims, cuts, -0.22, 0.18) if cuts else 1.0
    values = jax.random.normal(stream_key, dims, jnp.float32) * scale * loudness
    return jnp.minimum(jnp.maximum(values, -bound), bound).astype(kind)


def setup_inputs(seed: int = 0) -> dict:
    key_of = jax.random.split(jax.random.key(seed), 6)
    factor = gaussian(key_of[0], (2, N, N), (2 * N) ** -0.5, 0.125, ((1, 8), (2, 4)), jnp.float32)
    lower_inverse = draw_lower_inverse(jax.random.fold_in(key_of[5], 71), 0)
    upper_inverse = draw_upper_inverse(jax.random.fold_in(key_of[5], 71), 0)
    krylov_block = gaussian(key_of[3], (2, NRHS, N), 1.0, 6.0, ((2, 8),), jnp.float32)
    basis = gaussian(key_of[4], (2, NB, N), (2 * N) ** -0.5, 0.125, ((2, 8),), jnp.float32)
    return {"factor": factor, "lower_inverse": lower_inverse, "upper_inverse": upper_inverse, "krylov_block": krylov_block, "basis": basis}


def real_dot(left, right):
    return jnp.dot(left, right, preferred_element_type=jnp.float32, precision=lax.Precision.HIGHEST)


def apply_tile(matrix, vectors):
    real_part = real_dot(vectors[0], matrix[0].T) - real_dot(vectors[1], matrix[1].T)
    imag_part = real_dot(vectors[0], matrix[1].T) + real_dot(vectors[1], matrix[0].T)
    return jnp.stack([real_part, imag_part])


def herm_dot(basis_part, vectors):
    real_part = real_dot(basis_part[0], vectors[0].T) + real_dot(basis_part[1], vectors[1].T)
    imag_part = real_dot(basis_part[0], vectors[1].T) - real_dot(basis_part[1], vectors[0].T)
    return jnp.stack([real_part, imag_part])


def combine(basis_part, coeffs):
    real_part = real_dot(coeffs[0].T, basis_part[0]) - real_dot(coeffs[1].T, basis_part[1])
    imag_part = real_dot(coeffs[0].T, basis_part[1]) + real_dot(coeffs[1].T, basis_part[0])
    return jnp.stack([real_part, imag_part])


def sweep(factor, inverse, source, backward):
    start = jnp.zeros(source.shape, jnp.float32)

    def step(index, current):
        k = (KT - 1 - index) if backward else index
        k = jnp.asarray(k).astype(jnp.int32)
        rows = lax.dynamic_slice_in_dim(factor, k * TILE, TILE, 1)
        partial_value = apply_tile(rows, current)
        given = lax.dynamic_slice_in_dim(source, k * TILE, TILE, 2)
        inv = lax.dynamic_slice_in_dim(inverse, k * TILE, TILE, 2)
        piece = apply_tile(inv, given - partial_value)
        return lax.dynamic_update_slice_in_dim(current, piece, k * TILE, 2)

    return lax.fori_loop(0, KT, step, start)


def reference(factor, lower_inverse, upper_inverse, krylov_block, basis):
    solved = sweep(factor, lower_inverse, krylov_block, False)
    solution = sweep(factor, upper_inverse, solved, True)
    first = herm_dot(basis, solution)
    middle = solution - combine(basis, first)
    second = herm_dot(basis, middle)
    projected = middle - combine(basis, second)
    return projected, first + second
```

```python
import functools

import jax
import jax.numpy as jnp
from jax import lax
from jax.experimental import pallas as pl
from jax.experimental.pallas import tpu as pltpu
from jax.sharding import PartitionSpec as P

MESH = pl.DeviceIdType.MESH
F32 = jnp.float32
BF16 = jnp.bfloat16


def split(value):
    high = value.astype(BF16)
    low = (value - high.astype(F32)).astype(BF16)
    return high, low


def dot_nt(left, right):
    return lax.dot_general(left, right, (((1,), (1,)), ((), ())), preferred_element_type=F32)


def dot_nn(left, right):
    return lax.dot_general(left, right, (((1,), (0,)), ((), ())), preferred_element_type=F32)


def product(left, high, low, dot):
    rows = left.shape[0]
    left_high, left_low = split(left)
    both = dot(jnp.concatenate([left_high, left_low], 0), high)
    return both[:rows] + (both[rows:] + dot(left_high, low))


def complex_left(pieces, nvec):
    re = [x[:nvec] for x in pieces]
    im = [x[nvec:] for x in pieces]
    top = jnp.concatenate(re + [-x for x in im], 1)
    bottom = jnp.concatenate(im + re, 1)
    return jnp.concatenate([top, bottom], 0)


def kernel(
    R, C, factor, lower, upper, krylov, basis, projected, coefficients,
    inv_hi, inv_lo, fac_hi, fac_lo, bas_hi, bas_lo,
    end_hi, end_lo, lead_hi, lead_lo, gather,
    psend, precv, ybuf, xbuf, bcast, vbuf, vrecv, fsend, frecv, gacc, grecv,
    psend_sem, precv_sem, bsend_sem, brecv_sem, vsend_sem, vrecv_sem, xsend_sem, xrecv_sem,
    fsend_sem, frecv_sem, gsend_sem, grecv_sem, tsend_sem, trecv_sem, ysend_sem, yrecv_sem,
    ready_sem,
):
    tile, rows = lower.shape[1], lower.shape[2]
    width = factor.shape[2]
    nvec = krylov.shape[1]
    nb = basis.shape[1]
    share = tile // rows
    per = tile // width
    pieces = width // rows
    steps = R.bit_length() - 1
    r = lax.axis_index("row")
    c = lax.axis_index("col")
    t, p = r // share, r % share
    j, h = c // per, c % per
    solver = j == t

    barrier = pltpu.get_barrier_semaphore()

    def greet_mate(i, carry):
        pl.semaphore_signal(barrier, inc=1, device_id=(t * share + (p + 1 + i) % share, c), device_id_type=MESH)
        return carry

    def greet_tile(i, carry):
        pl.semaphore_signal(barrier, inc=1, device_id=((r + (1 + i) * share) % R, c), device_id_type=MESH)
        return carry

    def greet_col(i, carry):
        pl.semaphore_signal(barrier, inc=1, device_id=(r, (c + 1 + i) % C), device_id_type=MESH)
        return carry

    lax.fori_loop(0, share - 1, greet_mate, 0)
    lax.fori_loop(0, R // share - 1, greet_tile, 0)
    lax.fori_loop(0, C - 1, greet_col, 0)

    def prepare(ref, slot):
        high, low = split(jnp.concatenate([ref[0], ref[1]], 1))
        inv_hi[slot] = high
        inv_lo[slot] = low

    @pl.when(solver)
    def _():
        prepare(lower, 0)

    @pl.when(jnp.logical_not(solver))
    def _():
        high, low = split(jnp.concatenate([factor[0], factor[1]], 1))
        fac_hi[...] = high
        fac_lo[...] = low

    def prepare_basis():
        top = jnp.concatenate([basis[0], basis[1]], 1)
        bottom = jnp.concatenate([-basis[1], basis[0]], 1)
        high, low = split(jnp.concatenate([top, bottom], 0))
        bas_hi[...] = high
        bas_lo[...] = low
        gacc[0] = product(top, high, low, dot_nt)

    def remote(src, dst, send, recv, dest):
        return pltpu.make_async_remote_copy(
            src_ref=src, dst_ref=dst, send_sem=send, recv_sem=recv, device_id=dest, device_id_type=MESH
        )

    def each(first_index, last_index, act):
        def body(i, carry):
            act(i)
            return carry

        lax.fori_loop(first_index, last_index, body, 0)

    def gram_copy(i):
        other = r + (1 << i) * (1 - 2 * ((r // (1 << i)) % 2))
        return remote(gacc.at[i], grecv.at[i], gsend_sem.at[i], grecv_sem.at[i], (other, c))

    def gram_all():
        for i in range(steps):
            copy = gram_copy(i)
            copy.start()
            copy.wait_recv()
            gacc[i + 1] = gacc[i] + grecv[i]
        top = gacc[steps]
        gram = jnp.concatenate([top, jnp.concatenate([-top[:, nb:], top[:, :nb]], 1)], 0)
        row_id = lax.broadcasted_iota(jnp.int32, gram.shape, 0)
        col_id = lax.broadcasted_iota(jnp.int32, gram.shape, 1)
        twice = jnp.where(row_id == col_id, 2.0, 0.0) - gram
        spread = product(twice, bas_hi[...], bas_lo[...], dot_nn)
        high, low = split(jnp.concatenate([twice, spread], 1))
        end_hi[...] = high
        end_lo[...] = low

    def t_copy(d):
        q = (p + d) % share
        return remote(basis, gather.at[p], tsend_sem.at[d], trecv_sem.at[p], (t * share + q, c))

    def lead_send():
        for d in range(1, share):
            t_copy(d).start()
        gather[p] = basis[...]

    def lead_all():
        for d in range(1, share):
            q = (p + d) % share
            remote(basis, gather.at[q], tsend_sem.at[d], trecv_sem.at[q], (t * share + q, c)).wait_recv()
        left = jnp.concatenate(
            [jnp.concatenate([gather[q, i] for q in range(share)], 1) for i in range(2)], 0
        )
        out = product(left, inv_hi[1], inv_lo[1], dot_nn)
        one = out[:nb, :rows] + out[nb:, rows:]
        two = out[nb:, :rows] - out[:nb, rows:]
        whole = jnp.concatenate([jnp.concatenate([one, two], 1), jnp.concatenate([-two, one], 1)], 0)
        high, low = split(whole)
        lead_hi[...] = high
        lead_lo[...] = low

    def side_work():
        gram_all()

        @pl.when(t == 0)
        def _():
            lead_send()
            lead_all()

    def part_copy(sweep, d):
        q = (p + d) % share
        return remote(
            psend.at[sweep, q], precv.at[sweep, p], psend_sem.at[sweep, q], precv_sem.at[sweep, p], (t * share + q, c)
        )

    def part_arrival(sweep, d):
        q = (p + d) % share
        return remote(
            psend.at[sweep, q], precv.at[sweep, q], psend_sem.at[sweep, q], precv_sem.at[sweep, q], (t * share + q, c)
        ), q

    def v_copy(cc):
        return remote(vbuf, vrecv.at[c], vsend_sem.at[cc], vrecv_sem.at[c], (r, cc))

    def v_each(act):
        @pl.when(t > 0)
        def _():
            for hh in range(per):
                act(v_copy(t * per + hh))

        @pl.when(t == 0)
        def _():
            each(1, C, lambda d: act(v_copy((c + d) % C)))

    def v_sum(first_col, last_col, value):
        def body(cc, total):
            @pl.when(cc != c)
            def _():
                remote(vbuf, vrecv.at[cc], vsend_sem.at[0], vrecv_sem.at[cc], (r, cc)).wait_recv()

            return total - vrecv[cc]

        return lax.fori_loop(first_col, last_col, body, value)

    def f_copy(d):
        return remote(fsend, frecv.at[r], fsend_sem.at[d], frecv_sem.at[r], ((r + d) % R, c))

    def send_first(value, high, low):
        wide_value = jnp.concatenate([value[:nvec], value[nvec:]], 1)
        fsend[...] = product(wide_value, high, low, dot_nt)
        each(1, R, lambda d: f_copy(d).start())

    def multiply(sweep, g):
        out = product(complex_left([g], nvec), inv_hi[sweep], inv_lo[sweep], dot_nt)
        for q in range(share):
            psend[sweep, q] = out[:, q * rows:(q + 1) * rows]

    def solve(sweep, g):
        multiply(sweep, g)
        return exchange(sweep)

    def exchange(sweep):
        for d in range(1, share):
            part_copy(sweep, d).start()
        total = psend[sweep, p]
        for d in range(1, share):
            arrival, q = part_arrival(sweep, d)
            arrival.wait_recv()
            total = total + precv[sweep, q]
        return total

    def b_copy(buf, rr):
        return remote(buf, bcast.at[p % pieces], bsend_sem.at[rr], brecv_sem.at[p % pieces], (rr, c))

    def x_copy(tt):
        cc = tt * per + h
        return remote(xbuf, xbuf, xsend_sem.at[tt], xrecv_sem.at[0], (r, cc))

    def y_copy(tt):
        return remote(ybuf, ybuf, ysend_sem.at[tt], yrecv_sem.at[0], (r, tt * per + h))

    speaks = p // pieces == h

    @pl.when(solver != (t == 0))
    def _():
        prepare(upper, 1)

    @pl.when(j > 0)
    def _():
        prepare_basis()

    @pl.when(jnp.logical_and(solver, t == 0))
    def _():
        multiply(0, jnp.concatenate([krylov[0], krylov[1]], 0))

    pl.semaphore_wait(barrier, share - 1 + R // share - 1 + C - 1)
    for d in range(1, share):
        pl.semaphore_signal(
            ready_sem, inc=1, device_id=(t * share + (p + d) % share, c), device_id_type=MESH
        )

    @pl.when(j > 0)
    def _():
        side_work()

    @pl.when(solver)
    def _():
        @pl.when(t > 0)
        def _():
            b = jnp.concatenate([krylov[0], krylov[1]], 0)
            multiply(0, v_sum(0, t * per, b))

        ybuf[...] = exchange(0)
        pl.semaphore_wait(ready_sem, share - 1)

        @pl.when(speaks)
        def _():
            each((t + 1) * share, R, lambda rr: b_copy(ybuf, rr).start())

        @pl.when(t == 0)
        def _():
            each(1, C // per, lambda tt: y_copy(tt).start())
            prepare(upper, 1)

    @pl.when(jnp.logical_not(solver))
    def _():
        pl.semaphore_wait(ready_sem, share - 1)
        got = []
        for i in range(pieces):
            remote(ybuf, bcast.at[i], bsend_sem.at[0], brecv_sem.at[i], (r, t * per)).wait_recv()
            got.append(bcast[i])
        value = product(complex_left(got, nvec), fac_hi[...], fac_lo[...], dot_nt)
        vbuf[...] = value
        v_each(lambda copy: copy.start())
        vrecv[c] = value

    @pl.when(j == 0)
    def _():
        prepare_basis()
        side_work()

    @pl.when(t == 0)
    def _():
        @pl.when(jnp.logical_not(solver))
        def _():
            remote(ybuf, ybuf, ysend_sem.at[0], yrecv_sem.at[0], (r, h)).wait_recv()

        g = v_sum(per, C, ybuf[...])
        send_first(g, lead_hi[...], lead_lo[...])
        xbuf[...] = solve(1, g)

    @pl.when(t > 0)
    def _():
        @pl.when(solver)
        def _():
            xbuf[...] = solve(1, v_sum((t + 1) * per, C, ybuf[...]))

            @pl.when(speaks)
            def _():
                each(0, t * share, lambda rr: b_copy(xbuf, rr).start())

            each(0, t, lambda tt: x_copy(tt).start())
            each(t + 1, C // per, lambda tt: x_copy(tt).start())

        @pl.when(jnp.logical_not(solver))
        def _():
            remote(ybuf, xbuf, xsend_sem.at[0], xrecv_sem.at[0], (r, t * per)).wait_recv()

        send_first(xbuf[...], bas_hi[...], bas_lo[...])

    frecv[r] = fsend[...]

    def f_wait(d):
        q = (r + d) % R
        remote(fsend, frecv.at[q], fsend_sem.at[d], frecv_sem.at[q], (q, c)).wait_recv()

    each(1, R, f_wait)
    first = frecv[0]
    for i in range(1, R):
        first = first + frecv[i]
    ends = product(first, end_hi[...], end_lo[...], dot_nn)
    coefficients[0] = ends[:, :nb]
    coefficients[1] = ends[:, nb:2 * nb]
    projected[0] = xbuf[:nvec] - ends[:, 2 * nb:2 * nb + rows]
    projected[1] = xbuf[nvec:] - ends[:, 2 * nb + rows:]

    each(1, R, lambda d: f_copy(d).wait_send())
    for i in range(steps):
        gram_copy(i).wait_send()

    def parts_sent(sweep):
        for d in range(1, share):
            part_copy(sweep, d).wait_send()

    @pl.when(t == 0)
    def _():
        parts_sent(1)
        for d in range(1, share):
            t_copy(d).wait_send()

    @pl.when(solver)
    def _():
        parts_sent(0)

        @pl.when(speaks)
        def _():
            each((t + 1) * share, R, lambda rr: b_copy(ybuf, rr).wait_send())

        @pl.when(t == 0)
        def _():
            each(1, C // per, lambda tt: y_copy(tt).wait_send())

        @pl.when(t > 0)
        def _():
            parts_sent(1)

            @pl.when(speaks)
            def _():
                each(0, t * share, lambda rr: b_copy(xbuf, rr).wait_send())

            each(0, t, lambda tt: x_copy(tt).wait_send())
            each(t + 1, C // per, lambda tt: x_copy(tt).wait_send())

    @pl.when(jnp.logical_not(solver))
    def _():
        v_each(lambda copy: copy.wait_send())


def hub_kernel(
    R, C, factor, lower, upper, krylov, basis, projected, coefficients,
    fac_in, low_in, up_in, kry_in, bas_in, up_recv, f_recv,
    low_hi, low_lo, up_hi, up_lo, fac_hi, fac_lo, lead_hi, lead_lo,
    bas_hi, bas_lo, end_hi, end_lo, gather, gather_one,
    asend, arecv, ybuf, yrecv, dsend, drecv, esend, erecv, xrecv,
    fsend, frecv, gacc, grecv,
    load_sem, asend_sem, arecv_sem, ysend_sem, yrecv_sem, dsend_sem, drecv_sem,
    esend_sem, erecv_sem, xsend_sem, xrecv_sem, fsend_sem, frecv_sem,
    usend_sem, urecv_sem, msend_sem, mrecv_sem, tsend_sem, trecv_sem, osend_sem, orecv_sem,
    gsend_sem, grecv_sem, hsend_sem, hrecv_sem,
):
    tile, rows = lower.shape[1], lower.shape[2]
    width = factor.shape[2]
    nvec = krylov.shape[1]
    nb = basis.shape[1]
    share = tile // rows
    per = tile // width
    half = share // 2
    steps = R.bit_length() - 1
    r = lax.axis_index("row")
    c = lax.axis_index("col")
    me = r * C + c
    t, p = r // share, r % share
    y, z = p % half, p // half
    lead = per - 1
    main = c == lead
    hub = main & (z == 1 - t)
    side = c == 0

    def remote(src, dst, send, recv, dest):
        return pltpu.make_async_remote_copy(
            src_ref=src, dst_ref=dst, send_sem=send, recv_sem=recv, device_id=dest, device_id_type=MESH
        )

    def load(i, src, dst):
        return pltpu.make_async_copy(src, dst, load_sem.at[i])

    loads = [
        load(0, lower, low_in), load(1, krylov, kry_in), load(2, factor, fac_in), load(3, upper, up_in),
        load(4, basis, bas_in),
    ]

    @pl.when(main)
    def _():
        for i in range(4):
            loads[i].start()

    loads[4].start()

    barrier = pltpu.get_barrier_semaphore()

    def greet(i, carry):
        other = (me + 1 + i) % (R * C)
        pl.semaphore_signal(barrier, inc=1, device_id=(other // C, other % C), device_id_type=MESH)
        return carry

    lax.fori_loop(0, R * C - 1, greet, 0)

    def when(cond):
        return pl.when(cond)

    def pair(ref, axis=1):
        return jnp.concatenate([ref[0], ref[1]], axis)

    def a_copy(d):
        q = (p + d) % share
        return remote(asend.at[q], arecv.at[p], asend_sem.at[q], arecv_sem.at[p], (t * share + q, c))

    def a_wait(d):
        q = (p + d) % share
        remote(asend.at[q], arecv.at[q], asend_sem.at[q], arecv_sem.at[q], (t * share + q, c)).wait_recv()
        return q

    def y_copy(i):
        return remote(ybuf, yrecv.at[p], ysend_sem.at[i], yrecv_sem.at[p], (share + i, c))

    def y_hub():
        return remote(ybuf, yrecv.at[p], ysend_sem.at[share], yrecv_sem.at[p], (half + y, c))

    def y_wait(q):
        remote(ybuf, yrecv.at[q], ysend_sem.at[0], yrecv_sem.at[q], ((r + 1) % R, c)).wait_recv()

    def u_copy():
        return remote(upper, up_recv, usend_sem.at[0], urecv_sem.at[0], (t * share + (1 - z) * half + y, c))

    def m_near():
        return remote(factor, f_recv.at[0, 0], msend_sem.at[0], mrecv_sem.at[0], (r, lead))

    def m_far():
        h = c % per
        return remote(factor, f_recv.at[z, h], msend_sem.at[0], mrecv_sem.at[z * per + h], (half + y, lead))

    def m_wait(zz, h):
        remote(factor, f_recv.at[zz, h], msend_sem.at[0], mrecv_sem.at[zz * per + h], ((r + 1) % R, c)).wait_recv()

    def t_copy(i):
        return remote(basis, gather.at[p], tsend_sem.at[i], trecv_sem.at[p], (half + i, lead))

    def t_wait(q):
        remote(basis, gather.at[q], tsend_sem.at[0], trecv_sem.at[q], ((r + 1) % R, c)).wait_recv()

    def o_copy():
        return remote(basis, gather_one.at[z], osend_sem.at[0], orecv_sem.at[z], (half + y, lead))

    def o_wait(zz):
        remote(basis, gather_one.at[zz], osend_sem.at[0], orecv_sem.at[zz], ((r + 1) % R, c)).wait_recv()

    def d_copy(i):
        return remote(dsend.at[i], drecv.at[p], dsend_sem.at[i], drecv_sem.at[p], (share + i, c))

    def d_wait(q):
        remote(dsend.at[0], drecv.at[q], dsend_sem.at[0], drecv_sem.at[q], ((r + 1) % R, c)).wait_recv()

    def e_copy(i):
        return remote(esend, erecv.at[y], esend_sem.at[i], erecv_sem.at[y], (half + i, c))

    def e_wait(i):
        remote(esend, erecv.at[i], esend_sem.at[0], erecv_sem.at[i], ((r + 1) % R, c)).wait_recv()

    def x_copy(i):
        k, cc = i // C, i % C
        return remote(esend.at[k], xrecv.at[y], xsend_sem.at[i], xrecv_sem.at[y], (t * share + k, cc))

    def x_wait(i):
        remote(esend.at[0], xrecv.at[i], xsend_sem.at[0], xrecv_sem.at[i], ((r + 1) % R, c)).wait_recv()

    def f_copy(i):
        return remote(fsend, frecv.at[y], fsend_sem.at[i], frecv_sem.at[y], (i // C, i % C))

    def f_wait(i):
        remote(fsend, frecv.at[i], fsend_sem.at[0], frecv_sem.at[i], ((r + 1) % R, c)).wait_recv()

    def g_copy(i):
        other = r + (1 << i) * (1 - 2 * ((r // (1 << i)) % 2))
        return remote(gacc.at[i], grecv.at[i], gsend_sem.at[i], grecv_sem.at[i], (other, c))

    def h_copy(cc):
        return remote(gacc.at[steps], grecv.at[steps], hsend_sem.at[cc], hrecv_sem.at[0], (r, cc))

    def each(first_index, last_index, act, skip=None):
        def body(i, carry):
            if skip is None:
                act(i)
            else:
                @pl.when(i != skip)
                def _():
                    act(i)
            return carry

        lax.fori_loop(first_index, last_index, body, 0)

    def store(hi, lo, index, value):
        high, low = split(value)
        hi[index] = high
        lo[index] = low

    def wide(value):
        return jnp.concatenate([value[:nvec], value[nvec:]], 1)

    def start_sends():
        @when(side & (t == 1))
        def _():
            m_near().start()

        @when((c >= per) & (t == 0))
        def _():
            m_far().start()

        @when(main & jnp.logical_not(hub))
        def _():
            u_copy().start()

        @when(main & (t == 0))
        def _():
            each(0, half, lambda i: t_copy(i).start(), jnp.where(z == 1, y, half))

        @when(main & (t == 1))
        def _():
            o_copy().start()

    def put_slices(ref, out):
        for k in range(share):
            ref[k] = out[:, k * rows:(k + 1) * rows]

    def inverse_times(hi, lo, values):
        left = jnp.concatenate([complex_left([v], nvec) for v in values], 1)
        return product(left, hi, lo, dot_nt)

    def factor_times(values, count):
        left = jnp.concatenate(
            [complex_left(values[h * half:(h + 1) * half], nvec) for h in range(per)], 1
        )
        return product(left, fac_hi[:count], fac_lo[:count], dot_nt)

    span = 2 * rows
    broad = 2 * width

    @when(main & (t == 0))
    def _():
        loads[0].wait()
        loads[1].wait()
        store(low_hi, low_lo, ..., pair(low_in))
        put_slices(asend, inverse_times(low_hi[...], low_lo[...], [pair(kry_in, 0)]))

    pl.semaphore_wait(barrier, R * C - 1)

    @when(main & (t == 0))
    def _():
        for d in range(1, share):
            a_copy(d).start()

    start_sends()

    @when(main & (t == 0))
    def _():
        total = asend[p]
        for d in range(1, share):
            q = a_wait(d)
            total = total + arecv[q]
        ybuf[...] = total
        for i in range(share - 1, -1, -1):
            y_copy(i).start()

        @when(z == 0)
        def _():
            y_hub().start()

        loads[2].wait()
        loads[3].wait()

    loads[4].wait()

    def prepare_basis():
        top = pair(bas_in)
        bottom = jnp.concatenate([-bas_in[1], bas_in[0]], 1)
        store(bas_hi, bas_lo, ..., jnp.concatenate([top, bottom], 0))
        return top

    def prepare_end(top):
        gram = jnp.concatenate([top, jnp.concatenate([-top[:, nb:], top[:, :nb]], 1)], 0)
        row_id = lax.broadcasted_iota(jnp.int32, gram.shape, 0)
        col_id = lax.broadcasted_iota(jnp.int32, gram.shape, 1)
        twice = jnp.where(row_id == col_id, 2.0, 0.0) - gram
        spread = product(twice, bas_hi[...], bas_lo[...], dot_nn)
        store(end_hi, end_lo, ..., jnp.concatenate([twice, spread], 1))

    def end_from_side():
        prepare_basis()
        remote(gacc.at[0], grecv.at[steps], hsend_sem.at[0], hrecv_sem.at[0], (r, 0)).wait_recv()
        prepare_end(grecv[steps])

    @when(side)
    def _():
        gacc[0] = product(prepare_basis(), bas_hi[...], bas_lo[...], dot_nt)
        for i in range(steps):
            copy = g_copy(i)
            copy.start()
            copy.wait_recv()
            gacc[i + 1] = gacc[i] + grecv[i]
        each(1, C, lambda cc: h_copy(cc).start())
        prepare_end(gacc[steps])

    @when(c > lead)
    def _():
        end_from_side()

    @when(main & (t == 1))
    def _():
        for i in range(4):
            loads[i].wait()
        store(low_hi, low_lo, ..., pair(low_in))
        store(fac_hi, fac_lo, (slice(0, rows), slice(broad, 2 * broad)), pair(fac_in))
        m_wait(0, 0)
        store(fac_hi, fac_lo, (slice(0, rows), slice(0, broad)), pair(f_recv.at[0, 0]))

        @when(hub)
        def _():
            store(up_hi, up_lo, (slice(None), slice(0, span)), pair(up_in))

        for q in range(share):
            y_wait(q)
        g = pair(kry_in, 0) - factor_times([yrecv[q] for q in range(share)], rows)
        out = inverse_times(low_hi[...], low_lo[...], [g])
        for i in range(half):
            for k in range(2):
                dsend[i, k] = out[:, (k * half + i) * rows:(k * half + i + 1) * rows]
        each(0, half, lambda i: d_copy(i).start(), jnp.where(hub, y, half))

        @when(hub)
        def _():
            drecv[p] = dsend[y]
            remote(upper, up_recv, usend_sem.at[0], urecv_sem.at[0], ((r + 1) % R, c)).wait_recv()
            store(up_hi, up_lo, (slice(None), slice(span, 2 * span)), pair(up_recv))

            each(0, share, d_wait, p)
            parts = [drecv[q] for q in range(share)]
            total = (parts[0] + parts[1]) + (parts[2] + parts[3])
            put_slices(esend, inverse_times(up_hi[...], up_lo[...], [total[0], total[1]]))
            for i in range(half):
                e_copy(i).start()
            each(0, share * C, lambda i: x_copy(i).start(), p * C + c)
            xrecv[y] = esend[p]

        end_from_side()

    @when(main & (t == 0))
    def _():
        @when(hub)
        def _():
            store(up_hi, up_lo, (slice(None), slice(span, 2 * span)), pair(up_in))
            gather[p] = bas_in[...]
            each(0, share, t_wait, p)
            each(0, 2, o_wait)
            stacked = jnp.concatenate(
                [jnp.concatenate([gather[q, i] for q in range(share)], 1) for i in range(2)], 0
            )
            for k in range(2):
                one = gather_one[k]
                high, low = split(jnp.concatenate([
                    jnp.concatenate([one[0], one[1]], 1), jnp.concatenate([-one[1], one[0]], 1)
                ], 0))
                at = slice((2 + k) * span, (3 + k) * span)
                lead_hi[:, at] = high
                lead_lo[:, at] = low
            end_from_side()
            remote(upper, up_recv, usend_sem.at[0], urecv_sem.at[0], ((r + 1) % R, c)).wait_recv()
            store(up_hi, up_lo, (slice(None), slice(0, span)), pair(up_recv))
            for k in range(2):
                at = slice(k * span, (k + 1) * span)
                out = product(stacked, up_hi[:, at], up_lo[:, at], dot_nn)
                one = out[:nb, :rows] + out[nb:, rows:]
                two = out[nb:, :rows] - out[:nb, rows:]
                store(lead_hi, lead_lo, (slice(None), at), jnp.concatenate(
                    [jnp.concatenate([one, two], 1), jnp.concatenate([-two, one], 1)], 0
                ))
            for k in range(2):
                for h in range(per):
                    m_wait(k, h)
                    store(
                        fac_hi, fac_lo, (slice(k * rows, (k + 1) * rows), slice(h * broad, (h + 1) * broad)),
                        pair(f_recv.at[k, h]),
                    )
            y_wait(y)
            yrecv[half + y] = ybuf[...]

            for i in range(half):
                e_wait(i)
            x = [erecv[0, k] + erecv[1, k] for k in range(share)]
            out = factor_times(x, 2 * rows)
            w = [yrecv[k * half + y] - out[:, k * rows:(k + 1) * rows] for k in range(2)]
            mine = [jnp.where(y == 0, x[k * half], x[k * half + 1]) for k in range(2)]
            fsend[...] = product(
                jnp.concatenate([wide(v) for v in w + mine], 1), lead_hi[...], lead_lo[...], dot_nt
            )
            each(0, R * C, lambda i: f_copy(R * C - 1 - i).start(), R * C - 1 - me)
            frecv[y] = fsend[...]
            put_slices(esend, inverse_times(up_hi[...], up_lo[...], w))
            each(0, share * C, lambda i: x_copy(i).start(), p * C + c)
            xrecv[y] = esend[p]

        @when(jnp.logical_not(hub))
        def _():
            end_from_side()

    each(0, half, f_wait, jnp.where(hub & (t == 0), y, half))
    first = frecv[0] + frecv[1]
    ends = product(first, end_hi[...], end_lo[...], dot_nn)
    coefficients[0] = ends[:, :nb]
    coefficients[1] = ends[:, nb:2 * nb]
    each(0, half, x_wait, jnp.where(hub, y, half))
    x = xrecv[0] + xrecv[1]
    projected[0] = x[:nvec] - ends[:, 2 * nb:2 * nb + rows]
    projected[1] = x[nvec:] - ends[:, 2 * nb + rows:]

    @when(side)
    def _():
        for i in range(steps):
            g_copy(i).wait_send()
        each(1, C, lambda cc: h_copy(cc).wait_send())

        @when(t == 1)
        def _():
            m_near().wait_send()

    @when((c >= per) & (t == 0))
    def _():
        m_far().wait_send()

    @when(main)
    def _():
        @when(jnp.logical_not(hub))
        def _():
            u_copy().wait_send()

        @when(t == 0)
        def _():
            each(0, half, lambda i: t_copy(i).wait_send(), jnp.where(z == 1, y, half))
            for d in range(1, share):
                a_copy(d).wait_send()
            for i in range(share):
                y_copy(i).wait_send()

            @when(z == 0)
            def _():
                y_hub().wait_send()

        @when(t == 1)
        def _():
            o_copy().wait_send()
            each(0, half, lambda i: d_copy(i).wait_send(), jnp.where(hub, y, half))

        @when(hub)
        def _():
            each(0, share * C, lambda i: x_copy(i).wait_send(), p * C + c)

            @when(t == 1)
            def _():
                for i in range(half):
                    e_copy(i).wait_send()

            @when(t == 0)
            def _():
                each(0, R * C, lambda i: f_copy(i).wait_send(), me)


def hub_call(R, C, factor, lower, upper, krylov, basis):
    tile, rows = lower.shape[1], lower.shape[2]
    width = factor.shape[2]
    nvec, nb = krylov.shape[1], basis.shape[1]
    share, per = tile // rows, tile // width
    half = share // 2
    steps = R.bit_length() - 1
    dma = pltpu.SemaphoreType.DMA
    vmem = pl.BlockSpec(memory_space=pltpu.VMEM)
    block = (2 * nvec, rows)
    f32 = lambda *shape: pltpu.VMEM(shape, F32)
    bf16 = lambda *shape: [pltpu.VMEM(shape, BF16)] * 2
    return pl.pallas_call(
        functools.partial(hub_kernel, R, C),
        out_shape=(
            jax.ShapeDtypeStruct(krylov.shape, F32),
            jax.ShapeDtypeStruct((2, nvec, nb), F32),
        ),
        in_specs=[pl.BlockSpec(memory_space=pl.ANY)] * 5,
        out_specs=(vmem, vmem),
        scratch_shapes=[
            f32(*factor.shape), f32(*lower.shape), f32(*upper.shape), f32(*krylov.shape), f32(*basis.shape),
            f32(*upper.shape), f32(2, per, *factor.shape),
            *bf16(tile, 2 * rows), *bf16(tile, 4 * rows), *bf16(2 * rows, 2 * tile), *bf16(2 * nb, 8 * rows),
            *bf16(2 * nb, 2 * rows), *bf16(2 * nb, 2 * nb + 2 * rows),
            f32(share, *basis.shape), f32(2, *basis.shape),
            f32(share, *block), f32(share, *block), f32(*block), f32(share, *block),
            f32(half, 2, *block), f32(share, 2, *block), f32(share, *block), f32(2, share, *block),
            f32(half, *block), f32(nvec, 2 * nb), f32(half, nvec, 2 * nb),
            f32(steps + 1, nb, 2 * nb), f32(steps + 1, nb, 2 * nb),
            dma((5,)), dma((share,)), dma((share,)), dma((share + 1,)), dma((share,)),
            dma((half,)), dma((share,)), dma((half,)), dma((half,)),
            dma((share * C,)), dma((half,)), dma((R * C,)), dma((half,)),
            dma((1,)), dma((1,)), dma((1,)), dma((2 * per,)), dma((half,)), dma((share,)), dma((1,)), dma((2,)),
            dma((steps,)), dma((steps,)), dma((C,)), dma((1,)),
        ],
        compiler_params=pltpu.CompilerParams(collective_id=0, has_side_effects=True),
        name="krylov_hubs",
    )(factor, lower, upper, krylov, basis)


def finish(projected, turned, projected_out, turned_out):
    projected_out[...] = projected[...]
    turned_out[...] = turned[...]


def general_call(R, C, factor, lower, upper, krylov, basis):
    tile, rows = lower.shape[1], lower.shape[2]
    width = factor.shape[2]
    nvec, nb = krylov.shape[1], basis.shape[1]
    share, per, pieces = tile // rows, tile // width, width // rows
    steps = R.bit_length() - 1
    dma = pltpu.SemaphoreType.DMA
    vmem = pl.BlockSpec(memory_space=pltpu.VMEM)
    block = (2 * nvec, rows)
    return pl.pallas_call(
        functools.partial(kernel, R, C),
        out_shape=(
            jax.ShapeDtypeStruct(krylov.shape, F32),
            jax.ShapeDtypeStruct((2, nvec, nb), F32),
        ),
        in_specs=[vmem] * 5,
        out_specs=(vmem, vmem),
        scratch_shapes=[
            pltpu.VMEM((2, tile, 2 * rows), BF16),
            pltpu.VMEM((2, tile, 2 * rows), BF16),
            pltpu.VMEM((rows, 2 * width), BF16),
            pltpu.VMEM((rows, 2 * width), BF16),
            pltpu.VMEM((2 * nb, 2 * rows), BF16),
            pltpu.VMEM((2 * nb, 2 * rows), BF16),
            pltpu.VMEM((2 * nb, 2 * nb + 2 * rows), BF16),
            pltpu.VMEM((2 * nb, 2 * nb + 2 * rows), BF16),
            pltpu.VMEM((2 * nb, 2 * rows), BF16),
            pltpu.VMEM((2 * nb, 2 * rows), BF16),
            pltpu.VMEM((share, 2, nb, rows), F32),
            pltpu.VMEM((2, share) + block, F32),
            pltpu.VMEM((2, share) + block, F32),
            pltpu.VMEM(block, F32),
            pltpu.VMEM(block, F32),
            pltpu.VMEM((pieces,) + block, F32),
            pltpu.VMEM(block, F32),
            pltpu.VMEM((C,) + block, F32),
            pltpu.VMEM((nvec, 2 * nb), F32),
            pltpu.VMEM((R, nvec, 2 * nb), F32),
            pltpu.VMEM((steps + 1, nb, 2 * nb), F32),
            pltpu.VMEM((steps, nb, 2 * nb), F32),
            dma((2, share)),
            dma((2, share)),
            dma((R,)),
            dma((pieces,)),
            dma((C,)),
            dma((C,)),
            dma((C // per,)),
            dma((1,)),
            dma((R,)),
            dma((R,)),
            dma((steps,)),
            dma((steps,)),
            dma((share,)),
            dma((share,)),
            dma((C // per,)),
            dma((1,)),
            pltpu.SemaphoreType.REGULAR,
        ],
        compiler_params=pltpu.CompilerParams(collective_id=0, has_side_effects=True),
        name="krylov_step",
    )(factor, lower, upper, krylov, basis)


def local(R, C, factor, lower, upper, krylov, basis):
    tile, rows = lower.shape[1], lower.shape[2]
    share, per = tile // rows, tile // factor.shape[2]
    vmem = pl.BlockSpec(memory_space=pltpu.VMEM)
    paired = R == 2 * share and C == 2 * per and share == 4 and per == 2
    call = hub_call if paired else general_call
    projected, turned = call(R, C, factor, lower, upper, krylov, basis)
    projected, turned = pl.pallas_call(
        finish,
        out_shape=(jax.ShapeDtypeStruct(projected.shape, F32), jax.ShapeDtypeStruct(turned.shape, F32)),
        in_specs=[vmem] * 2,
        out_specs=(vmem, vmem),
        name="finish",
    )(projected, turned)
    return projected, turned.transpose(0, 2, 1)


def solution(mesh):
    in_specs = (
        P(None, "row", "col"),
        P(None, None, "row"),
        P(None, None, "row"),
        P(None, None, "row"),
        P(None, None, "row"),
    )
    out_specs = (P(None, None, "row"), P())
    body = functools.partial(local, mesh.shape["row"], mesh.shape["col"])
    return jax.shard_map(body, mesh=mesh, in_specs=in_specs, out_specs=out_specs, check_vma=False)
```

```python
import functools

import jax
import jax.numpy as jnp
from jax import lax
from jax.experimental import pallas as pl
from jax.experimental.pallas import tpu as pltpu
from jax.sharding import PartitionSpec as P

MESH = pl.DeviceIdType.MESH
F32 = jnp.float32
BF16 = jnp.bfloat16


def split(value):
    high = value.astype(BF16)
    low = (value - high.astype(F32)).astype(BF16)
    return high, low


def dot_nt(left, right):
    return lax.dot_general(left, right, (((1,), (1,)), ((), ())), preferred_element_type=F32)


def dot_nn(left, right):
    return lax.dot_general(left, right, (((1,), (0,)), ((), ())), preferred_element_type=F32)


def product(left, high, low, dot):
    rows = left.shape[0]
    left_high, left_low = split(left)
    both = dot(jnp.concatenate([left_high, left_low], 0), high)
    return both[:rows] + (both[rows:] + dot(left_high, low))


def complex_left(pieces, nvec):
    re = [x[:nvec] for x in pieces]
    im = [x[nvec:] for x in pieces]
    top = jnp.concatenate(re + [-x for x in im], 1)
    bottom = jnp.concatenate(im + re, 1)
    return jnp.concatenate([top, bottom], 0)


def kernel(
    R, C, factor, lower, upper, krylov, basis, projected, coefficients,
    inv_hi, inv_lo, fac_hi, fac_lo, bas_hi, bas_lo,
    end_hi, end_lo, lead_hi, lead_lo, gather,
    psend, precv, ybuf, xbuf, bcast, vbuf, vrecv, fsend, frecv, gacc, grecv,
    psend_sem, precv_sem, bsend_sem, brecv_sem, vsend_sem, vrecv_sem, xsend_sem, xrecv_sem,
    fsend_sem, frecv_sem, gsend_sem, grecv_sem, tsend_sem, trecv_sem, ysend_sem, yrecv_sem,
    ready_sem,
):
    tile, rows = lower.shape[1], lower.shape[2]
    width = factor.shape[2]
    nvec = krylov.shape[1]
    nb = basis.shape[1]
    share = tile // rows
    per = tile // width
    pieces = width // rows
    steps = R.bit_length() - 1
    r = lax.axis_index("row")
    c = lax.axis_index("col")
    t, p = r // share, r % share
    j, h = c // per, c % per
    solver = j == t

    barrier = pltpu.get_barrier_semaphore()

    def greet_mate(i, carry):
        pl.semaphore_signal(barrier, inc=1, device_id=(t * share + (p + 1 + i) % share, c), device_id_type=MESH)
        return carry

    def greet_tile(i, carry):
        pl.semaphore_signal(barrier, inc=1, device_id=((r + (1 + i) * share) % R, c), device_id_type=MESH)
        return carry

    def greet_col(i, carry):
        pl.semaphore_signal(barrier, inc=1, device_id=(r, (c + 1 + i) % C), device_id_type=MESH)
        return carry

    lax.fori_loop(0, share - 1, greet_mate, 0)
    lax.fori_loop(0, R // share - 1, greet_tile, 0)
    lax.fori_loop(0, C - 1, greet_col, 0)

    def prepare(ref, slot):
        high, low = split(jnp.concatenate([ref[0], ref[1]], 1))
        inv_hi[slot] = high
        inv_lo[slot] = low

    @pl.when(solver)
    def _():
        prepare(lower, 0)

    @pl.when(jnp.logical_not(solver))
    def _():
        high, low = split(jnp.concatenate([factor[0], factor[1]], 1))
        fac_hi[...] = high
        fac_lo[...] = low

    def prepare_basis():
        top = jnp.concatenate([basis[0], basis[1]], 1)
        bottom = jnp.concatenate([-basis[1], basis[0]], 1)
        high, low = split(jnp.concatenate([top, bottom], 0))
        bas_hi[...] = high
        bas_lo[...] = low
        gacc[0] = product(top, high, low, dot_nt)

    def remote(src, dst, send, recv, dest):
        return pltpu.make_async_remote_copy(
            src_ref=src, dst_ref=dst, send_sem=send, recv_sem=recv, device_id=dest, device_id_type=MESH
        )

    def each(first_index, last_index, act):
        def body(i, carry):
            act(i)
            return carry

        lax.fori_loop(first_index, last_index, body, 0)

    def gram_copy(i):
        other = r + (1 << i) * (1 - 2 * ((r // (1 << i)) % 2))
        return remote(gacc.at[i], grecv.at[i], gsend_sem.at[i], grecv_sem.at[i], (other, c))

    def gram_all():
        for i in range(steps):
            copy = gram_copy(i)
            copy.start()
            copy.wait_recv()
            gacc[i + 1] = gacc[i] + grecv[i]
        top = gacc[steps]
        gram = jnp.concatenate([top, jnp.concatenate([-top[:, nb:], top[:, :nb]], 1)], 0)
        row_id = lax.broadcasted_iota(jnp.int32, gram.shape, 0)
        col_id = lax.broadcasted_iota(jnp.int32, gram.shape, 1)
        twice = jnp.where(row_id == col_id, 2.0, 0.0) - gram
        spread = product(twice, bas_hi[...], bas_lo[...], dot_nn)
        high, low = split(jnp.concatenate([twice, spread], 1))
        end_hi[...] = high
        end_lo[...] = low

    def t_copy(d):
        q = (p + d) % share
        return remote(basis, gather.at[p], tsend_sem.at[d], trecv_sem.at[p], (t * share + q, c))

    def lead_send():
        for d in range(1, share):
            t_copy(d).start()
        gather[p] = basis[...]

    def lead_all():
        for d in range(1, share):
            q = (p + d) % share
            remote(basis, gather.at[q], tsend_sem.at[d], trecv_sem.at[q], (t * share + q, c)).wait_recv()
        left = jnp.concatenate(
            [jnp.concatenate([gather[q, i] for q in range(share)], 1) for i in range(2)], 0
        )
        out = product(left, inv_hi[1], inv_lo[1], dot_nn)
        one = out[:nb, :rows] + out[nb:, rows:]
        two = out[nb:, :rows] - out[:nb, rows:]
        whole = jnp.concatenate([jnp.concatenate([one, two], 1), jnp.concatenate([-two, one], 1)], 0)
        high, low = split(whole)
        lead_hi[...] = high
        lead_lo[...] = low

    def side_work():
        gram_all()

        @pl.when(t == 0)
        def _():
            lead_send()
            lead_all()

    def part_copy(sweep, d):
        q = (p + d) % share
        return remote(
            psend.at[sweep, q], precv.at[sweep, p], psend_sem.at[sweep, q], precv_sem.at[sweep, p], (t * share + q, c)
        )

    def part_arrival(sweep, d):
        q = (p + d) % share
        return remote(
            psend.at[sweep, q], precv.at[sweep, q], psend_sem.at[sweep, q], precv_sem.at[sweep, q], (t * share + q, c)
        ), q

    def v_copy(cc):
        return remote(vbuf, vrecv.at[c], vsend_sem.at[cc], vrecv_sem.at[c], (r, cc))

    def v_each(act):
        @pl.when(t > 0)
        def _():
            for hh in range(per):
                act(v_copy(t * per + hh))

        @pl.when(t == 0)
        def _():
            each(1, C, lambda d: act(v_copy((c + d) % C)))

    def v_sum(first_col, last_col, value):
        def body(cc, total):
            @pl.when(cc != c)
            def _():
                remote(vbuf, vrecv.at[cc], vsend_sem.at[0], vrecv_sem.at[cc], (r, cc)).wait_recv()

            return total - vrecv[cc]

        return lax.fori_loop(first_col, last_col, body, value)

    def f_copy(d):
        return remote(fsend, frecv.at[r], fsend_sem.at[d], frecv_sem.at[r], ((r + d) % R, c))

    def send_first(value, high, low):
        wide_value = jnp.concatenate([value[:nvec], value[nvec:]], 1)
        fsend[...] = product(wide_value, high, low, dot_nt)
        each(1, R, lambda d: f_copy(d).start())

    def multiply(sweep, g):
        out = product(complex_left([g], nvec), inv_hi[sweep], inv_lo[sweep], dot_nt)
        for q in range(share):
            psend[sweep, q] = out[:, q * rows:(q + 1) * rows]

    def solve(sweep, g):
        multiply(sweep, g)
        return exchange(sweep)

    def exchange(sweep):
        for d in range(1, share):
            part_copy(sweep, d).start()
        total = psend[sweep, p]
        for d in range(1, share):
            arrival, q = part_arrival(sweep, d)
            arrival.wait_recv()
            total = total + precv[sweep, q]
        return total

    def b_copy(buf, rr):
        return remote(buf, bcast.at[p % pieces], bsend_sem.at[rr], brecv_sem.at[p % pieces], (rr, c))

    def x_copy(tt):
        cc = tt * per + h
        return remote(xbuf, xbuf, xsend_sem.at[tt], xrecv_sem.at[0], (r, cc))

    def y_copy(tt):
        return remote(ybuf, ybuf, ysend_sem.at[tt], yrecv_sem.at[0], (r, tt * per + h))

    speaks = p // pieces == h

    @pl.when(solver != (t == 0))
    def _():
        prepare(upper, 1)

    @pl.when(j > 0)
    def _():
        prepare_basis()

    @pl.when(jnp.logical_and(solver, t == 0))
    def _():
        multiply(0, jnp.concatenate([krylov[0], krylov[1]], 0))

    pl.semaphore_wait(barrier, share - 1 + R // share - 1 + C - 1)
    for d in range(1, share):
        pl.semaphore_signal(
            ready_sem, inc=1, device_id=(t * share + (p + d) % share, c), device_id_type=MESH
        )

    @pl.when(j > 0)
    def _():
        side_work()

    @pl.when(solver)
    def _():
        @pl.when(t > 0)
        def _():
            b = jnp.concatenate([krylov[0], krylov[1]], 0)
            multiply(0, v_sum(0, t * per, b))

        ybuf[...] = exchange(0)
        pl.semaphore_wait(ready_sem, share - 1)

        @pl.when(speaks)
        def _():
            each((t + 1) * share, R, lambda rr: b_copy(ybuf, rr).start())

        @pl.when(t == 0)
        def _():
            each(1, C // per, lambda tt: y_copy(tt).start())
            prepare(upper, 1)

    @pl.when(jnp.logical_not(solver))
    def _():
        pl.semaphore_wait(ready_sem, share - 1)
        got = []
        for i in range(pieces):
            remote(ybuf, bcast.at[i], bsend_sem.at[0], brecv_sem.at[i], (r, t * per)).wait_recv()
            got.append(bcast[i])
        value = product(complex_left(got, nvec), fac_hi[...], fac_lo[...], dot_nt)
        vbuf[...] = value
        v_each(lambda copy: copy.start())
        vrecv[c] = value

    @pl.when(j == 0)
    def _():
        prepare_basis()
        side_work()

    @pl.when(t == 0)
    def _():
        @pl.when(jnp.logical_not(solver))
        def _():
            remote(ybuf, ybuf, ysend_sem.at[0], yrecv_sem.at[0], (r, h)).wait_recv()

        g = v_sum(per, C, ybuf[...])
        send_first(g, lead_hi[...], lead_lo[...])
        xbuf[...] = solve(1, g)

    @pl.when(t > 0)
    def _():
        @pl.when(solver)
        def _():
            xbuf[...] = solve(1, v_sum((t + 1) * per, C, ybuf[...]))

            @pl.when(speaks)
            def _():
                each(0, t * share, lambda rr: b_copy(xbuf, rr).start())

            each(0, t, lambda tt: x_copy(tt).start())
            each(t + 1, C // per, lambda tt: x_copy(tt).start())

        @pl.when(jnp.logical_not(solver))
        def _():
            remote(ybuf, xbuf, xsend_sem.at[0], xrecv_sem.at[0], (r, t * per)).wait_recv()

        send_first(xbuf[...], bas_hi[...], bas_lo[...])

    frecv[r] = fsend[...]

    def f_wait(d):
        q = (r + d) % R
        remote(fsend, frecv.at[q], fsend_sem.at[d], frecv_sem.at[q], (q, c)).wait_recv()

    each(1, R, f_wait)
    first = frecv[0]
    for i in range(1, R):
        first = first + frecv[i]
    ends = product(first, end_hi[...], end_lo[...], dot_nn)
    coefficients[0] = ends[:, :nb]
    coefficients[1] = ends[:, nb:2 * nb]
    projected[0] = xbuf[:nvec] - ends[:, 2 * nb:2 * nb + rows]
    projected[1] = xbuf[nvec:] - ends[:, 2 * nb + rows:]

    each(1, R, lambda d: f_copy(d).wait_send())
    for i in range(steps):
        gram_copy(i).wait_send()

    def parts_sent(sweep):
        for d in range(1, share):
            part_copy(sweep, d).wait_send()

    @pl.when(t == 0)
    def _():
        parts_sent(1)
        for d in range(1, share):
            t_copy(d).wait_send()

    @pl.when(solver)
    def _():
        parts_sent(0)

        @pl.when(speaks)
        def _():
            each((t + 1) * share, R, lambda rr: b_copy(ybuf, rr).wait_send())

        @pl.when(t == 0)
        def _():
            each(1, C // per, lambda tt: y_copy(tt).wait_send())

        @pl.when(t > 0)
        def _():
            parts_sent(1)

            @pl.when(speaks)
            def _():
                each(0, t * share, lambda rr: b_copy(xbuf, rr).wait_send())

            each(0, t, lambda tt: x_copy(tt).wait_send())
            each(t + 1, C // per, lambda tt: x_copy(tt).wait_send())

    @pl.when(jnp.logical_not(solver))
    def _():
        v_each(lambda copy: copy.wait_send())


def hub_kernel(
    R, C, factor, lower, upper, krylov, basis, projected, coefficients,
    fac_in, low_in, up_in, kry_in, bas_in, up_recv, f_recv,
    low_hi, low_lo, up_hi, up_lo, fac_hi, fac_lo, lead_hi, lead_lo,
    bas_hi, bas_lo, end_hi, end_lo, gather, gather_one,
    asend, arecv, ybuf, yrecv, dsend, drecv, esend, erecv, xrecv,
    fsend, frecv, gacc, grecv,
    load_sem, asend_sem, arecv_sem, ysend_sem, yrecv_sem, dsend_sem, drecv_sem,
    esend_sem, erecv_sem, xsend_sem, xrecv_sem, fsend_sem, frecv_sem,
    usend_sem, urecv_sem, msend_sem, mrecv_sem, tsend_sem, trecv_sem, osend_sem, orecv_sem,
    gsend_sem, grecv_sem, hsend_sem, hrecv_sem, next_sem, all_sem,
):
    tile, rows = lower.shape[1], lower.shape[2]
    width = factor.shape[2]
    nvec = krylov.shape[1]
    nb = basis.shape[1]
    share = tile // rows
    per = tile // width
    half = share // 2
    steps = R.bit_length() - 1
    r = lax.axis_index("row")
    c = lax.axis_index("col")
    me = r * C + c
    t, p = r // share, r % share
    y, z = p % half, p // half
    lead = per - 1
    main = c == lead
    hub = main & (z == 1 - t)
    side = c == 0

    def partner(i):
        return r + (1 << i) * (1 - 2 * ((r // (1 << i)) % 2))

    def remote(src, dst, send, recv, dest):
        return pltpu.make_async_remote_copy(
            src_ref=src, dst_ref=dst, send_sem=send, recv_sem=recv, device_id=dest, device_id_type=MESH
        )

    def load(i, src, dst):
        return pltpu.make_async_copy(src, dst, load_sem.at[i])

    loads = [
        load(0, lower, low_in), load(1, krylov, kry_in), load(2, factor, fac_in), load(3, upper, up_in),
        load(4, basis, bas_in),
    ]

    @pl.when(main)
    def _():
        for i in range(4):
            loads[i].start()

    loads[4].start()

    barrier = pltpu.get_barrier_semaphore()
    guide = (c == per) & (t == 0) & (z == 1)
    far = (c >= per) & (t == 0)

    def greet(rr, cc):
        pl.semaphore_signal(barrier, inc=1, device_id=(rr, cc), device_id_type=MESH)

    @pl.when(main)
    def _():
        for d in range(1, share):
            greet(t * share + (p + d) % share, c)
        greet(r, 0)

        @pl.when(t == 1)
        def _():
            for q in range(share):
                greet(q, 0)

        @pl.when(hub & (t == 0))
        def _():
            greet(y, per)
            for cc in range(per + 1, C):
                greet(y, cc)
                greet(r, cc)

    @pl.when(side)
    def _():
        for i in range(steps):
            greet(partner(i), c)

    @pl.when(c >= per)
    def _():
        greet(r, 0)

    for i in range(half):
        @pl.when(jnp.logical_not(guide & (y == i)))
        def _():
            greet(half + i, per)

    def arrive():
        count = jnp.where(main, share - 1, jnp.where(
            side, steps + 1 + C - per + jnp.where(t == 0, share, 0),
            jnp.where(guide, R * C - 1, jnp.where(far, 1, 0)),
        ))
        @pl.when(main | side | far)
        def _():
            pl.semaphore_wait(barrier, count)

        @pl.when(side & (t == 0))
        def _():
            pl.semaphore_signal(next_sem, inc=1, device_id=(r, lead), device_id_type=MESH)

        @pl.when(guide)
        def _():
            for i in range(2):
                pl.semaphore_signal(all_sem, inc=1, device_id=(half * (i + 1) + y, lead), device_id_type=MESH)

    def when(cond):
        return pl.when(cond)

    def pair(ref, axis=1):
        return jnp.concatenate([ref[0], ref[1]], axis)

    def a_copy(d):
        q = (p + d) % share
        return remote(asend.at[q], arecv.at[p], asend_sem.at[q], arecv_sem.at[p], (t * share + q, c))

    def a_wait(d):
        q = (p + d) % share
        remote(asend.at[q], arecv.at[q], asend_sem.at[q], arecv_sem.at[q], (t * share + q, c)).wait_recv()
        return q

    def y_copy(i):
        return remote(ybuf, yrecv.at[p], ysend_sem.at[i], yrecv_sem.at[p], (share + i, c))

    def y_hub():
        return remote(ybuf, yrecv.at[p], ysend_sem.at[share], yrecv_sem.at[p], (half + y, c))

    def y_wait(q):
        remote(ybuf, yrecv.at[q], ysend_sem.at[0], yrecv_sem.at[q], ((r + 1) % R, c)).wait_recv()

    def u_copy():
        return remote(upper, up_recv, usend_sem.at[0], urecv_sem.at[0], (t * share + (1 - z) * half + y, c))

    def m_near():
        return remote(factor, f_recv.at[0, 0], msend_sem.at[0], mrecv_sem.at[0], (r, lead))

    def m_far():
        h = c % per
        return remote(factor, f_recv.at[z, h], msend_sem.at[0], mrecv_sem.at[z * per + h], (half + y, lead))

    def m_wait(zz, h):
        remote(factor, f_recv.at[zz, h], msend_sem.at[0], mrecv_sem.at[zz * per + h], ((r + 1) % R, c)).wait_recv()

    def t_copy(i):
        return remote(basis, gather.at[p], tsend_sem.at[i], trecv_sem.at[p], (half + i, lead))

    def t_wait(q):
        remote(basis, gather.at[q], tsend_sem.at[0], trecv_sem.at[q], ((r + 1) % R, c)).wait_recv()

    def o_copy():
        return remote(basis, gather_one.at[z], osend_sem.at[0], orecv_sem.at[z], (half + y, lead))

    def o_wait(zz):
        remote(basis, gather_one.at[zz], osend_sem.at[0], orecv_sem.at[zz], ((r + 1) % R, c)).wait_recv()

    def d_copy(i):
        return remote(dsend.at[i], drecv.at[p], dsend_sem.at[i], drecv_sem.at[p], (share + i, c))

    def d_wait(q):
        remote(dsend.at[0], drecv.at[q], dsend_sem.at[0], drecv_sem.at[q], ((r + 1) % R, c)).wait_recv()

    def e_copy(i):
        return remote(esend, erecv.at[y], esend_sem.at[i], erecv_sem.at[y], (half + i, c))

    def e_wait(i):
        remote(esend, erecv.at[i], esend_sem.at[0], erecv_sem.at[i], ((r + 1) % R, c)).wait_recv()

    def x_copy(i):
        k, cc = i // C, i % C
        return remote(esend.at[k], xrecv.at[y], xsend_sem.at[i], xrecv_sem.at[y], (t * share + k, cc))

    def x_wait(i):
        remote(esend.at[0], xrecv.at[i], xsend_sem.at[0], xrecv_sem.at[i], ((r + 1) % R, c)).wait_recv()

    def f_copy(i):
        return remote(fsend, frecv.at[y], fsend_sem.at[i], frecv_sem.at[y], (i // C, i % C))

    def f_wait(i):
        remote(fsend, frecv.at[i], fsend_sem.at[0], frecv_sem.at[i], ((r + 1) % R, c)).wait_recv()

    def both(i):
        x_copy(i).start()
        f_copy(i).start()

    def g_copy(i):
        return remote(gacc.at[i], grecv.at[i], gsend_sem.at[i], grecv_sem.at[i], (partner(i), c))

    def h_copy(cc):
        return remote(gacc.at[steps], grecv.at[steps], hsend_sem.at[cc], hrecv_sem.at[0], (r, cc))

    def each(first_index, last_index, act, skip=None):
        def body(i, carry):
            if skip is None:
                act(i)
            else:
                @pl.when(i != skip)
                def _():
                    act(i)
            return carry

        lax.fori_loop(first_index, last_index, body, 0)

    def store(hi, lo, index, value):
        high, low = split(value)
        hi[index] = high
        lo[index] = low

    def wide(value):
        return jnp.concatenate([value[:nvec], value[nvec:]], 1)

    def start_sends():
        @when(side & (t == 1))
        def _():
            m_near().start()

        @when(far)
        def _():
            m_far().start()

        @when(main & (t == 1) & (z == 1))
        def _():
            u_copy().start()

    def put_slices(ref, out):
        for k in range(share):
            ref[k] = out[:, k * rows:(k + 1) * rows]

    def inverse_times(hi, lo, values):
        left = jnp.concatenate([complex_left([v], nvec) for v in values], 1)
        return product(left, hi, lo, dot_nt)

    def factor_times(values, count):
        left = jnp.concatenate(
            [complex_left(values[h * half:(h + 1) * half], nvec) for h in range(per)], 1
        )
        return product(left, fac_hi[:count], fac_lo[:count], dot_nt)

    span = 2 * rows
    broad = 2 * width

    @when(main & (t == 0))
    def _():
        loads[0].wait()
        loads[1].wait()
        store(low_hi, low_lo, ..., pair(low_in))
        put_slices(asend, inverse_times(low_hi[...], low_lo[...], [pair(kry_in, 0)]))

    arrive()

    @when(main & (t == 0))
    def _():
        for d in range(1, share):
            a_copy(d).start()

    start_sends()

    @when(main & (t == 0))
    def _():
        total = asend[p]
        for d in range(1, share):
            q = a_wait(d)
            total = total + arecv[q]
        ybuf[...] = total
        pl.semaphore_wait(next_sem, 1)
        for i in range(share - 1, -1, -1):
            y_copy(i).start()

        @when(z == 0)
        def _():
            y_hub().start()

        each(0, half, lambda i: t_copy(i).start(), jnp.where(z == 1, y, half))

        @when(z == 0)
        def _():
            u_copy().start()

        loads[2].wait()
        loads[3].wait()

    loads[4].wait()

    def prepare_basis():
        top = pair(bas_in)
        bottom = jnp.concatenate([-bas_in[1], bas_in[0]], 1)
        store(bas_hi, bas_lo, ..., jnp.concatenate([top, bottom], 0))
        return top

    def prepare_end(top):
        gram = jnp.concatenate([top, jnp.concatenate([-top[:, nb:], top[:, :nb]], 1)], 0)
        row_id = lax.broadcasted_iota(jnp.int32, gram.shape, 0)
        col_id = lax.broadcasted_iota(jnp.int32, gram.shape, 1)
        twice = jnp.where(row_id == col_id, 2.0, 0.0) - gram
        spread = product(twice, bas_hi[...], bas_lo[...], dot_nn)
        store(end_hi, end_lo, ..., jnp.concatenate([twice, spread], 1))

    def end_from_side():
        prepare_basis()
        remote(gacc.at[0], grecv.at[steps], hsend_sem.at[0], hrecv_sem.at[0], (r, 0)).wait_recv()
        prepare_end(grecv[steps])

    @when(side)
    def _():
        gacc[0] = product(prepare_basis(), bas_hi[...], bas_lo[...], dot_nt)
        for i in range(steps):
            copy = g_copy(i)
            copy.start()
            copy.wait_recv()
            gacc[i + 1] = gacc[i] + grecv[i]
        each(1, C, lambda cc: h_copy(cc).start())
        prepare_end(gacc[steps])

    @when(c > lead)
    def _():
        end_from_side()

    @when(main & (t == 1))
    def _():
        for i in range(4):
            loads[i].wait()
        store(low_hi, low_lo, ..., pair(low_in))
        store(fac_hi, fac_lo, (slice(0, rows), slice(broad, 2 * broad)), pair(fac_in))
        m_wait(0, 0)
        store(fac_hi, fac_lo, (slice(0, rows), slice(0, broad)), pair(f_recv.at[0, 0]))

        @when(hub)
        def _():
            store(up_hi, up_lo, (slice(None), slice(0, span)), pair(up_in))

        for q in range(share):
            y_wait(q)
        g = pair(kry_in, 0) - factor_times([yrecv[q] for q in range(share)], rows)
        out = inverse_times(low_hi[...], low_lo[...], [g])
        for i in range(half):
            for k in range(2):
                dsend[i, k] = out[:, (k * half + i) * rows:(k * half + i + 1) * rows]
        each(0, half, lambda i: d_copy(i).start(), jnp.where(hub, y, half))
        o_copy().start()

        @when(hub)
        def _():
            drecv[p] = dsend[y]
            remote(upper, up_recv, usend_sem.at[0], urecv_sem.at[0], ((r + 1) % R, c)).wait_recv()
            store(up_hi, up_lo, (slice(None), slice(span, 2 * span)), pair(up_recv))

            each(0, share, d_wait, p)
            parts = [drecv[q] for q in range(share)]
            total = (parts[0] + parts[1]) + (parts[2] + parts[3])
            put_slices(esend, inverse_times(up_hi[...], up_lo[...], [total[0], total[1]]))
            for i in range(half):
                e_copy(i).start()
            pl.semaphore_wait(all_sem, 1)
            each(0, share * C, lambda i: x_copy(i).start(), p * C + c)
            xrecv[y] = esend[p]

        end_from_side()

    @when(main & (t == 0))
    def _():
        @when(hub)
        def _():
            store(up_hi, up_lo, (slice(None), slice(span, 2 * span)), pair(up_in))
            gather[p] = bas_in[...]
            each(0, share, t_wait, p)
            stacked = jnp.concatenate(
                [jnp.concatenate([gather[q, i] for q in range(share)], 1) for i in range(2)], 0
            )
            remote(upper, up_recv, usend_sem.at[0], urecv_sem.at[0], ((r + 1) % R, c)).wait_recv()
            store(up_hi, up_lo, (slice(None), slice(0, span)), pair(up_recv))
            for k in range(2):
                at = slice(k * span, (k + 1) * span)
                out = product(stacked, up_hi[:, at], up_lo[:, at], dot_nn)
                one = out[:nb, :rows] + out[nb:, rows:]
                two = out[nb:, :rows] - out[:nb, rows:]
                store(lead_hi, lead_lo, (slice(None), at), jnp.concatenate(
                    [jnp.concatenate([one, two], 1), jnp.concatenate([-two, one], 1)], 0
                ))
            for k in range(2):
                for h in range(per):
                    m_wait(k, h)
                    store(
                        fac_hi, fac_lo, (slice(k * rows, (k + 1) * rows), slice(h * broad, (h + 1) * broad)),
                        pair(f_recv.at[k, h]),
                    )
            y_wait(y)
            yrecv[half + y] = ybuf[...]
            each(0, 2, o_wait)
            for k in range(2):
                one = gather_one[k]
                high, low = split(jnp.concatenate([
                    jnp.concatenate([one[0], one[1]], 1), jnp.concatenate([-one[1], one[0]], 1)
                ], 0))
                at = slice((2 + k) * span, (3 + k) * span)
                lead_hi[:, at] = high
                lead_lo[:, at] = low
            pl.semaphore_wait(all_sem, 1)

            for i in range(half):
                e_wait(i)
            x = [erecv[0, k] + erecv[1, k] for k in range(share)]
            out = factor_times(x, 2 * rows)
            w = [yrecv[k * half + y] - out[:, k * rows:(k + 1) * rows] for k in range(2)]
            mine = [jnp.where(y == 0, x[k * half], x[k * half + 1]) for k in range(2)]
            put_slices(esend, inverse_times(up_hi[...], up_lo[...], w))
            fsend[...] = product(
                jnp.concatenate([wide(v) for v in w + mine], 1), lead_hi[...], lead_lo[...], dot_nt
            )
            each(0, share * C, lambda i: both(i), p * C + c)
            each(share * C, R * C, lambda i: f_copy(i).start())
            xrecv[y] = esend[p]
            frecv[y] = fsend[...]
            end_from_side()

        @when(jnp.logical_not(hub))
        def _():
            end_from_side()

    each(0, half, f_wait, jnp.where(hub & (t == 0), y, half))
    first = frecv[0] + frecv[1]
    ends = product(first, end_hi[...], end_lo[...], dot_nn)
    coefficients[0] = ends[:, :nb]
    coefficients[1] = ends[:, nb:2 * nb]
    each(0, half, x_wait, jnp.where(hub, y, half))
    x = xrecv[0] + xrecv[1]
    projected[0] = x[:nvec] - ends[:, 2 * nb:2 * nb + rows]
    projected[1] = x[nvec:] - ends[:, 2 * nb + rows:]

    @when(side)
    def _():
        for i in range(steps):
            g_copy(i).wait_send()
        each(1, C, lambda cc: h_copy(cc).wait_send())

        @when(t == 1)
        def _():
            m_near().wait_send()

    @when((c >= per) & (t == 0))
    def _():
        m_far().wait_send()

    @when(main)
    def _():
        @when(jnp.logical_not(hub))
        def _():
            u_copy().wait_send()

        @when(t == 0)
        def _():
            each(0, half, lambda i: t_copy(i).wait_send(), jnp.where(z == 1, y, half))
            for d in range(1, share):
                a_copy(d).wait_send()
            for i in range(share):
                y_copy(i).wait_send()

            @when(z == 0)
            def _():
                y_hub().wait_send()

        @when(t == 1)
        def _():
            o_copy().wait_send()
            each(0, half, lambda i: d_copy(i).wait_send(), jnp.where(hub, y, half))

        @when(hub)
        def _():
            each(0, share * C, lambda i: x_copy(i).wait_send(), p * C + c)

            @when(t == 1)
            def _():
                for i in range(half):
                    e_copy(i).wait_send()

            @when(t == 0)
            def _():
                each(0, R * C, lambda i: f_copy(i).wait_send(), me)


def hub_call(R, C, factor, lower, upper, krylov, basis):
    tile, rows = lower.shape[1], lower.shape[2]
    width = factor.shape[2]
    nvec, nb = krylov.shape[1], basis.shape[1]
    share, per = tile // rows, tile // width
    half = share // 2
    steps = R.bit_length() - 1
    dma = pltpu.SemaphoreType.DMA
    vmem = pl.BlockSpec(memory_space=pltpu.VMEM)
    block = (2 * nvec, rows)
    f32 = lambda *shape: pltpu.VMEM(shape, F32)
    bf16 = lambda *shape: [pltpu.VMEM(shape, BF16)] * 2
    return pl.pallas_call(
        functools.partial(hub_kernel, R, C),
        out_shape=(pltpu.VMEM(krylov.shape, F32), pltpu.VMEM((2, nvec, nb), F32)),
        in_specs=[pl.BlockSpec(memory_space=pl.ANY)] * 5,
        out_specs=(vmem, vmem),
        scratch_shapes=[
            f32(*factor.shape), f32(*lower.shape), f32(*upper.shape), f32(*krylov.shape), f32(*basis.shape),
            f32(*upper.shape), f32(2, per, *factor.shape),
            *bf16(tile, 2 * rows), *bf16(tile, 4 * rows), *bf16(2 * rows, 2 * tile), *bf16(2 * nb, 8 * rows),
            *bf16(2 * nb, 2 * rows), *bf16(2 * nb, 2 * nb + 2 * rows),
            f32(share, *basis.shape), f32(2, *basis.shape),
            f32(share, *block), f32(share, *block), f32(*block), f32(share, *block),
            f32(half, 2, *block), f32(share, 2, *block), f32(share, *block), f32(2, share, *block),
            f32(half, *block), f32(nvec, 2 * nb), f32(half, nvec, 2 * nb),
            f32(steps + 1, nb, 2 * nb), f32(steps + 1, nb, 2 * nb),
            dma((5,)), dma((share,)), dma((share,)), dma((share + 1,)), dma((share,)),
            dma((half,)), dma((share,)), dma((half,)), dma((half,)),
            dma((share * C,)), dma((half,)), dma((R * C,)), dma((half,)),
            dma((1,)), dma((1,)), dma((1,)), dma((2 * per,)), dma((half,)), dma((share,)), dma((1,)), dma((2,)),
            dma((steps,)), dma((steps,)), dma((C,)), dma((1,)),
            pltpu.SemaphoreType.REGULAR, pltpu.SemaphoreType.REGULAR,
        ],
        compiler_params=pltpu.CompilerParams(collective_id=0, has_side_effects=True),
        name="krylov_hubs",
    )(factor, lower, upper, krylov, basis)


def finish(projected, turned, projected_out, turned_out, sems):
    copies = [
        pltpu.make_async_copy(projected, projected_out, sems.at[0]),
        pltpu.make_async_copy(turned, turned_out, sems.at[1]),
    ]
    for copy in copies:
        copy.start()
    for copy in copies:
        copy.wait()


def general_call(R, C, factor, lower, upper, krylov, basis):
    tile, rows = lower.shape[1], lower.shape[2]
    width = factor.shape[2]
    nvec, nb = krylov.shape[1], basis.shape[1]
    share, per, pieces = tile // rows, tile // width, width // rows
    steps = R.bit_length() - 1
    dma = pltpu.SemaphoreType.DMA
    vmem = pl.BlockSpec(memory_space=pltpu.VMEM)
    block = (2 * nvec, rows)
    return pl.pallas_call(
        functools.partial(kernel, R, C),
        out_shape=(
            jax.ShapeDtypeStruct(krylov.shape, F32),
            jax.ShapeDtypeStruct((2, nvec, nb), F32),
        ),
        in_specs=[vmem] * 5,
        out_specs=(vmem, vmem),
        scratch_shapes=[
            pltpu.VMEM((2, tile, 2 * rows), BF16),
            pltpu.VMEM((2, tile, 2 * rows), BF16),
            pltpu.VMEM((rows, 2 * width), BF16),
            pltpu.VMEM((rows, 2 * width), BF16),
            pltpu.VMEM((2 * nb, 2 * rows), BF16),
            pltpu.VMEM((2 * nb, 2 * rows), BF16),
            pltpu.VMEM((2 * nb, 2 * nb + 2 * rows), BF16),
            pltpu.VMEM((2 * nb, 2 * nb + 2 * rows), BF16),
            pltpu.VMEM((2 * nb, 2 * rows), BF16),
            pltpu.VMEM((2 * nb, 2 * rows), BF16),
            pltpu.VMEM((share, 2, nb, rows), F32),
            pltpu.VMEM((2, share) + block, F32),
            pltpu.VMEM((2, share) + block, F32),
            pltpu.VMEM(block, F32),
            pltpu.VMEM(block, F32),
            pltpu.VMEM((pieces,) + block, F32),
            pltpu.VMEM(block, F32),
            pltpu.VMEM((C,) + block, F32),
            pltpu.VMEM((nvec, 2 * nb), F32),
            pltpu.VMEM((R, nvec, 2 * nb), F32),
            pltpu.VMEM((steps + 1, nb, 2 * nb), F32),
            pltpu.VMEM((steps, nb, 2 * nb), F32),
            dma((2, share)),
            dma((2, share)),
            dma((R,)),
            dma((pieces,)),
            dma((C,)),
            dma((C,)),
            dma((C // per,)),
            dma((1,)),
            dma((R,)),
            dma((R,)),
            dma((steps,)),
            dma((steps,)),
            dma((share,)),
            dma((share,)),
            dma((C // per,)),
            dma((1,)),
            pltpu.SemaphoreType.REGULAR,
        ],
        compiler_params=pltpu.CompilerParams(collective_id=0, has_side_effects=True),
        name="krylov_step",
    )(factor, lower, upper, krylov, basis)


def local(R, C, factor, lower, upper, krylov, basis):
    tile, rows = lower.shape[1], lower.shape[2]
    share, per = tile // rows, tile // factor.shape[2]
    vmem = pl.BlockSpec(memory_space=pltpu.VMEM)
    paired = R == 2 * share and C == 2 * per and share == 4 and per == 2
    call = hub_call if paired else general_call
    projected, turned = call(R, C, factor, lower, upper, krylov, basis)
    if paired:
        projected, turned = [pltpu.with_memory_space_constraint(x, pltpu.VMEM) for x in (projected, turned)]
    projected, turned = pl.pallas_call(
        finish,
        out_shape=(jax.ShapeDtypeStruct(projected.shape, F32), jax.ShapeDtypeStruct(turned.shape, F32)),
        in_specs=[vmem] * 2,
        out_specs=[pl.BlockSpec(memory_space=pl.ANY)] * 2,
        scratch_shapes=[pltpu.SemaphoreType.DMA((2,))],
        name="finish",
    )(projected, turned)
    return projected, turned.transpose(0, 2, 1)


def solution(mesh):
    in_specs = (
        P(None, "row", "col"),
        P(None, None, "row"),
        P(None, None, "row"),
        P(None, None, "row"),
        P(None, None, "row"),
    )
    out_specs = (P(None, None, "row"), P())
    body = functools.partial(local, mesh.shape["row"], mesh.shape["col"])
    return jax.shard_map(body, mesh=mesh, in_specs=in_specs, out_specs=out_specs, check_vma=False)
```

```python
import functools

import jax
import jax.numpy as jnp
from jax import lax
from jax.experimental import pallas as pl
from jax.experimental.pallas import tpu as pltpu
from jax.sharding import PartitionSpec as P

MESH = pl.DeviceIdType.MESH
F32 = jnp.float32
BF16 = jnp.bfloat16


def split(value):
    high = value.astype(BF16)
    low = (value - high.astype(F32)).astype(BF16)
    return high, low


def dot_nt(left, right):
    return lax.dot_general(left, right, (((1,), (1,)), ((), ())), preferred_element_type=F32)


def dot_nn(left, right):
    return lax.dot_general(left, right, (((1,), (0,)), ((), ())), preferred_element_type=F32)


def product(left, high, low, dot):
    rows = left.shape[0]
    left_high, left_low = split(left)
    both = dot(jnp.concatenate([left_high, left_low], 0), high)
    return both[:rows] + (both[rows:] + dot(left_high, low))


def complex_left(pieces, nvec):
    re = [x[:nvec] for x in pieces]
    im = [x[nvec:] for x in pieces]
    top = jnp.concatenate(re + [-x for x in im], 1)
    bottom = jnp.concatenate(im + re, 1)
    return jnp.concatenate([top, bottom], 0)


def kernel(
    R, C, factor, lower, upper, krylov, basis, projected, coefficients,
    inv_hi, inv_lo, fac_hi, fac_lo, bas_hi, bas_lo,
    end_hi, end_lo, lead_hi, lead_lo, gather,
    psend, precv, ybuf, xbuf, bcast, vbuf, vrecv, fsend, frecv, gacc, grecv,
    psend_sem, precv_sem, bsend_sem, brecv_sem, vsend_sem, vrecv_sem, xsend_sem, xrecv_sem,
    fsend_sem, frecv_sem, gsend_sem, grecv_sem, tsend_sem, trecv_sem, ysend_sem, yrecv_sem,
    ready_sem,
):
    tile, rows = lower.shape[1], lower.shape[2]
    width = factor.shape[2]
    nvec = krylov.shape[1]
    nb = basis.shape[1]
    share = tile // rows
    per = tile // width
    pieces = width // rows
    steps = R.bit_length() - 1
    r = lax.axis_index("row")
    c = lax.axis_index("col")
    t, p = r // share, r % share
    j, h = c // per, c % per
    solver = j == t

    barrier = pltpu.get_barrier_semaphore()

    def greet_mate(i, carry):
        pl.semaphore_signal(barrier, inc=1, device_id=(t * share + (p + 1 + i) % share, c), device_id_type=MESH)
        return carry

    def greet_tile(i, carry):
        pl.semaphore_signal(barrier, inc=1, device_id=((r + (1 + i) * share) % R, c), device_id_type=MESH)
        return carry

    def greet_col(i, carry):
        pl.semaphore_signal(barrier, inc=1, device_id=(r, (c + 1 + i) % C), device_id_type=MESH)
        return carry

    lax.fori_loop(0, share - 1, greet_mate, 0)
    lax.fori_loop(0, R // share - 1, greet_tile, 0)
    lax.fori_loop(0, C - 1, greet_col, 0)

    def prepare(ref, slot):
        high, low = split(jnp.concatenate([ref[0], ref[1]], 1))
        inv_hi[slot] = high
        inv_lo[slot] = low

    @pl.when(solver)
    def _():
        prepare(lower, 0)

    @pl.when(jnp.logical_not(solver))
    def _():
        high, low = split(jnp.concatenate([factor[0], factor[1]], 1))
        fac_hi[...] = high
        fac_lo[...] = low

    def prepare_basis():
        top = jnp.concatenate([basis[0], basis[1]], 1)
        bottom = jnp.concatenate([-basis[1], basis[0]], 1)
        high, low = split(jnp.concatenate([top, bottom], 0))
        bas_hi[...] = high
        bas_lo[...] = low
        gacc[0] = product(top, high, low, dot_nt)

    def remote(src, dst, send, recv, dest):
        return pltpu.make_async_remote_copy(
            src_ref=src, dst_ref=dst, send_sem=send, recv_sem=recv, device_id=dest, device_id_type=MESH
        )

    def each(first_index, last_index, act):
        def body(i, carry):
            act(i)
            return carry

        lax.fori_loop(first_index, last_index, body, 0)

    def gram_copy(i):
        other = r + (1 << i) * (1 - 2 * ((r // (1 << i)) % 2))
        return remote(gacc.at[i], grecv.at[i], gsend_sem.at[i], grecv_sem.at[i], (other, c))

    def gram_all():
        for i in range(steps):
            copy = gram_copy(i)
            copy.start()
            copy.wait_recv()
            gacc[i + 1] = gacc[i] + grecv[i]
        top = gacc[steps]
        gram = jnp.concatenate([top, jnp.concatenate([-top[:, nb:], top[:, :nb]], 1)], 0)
        row_id = lax.broadcasted_iota(jnp.int32, gram.shape, 0)
        col_id = lax.broadcasted_iota(jnp.int32, gram.shape, 1)
        twice = jnp.where(row_id == col_id, 2.0, 0.0) - gram
        spread = product(twice, bas_hi[...], bas_lo[...], dot_nn)
        high, low = split(jnp.concatenate([twice, spread], 1))
        end_hi[...] = high
        end_lo[...] = low

    def t_copy(d):
        q = (p + d) % share
        return remote(basis, gather.at[p], tsend_sem.at[d], trecv_sem.at[p], (t * share + q, c))

    def lead_send():
        for d in range(1, share):
            t_copy(d).start()
        gather[p] = basis[...]

    def lead_all():
        for d in range(1, share):
            q = (p + d) % share
            remote(basis, gather.at[q], tsend_sem.at[d], trecv_sem.at[q], (t * share + q, c)).wait_recv()
        left = jnp.concatenate(
            [jnp.concatenate([gather[q, i] for q in range(share)], 1) for i in range(2)], 0
        )
        out = product(left, inv_hi[1], inv_lo[1], dot_nn)
        one = out[:nb, :rows] + out[nb:, rows:]
        two = out[nb:, :rows] - out[:nb, rows:]
        whole = jnp.concatenate([jnp.concatenate([one, two], 1), jnp.concatenate([-two, one], 1)], 0)
        high, low = split(whole)
        lead_hi[...] = high
        lead_lo[...] = low

    def side_work():
        gram_all()

        @pl.when(t == 0)
        def _():
            lead_send()
            lead_all()

    def part_copy(sweep, d):
        q = (p + d) % share
        return remote(
            psend.at[sweep, q], precv.at[sweep, p], psend_sem.at[sweep, q], precv_sem.at[sweep, p], (t * share + q, c)
        )

    def part_arrival(sweep, d):
        q = (p + d) % share
        return remote(
            psend.at[sweep, q], precv.at[sweep, q], psend_sem.at[sweep, q], precv_sem.at[sweep, q], (t * share + q, c)
        ), q

    def v_copy(cc):
        return remote(vbuf, vrecv.at[c], vsend_sem.at[cc], vrecv_sem.at[c], (r, cc))

    def v_each(act):
        @pl.when(t > 0)
        def _():
            for hh in range(per):
                act(v_copy(t * per + hh))

        @pl.when(t == 0)
        def _():
            each(1, C, lambda d: act(v_copy((c + d) % C)))

    def v_sum(first_col, last_col, value):
        def body(cc, total):
            @pl.when(cc != c)
            def _():
                remote(vbuf, vrecv.at[cc], vsend_sem.at[0], vrecv_sem.at[cc], (r, cc)).wait_recv()

            return total - vrecv[cc]

        return lax.fori_loop(first_col, last_col, body, value)

    def f_copy(d):
        return remote(fsend, frecv.at[r], fsend_sem.at[d], frecv_sem.at[r], ((r + d) % R, c))

    def send_first(value, high, low):
        wide_value = jnp.concatenate([value[:nvec], value[nvec:]], 1)
        fsend[...] = product(wide_value, high, low, dot_nt)
        each(1, R, lambda d: f_copy(d).start())

    def multiply(sweep, g):
        out = product(complex_left([g], nvec), inv_hi[sweep], inv_lo[sweep], dot_nt)
        for q in range(share):
            psend[sweep, q] = out[:, q * rows:(q + 1) * rows]

    def solve(sweep, g):
        multiply(sweep, g)
        return exchange(sweep)

    def exchange(sweep):
        for d in range(1, share):
            part_copy(sweep, d).start()
        total = psend[sweep, p]
        for d in range(1, share):
            arrival, q = part_arrival(sweep, d)
            arrival.wait_recv()
            total = total + precv[sweep, q]
        return total

    def b_copy(buf, rr):
        return remote(buf, bcast.at[p % pieces], bsend_sem.at[rr], brecv_sem.at[p % pieces], (rr, c))

    def x_copy(tt):
        cc = tt * per + h
        return remote(xbuf, xbuf, xsend_sem.at[tt], xrecv_sem.at[0], (r, cc))

    def y_copy(tt):
        return remote(ybuf, ybuf, ysend_sem.at[tt], yrecv_sem.at[0], (r, tt * per + h))

    speaks = p // pieces == h

    @pl.when(solver != (t == 0))
    def _():
        prepare(upper, 1)

    @pl.when(j > 0)
    def _():
        prepare_basis()

    @pl.when(jnp.logical_and(solver, t == 0))
    def _():
        multiply(0, jnp.concatenate([krylov[0], krylov[1]], 0))

    pl.semaphore_wait(barrier, share - 1 + R // share - 1 + C - 1)
    for d in range(1, share):
        pl.semaphore_signal(
            ready_sem, inc=1, device_id=(t * share + (p + d) % share, c), device_id_type=MESH
        )

    @pl.when(j > 0)
    def _():
        side_work()

    @pl.when(solver)
    def _():
        @pl.when(t > 0)
        def _():
            b = jnp.concatenate([krylov[0], krylov[1]], 0)
            multiply(0, v_sum(0, t * per, b))

        ybuf[...] = exchange(0)
        pl.semaphore_wait(ready_sem, share - 1)

        @pl.when(speaks)
        def _():
            each((t + 1) * share, R, lambda rr: b_copy(ybuf, rr).start())

        @pl.when(t == 0)
        def _():
            each(1, C // per, lambda tt: y_copy(tt).start())
            prepare(upper, 1)

    @pl.when(jnp.logical_not(solver))
    def _():
        pl.semaphore_wait(ready_sem, share - 1)
        got = []
        for i in range(pieces):
            remote(ybuf, bcast.at[i], bsend_sem.at[0], brecv_sem.at[i], (r, t * per)).wait_recv()
            got.append(bcast[i])
        value = product(complex_left(got, nvec), fac_hi[...], fac_lo[...], dot_nt)
        vbuf[...] = value
        v_each(lambda copy: copy.start())
        vrecv[c] = value

    @pl.when(j == 0)
    def _():
        prepare_basis()
        side_work()

    @pl.when(t == 0)
    def _():
        @pl.when(jnp.logical_not(solver))
        def _():
            remote(ybuf, ybuf, ysend_sem.at[0], yrecv_sem.at[0], (r, h)).wait_recv()

        g = v_sum(per, C, ybuf[...])
        send_first(g, lead_hi[...], lead_lo[...])
        xbuf[...] = solve(1, g)

    @pl.when(t > 0)
    def _():
        @pl.when(solver)
        def _():
            xbuf[...] = solve(1, v_sum((t + 1) * per, C, ybuf[...]))

            @pl.when(speaks)
            def _():
                each(0, t * share, lambda rr: b_copy(xbuf, rr).start())

            each(0, t, lambda tt: x_copy(tt).start())
            each(t + 1, C // per, lambda tt: x_copy(tt).start())

        @pl.when(jnp.logical_not(solver))
        def _():
            remote(ybuf, xbuf, xsend_sem.at[0], xrecv_sem.at[0], (r, t * per)).wait_recv()

        send_first(xbuf[...], bas_hi[...], bas_lo[...])

    frecv[r] = fsend[...]

    def f_wait(d):
        q = (r + d) % R
        remote(fsend, frecv.at[q], fsend_sem.at[d], frecv_sem.at[q], (q, c)).wait_recv()

    each(1, R, f_wait)
    first = frecv[0]
    for i in range(1, R):
        first = first + frecv[i]
    ends = product(first, end_hi[...], end_lo[...], dot_nn)
    coefficients[0] = ends[:, :nb]
    coefficients[1] = ends[:, nb:2 * nb]
    projected[0] = xbuf[:nvec] - ends[:, 2 * nb:2 * nb + rows]
    projected[1] = xbuf[nvec:] - ends[:, 2 * nb + rows:]

    each(1, R, lambda d: f_copy(d).wait_send())
    for i in range(steps):
        gram_copy(i).wait_send()

    def parts_sent(sweep):
        for d in range(1, share):
            part_copy(sweep, d).wait_send()

    @pl.when(t == 0)
    def _():
        parts_sent(1)
        for d in range(1, share):
            t_copy(d).wait_send()

    @pl.when(solver)
    def _():
        parts_sent(0)

        @pl.when(speaks)
        def _():
            each((t + 1) * share, R, lambda rr: b_copy(ybuf, rr).wait_send())

        @pl.when(t == 0)
        def _():
            each(1, C // per, lambda tt: y_copy(tt).wait_send())

        @pl.when(t > 0)
        def _():
            parts_sent(1)

            @pl.when(speaks)
            def _():
                each(0, t * share, lambda rr: b_copy(xbuf, rr).wait_send())

            each(0, t, lambda tt: x_copy(tt).wait_send())
            each(t + 1, C // per, lambda tt: x_copy(tt).wait_send())

    @pl.when(jnp.logical_not(solver))
    def _():
        v_each(lambda copy: copy.wait_send())


def hub_kernel(
    R, C, factor, lower, upper, krylov, basis, projected, coefficients,
    fac_in, low_in, up_in, kry_in, bas_in, up_recv, f_recv,
    low_hi, low_lo, up_hi, up_lo, fac_hi, fac_lo,
    bas_hi, bas_lo, end_hi, end_lo, gather, gather_one,
    asend, arecv, ybuf, yrecv, dsend, drecv, esend, erecv, gsend, xrecv, gacc, grecv,
    load_sem, asend_sem, arecv_sem, ysend_sem, yrecv_sem, dsend_sem, drecv_sem,
    esend_sem, erecv_sem, xsend_sem, xrecv_sem, fsend_sem, frecv_sem,
    usend_sem, urecv_sem, msend_sem, mrecv_sem, tsend_sem, trecv_sem, osend_sem, orecv_sem,
    gsend_sem, grecv_sem, hsend_sem, hrecv_sem, next_sem, all_sem,
):
    tile, rows = lower.shape[1], lower.shape[2]
    width = factor.shape[2]
    nvec = krylov.shape[1]
    nb = basis.shape[1]
    share = tile // rows
    per = tile // width
    half = share // 2
    steps = R.bit_length() - 1
    r = lax.axis_index("row")
    c = lax.axis_index("col")
    me = r * C + c
    t, p = r // share, r % share
    y, z = p % half, p // half
    lead = per - 1
    both = 2 * nvec
    main = c == lead
    hub = main & (z == 1 - t)
    side = c == 0

    def partner(i):
        return r + (1 << i) * (1 - 2 * ((r // (1 << i)) % 2))

    def remote(src, dst, send, recv, dest):
        return pltpu.make_async_remote_copy(
            src_ref=src, dst_ref=dst, send_sem=send, recv_sem=recv, device_id=dest, device_id_type=MESH
        )

    def load(i, src, dst):
        return pltpu.make_async_copy(src, dst, load_sem.at[i])

    loads = [
        load(0, lower, low_in), load(1, krylov, kry_in), load(2, factor, fac_in), load(3, upper, up_in),
        load(4, basis, bas_in),
    ]

    @pl.when(main)
    def _():
        for i in range(4):
            loads[i].start()

    loads[4].start()

    barrier = pltpu.get_barrier_semaphore()
    guide = (c == per) & (t == 1) & (z == 0)
    far = (c >= per) & (t == 0)

    def greet(rr, cc):
        pl.semaphore_signal(barrier, inc=1, device_id=(rr, cc), device_id_type=MESH)

    @pl.when(main)
    def _():
        @pl.when(hub)
        def _():
            for d in range(1, share):
                greet(t * share + (p + d) % share, c)

        greet(r, 0)

        @pl.when(t == 1)
        def _():
            for i in range(half):
                greet(half + i, 0)

        @pl.when(hub & (t == 0))
        def _():
            for cc in range(per, C):
                greet(y, cc)
                greet(r, cc)

    @pl.when(side)
    def _():
        for i in range(steps):
            greet(partner(i), c)

    @pl.when(c >= per)
    def _():
        greet(r, 0)

    for i in range(half):
        @pl.when(jnp.logical_not(guide & (y == i)))
        def _():
            greet(share + i, per)

    def arrive():
        count = jnp.where(main, jnp.where(hub, half - 1, half), jnp.where(
            side, steps + 1 + C - per + jnp.where((t == 0) & (z == 1), share, 0),
            jnp.where(guide, R * C - 1, jnp.where(far, 1, 0)),
        ))
        @pl.when(main | side | far | guide)
        def _():
            pl.semaphore_wait(barrier, count)

        @pl.when(side & (t == 0) & (z == 1))
        def _():
            pl.semaphore_signal(next_sem, inc=1, device_id=(r, lead), device_id_type=MESH)

        @pl.when(guide)
        def _():
            for i in range(2):
                pl.semaphore_signal(all_sem, inc=1, device_id=(half * (i + 1) + y, lead), device_id_type=MESH)

    def when(cond):
        return pl.when(cond)

    def pair(ref, axis=1):
        return jnp.concatenate([ref[0], ref[1]], axis)

    def a_copy(i):
        i = (y + 1 + i) % half
        return remote(asend.at[i], arecv.at[p], asend_sem.at[i], arecv_sem.at[p], (half + i, c))

    def a_wait(q):
        remote(asend.at[0], arecv.at[q], asend_sem.at[0], arecv_sem.at[q], ((r + 1) % R, c)).wait_recv()

    def y_copy(i):
        i = (1 - i // half) * half + (y + 1 + i) % half
        return remote(ybuf, yrecv.at[y], ysend_sem.at[i], yrecv_sem.at[y], (share + i, c))

    def y_wait(i):
        remote(ybuf, yrecv.at[i], ysend_sem.at[0], yrecv_sem.at[i], ((r + 1) % R, c)).wait_recv()

    def u_copy():
        return remote(upper, up_recv, usend_sem.at[0], urecv_sem.at[0], (t * share + (1 - z) * half + y, c))

    def m_near():
        return remote(factor, f_recv.at[0, 0], msend_sem.at[0], mrecv_sem.at[0], (r, lead))

    def m_far():
        h = c % per
        return remote(factor, f_recv.at[z, h], msend_sem.at[0], mrecv_sem.at[z * per + h], (half + y, lead))

    def m_wait(zz, h):
        remote(factor, f_recv.at[zz, h], msend_sem.at[0], mrecv_sem.at[zz * per + h], ((r + 1) % R, c)).wait_recv()

    def t_copy(i):
        return remote(basis, gather.at[p], tsend_sem.at[i], trecv_sem.at[p], (half + i, lead))

    def t_wait(q):
        remote(basis, gather.at[q], tsend_sem.at[0], trecv_sem.at[q], ((r + 1) % R, c)).wait_recv()

    def o_copy():
        return remote(basis, gather_one.at[z], osend_sem.at[0], orecv_sem.at[z], (half + y, lead))

    def o_wait(zz):
        remote(basis, gather_one.at[zz], osend_sem.at[0], orecv_sem.at[zz], ((r + 1) % R, c)).wait_recv()

    def d_copy(i):
        i = (y + 1 + i) % half
        return remote(dsend.at[i], drecv.at[p], dsend_sem.at[i], drecv_sem.at[p], (share + i, c))

    def d_wait(q):
        remote(dsend.at[0], drecv.at[q], dsend_sem.at[0], drecv_sem.at[q], ((r + 1) % R, c)).wait_recv()

    def e_copy(i):
        h, k = i // half, (y + 1 + i) % half
        at = pl.ds(h * half, half)
        return remote(esend.at[at], erecv.at[y, at], esend_sem.at[i], erecv_sem.at[y * per + h], (half + k, c))

    def e_wait(i, h):
        at = pl.ds(h * half, half)
        remote(
            esend.at[at], erecv.at[i, at], esend_sem.at[0], erecv_sem.at[i * per + h], ((r + 1) % R, c)
        ).wait_recv()

    def x_copy(i):
        k, cc = i // C, i % C
        return remote(
            esend.at[k], xrecv.at[y, pl.ds(0, both)], xsend_sem.at[i], xrecv_sem.at[y], (t * share + k, cc)
        )

    def x_wait(i):
        remote(
            esend.at[0], xrecv.at[i, pl.ds(0, both)], xsend_sem.at[0], xrecv_sem.at[i], ((r + 1) % R, c)
        ).wait_recv()

    def f_copy(i):
        at = pl.ds(both, nvec)
        return remote(gsend.at[0, at], xrecv.at[y, at], fsend_sem.at[i], frecv_sem.at[y], (i // C, i % C))

    def f_wait(i):
        at = pl.ds(both, nvec)
        remote(gsend.at[0, at], xrecv.at[i, at], fsend_sem.at[0], frecv_sem.at[i], ((r + 1) % R, c)).wait_recv()

    def z_copy(i):
        k, cc = i // C, i % C
        return remote(gsend.at[k], xrecv.at[y], xsend_sem.at[i], xrecv_sem.at[y], (k, cc))

    def z_wait(i):
        remote(gsend.at[0], xrecv.at[i], xsend_sem.at[0], xrecv_sem.at[i], ((r + 1) % R, c)).wait_recv()

    def g_copy(i):
        return remote(gacc.at[i], grecv.at[i], gsend_sem.at[i], grecv_sem.at[i], (partner(i), c))

    def h_copy(cc):
        return remote(gacc.at[steps], grecv.at[steps], hsend_sem.at[cc], hrecv_sem.at[0], (r, cc))

    def each(first_index, last_index, act, skip=None):
        def body(i, carry):
            if skip is None:
                act(i)
            else:
                @pl.when(i != skip)
                def _():
                    act(i)
            return carry

        lax.fori_loop(first_index, last_index, body, 0)

    def store(hi, lo, index, value):
        high, low = split(value)
        hi[index] = high
        lo[index] = low

    def wide(value):
        return jnp.concatenate([value[:nvec], value[nvec:]], 1)

    def start_sends():
        @when(side & (t == 1))
        def _():
            m_near().start()

        @when(far)
        def _():
            m_far().start()

        @when(main & (t == 1) & (z == 1))
        def _():
            u_copy().start()

    def put_slices(ref, out):
        for k in range(share):
            ref[k] = out[:, k * rows:(k + 1) * rows]

    def put_pairs(ref, out):
        for i in range(half):
            for k in range(2):
                ref[i, k] = out[:, (k * half + i) * rows:(k * half + i + 1) * rows]

    def inverse_times(hi, lo, values):
        left = jnp.concatenate([complex_left([v], nvec) for v in values], 1)
        return product(left, hi, lo, dot_nt)

    def factor_times(values, count):
        left = jnp.concatenate(
            [complex_left(values[h * half:(h + 1) * half], nvec) for h in range(per)], 1
        )
        return product(left, fac_hi[:count], fac_lo[:count], dot_nt)

    span = 2 * rows
    broad = 2 * width

    @when(main & (t == 0))
    def _():
        loads[0].wait()
        loads[1].wait()
        store(low_hi, low_lo, ..., pair(low_in))
        put_pairs(asend, inverse_times(low_hi[...], low_lo[...], [pair(kry_in, 0)]))

    arrive()

    @when(main & (t == 0))
    def _():
        each(0, jnp.where(hub, half - 1, half), lambda i: a_copy(i).start())

    start_sends()

    @when(main & (t == 0))
    def _():
        @when(hub)
        def _():
            arecv[p] = asend[y]
            each(0, share, a_wait, p)
            parts = [arecv[q] for q in range(share)]
            ybuf[...] = (parts[0] + parts[1]) + (parts[2] + parts[3])
            pl.semaphore_wait(next_sem, 1)
            for i in range(share):
                y_copy(i).start()

        each(0, half, lambda i: t_copy(i).start(), jnp.where(hub, y, half))

        @when(jnp.logical_not(hub))
        def _():
            u_copy().start()

        loads[2].wait()
        loads[3].wait()

    loads[4].wait()

    def prepare_basis():
        top = pair(bas_in)
        bottom = jnp.concatenate([-bas_in[1], bas_in[0]], 1)
        store(bas_hi, bas_lo, ..., jnp.concatenate([top, bottom], 0))
        return top

    def prepare_end(top):
        gram = jnp.concatenate([top, jnp.concatenate([-top[:, nb:], top[:, :nb]], 1)], 0)
        row_id = lax.broadcasted_iota(jnp.int32, gram.shape, 0)
        col_id = lax.broadcasted_iota(jnp.int32, gram.shape, 1)
        twice = jnp.where(row_id == col_id, 2.0, 0.0) - gram
        spread = product(twice, bas_hi[...], bas_lo[...], dot_nn)
        store(end_hi, end_lo, ..., jnp.concatenate([twice, spread], 1))

    def end_from_side():
        prepare_basis()
        remote(gacc.at[0], grecv.at[steps], hsend_sem.at[0], hrecv_sem.at[0], (r, 0)).wait_recv()
        prepare_end(grecv[steps])

    @when(side)
    def _():
        gacc[0] = product(prepare_basis(), bas_hi[...], bas_lo[...], dot_nt)
        for i in range(steps):
            copy = g_copy(i)
            copy.start()
            copy.wait_recv()
            gacc[i + 1] = gacc[i] + grecv[i]
        each(1, C, lambda cc: h_copy(cc).start())
        prepare_end(gacc[steps])

    @when(c > lead)
    def _():
        end_from_side()

    @when(main & (t == 1))
    def _():
        for i in range(4):
            loads[i].wait()
        store(low_hi, low_lo, ..., pair(low_in))
        store(fac_hi, fac_lo, (slice(0, rows), slice(broad, 2 * broad)), pair(fac_in))
        m_wait(0, 0)
        store(fac_hi, fac_lo, (slice(0, rows), slice(0, broad)), pair(f_recv.at[0, 0]))

        @when(hub)
        def _():
            store(up_hi, up_lo, (slice(None), slice(0, span)), pair(up_in))

        for i in range(half):
            y_wait(i)
        g = pair(kry_in, 0) - factor_times([yrecv[q % half, q // half] for q in range(share)], rows)
        put_pairs(dsend, inverse_times(low_hi[...], low_lo[...], [g]))
        each(0, jnp.where(hub, half - 1, half), lambda i: d_copy(i).start())
        o_copy().start()

        @when(hub)
        def _():
            drecv[p] = dsend[y]
            remote(upper, up_recv, usend_sem.at[0], urecv_sem.at[0], ((r + 1) % R, c)).wait_recv()
            store(up_hi, up_lo, (slice(None), slice(span, 2 * span)), pair(up_recv))

            each(0, share, d_wait, p)
            parts = [drecv[q] for q in range(share)]
            total = (parts[0] + parts[1]) + (parts[2] + parts[3])
            put_slices(esend, inverse_times(up_hi[...], up_lo[...], [total[0], total[1]]))
            for i in range(per * half):
                e_copy(i).start()
            pl.semaphore_wait(all_sem, 1)
            each(0, share * C, lambda i: x_copy(i).start(), p * C + c)
            xrecv[y, :both] = esend[p]

        end_from_side()

    @when(main & (t == 0))
    def _():
        @when(hub)
        def _():
            store(up_hi, up_lo, (slice(None), slice(span, 2 * span)), pair(up_in))
            gather[p] = bas_in[...]
            each(0, share, t_wait, p)
            stacked = jnp.concatenate(
                [jnp.concatenate([gather[q, i] for q in range(share)], 1) for i in range(2)], 0
            )
            remote(upper, up_recv, usend_sem.at[0], urecv_sem.at[0], ((r + 1) % R, c)).wait_recv()
            store(up_hi, up_lo, (slice(None), slice(0, span)), pair(up_recv))
            real, imag = [], []
            for k in range(2):
                at = slice(k * span, (k + 1) * span)
                out = product(stacked, up_hi[:, at], up_lo[:, at], dot_nn)
                real.append(out[:nb, :rows] + out[nb:, rows:])
                imag.append(out[:nb, rows:] - out[nb:, :rows])
            real, imag = jnp.concatenate(real, 1), jnp.concatenate(imag, 1)
            high, low = split(jnp.concatenate([real, imag], 1))
            known = product(complex_left([ybuf[0], ybuf[1]], nvec), high, low, dot_nt)
            for h in range(per):
                for k in range(2):
                    m_wait(k, h)
                    store(
                        fac_hi, fac_lo, (slice(k * rows, (k + 1) * rows), slice(h * broad, (h + 1) * broad)),
                        pair(f_recv.at[k, h]),
                    )
            each(0, 2, o_wait)
            empty = jnp.zeros((nb, rows), F32)
            for h in range(per):
                at = slice(h * broad, (h + 1) * broad)
                out = product(
                    jnp.concatenate([real, imag], 0), fac_hi[:span, at], fac_lo[:span, at], dot_nn
                )
                one = gather_one[h]
                own_re = jnp.where(y == 0, jnp.concatenate([one[0], empty], 1), jnp.concatenate([empty, one[0]], 1))
                own_im = jnp.where(y == 0, jnp.concatenate([one[1], empty], 1), jnp.concatenate([empty, one[1]], 1))
                store(fac_hi, fac_lo, (slice(span, span + nb), at), jnp.concatenate([
                    own_re - (out[:nb, :width] - out[nb:, width:]),
                    -own_im - (out[:nb, width:] + out[nb:, :width]),
                ], 1))
            pl.semaphore_wait(all_sem, 1)

            out = 0.0
            for h in range(per):
                for i in range(half):
                    e_wait(i, h)
                x = [erecv[0, h * half + k] + erecv[1, h * half + k] for k in range(half)]
                at = slice(h * broad, (h + 1) * broad)
                out = out + product(complex_left(x, nvec), fac_hi[:, at], fac_lo[:, at], dot_nt)
            w = [ybuf[k] - out[:, k * rows:(k + 1) * rows] for k in range(2)]
            first = wide(known + out[:, span:])
            for k in range(share):
                gsend[k, both:] = first
            out = inverse_times(up_hi[...], up_lo[...], w)
            for k in range(share):
                gsend[k, :both] = out[:, k * rows:(k + 1) * rows]
            each(0, share * C, lambda i: z_copy(i).start(), p * C + c)
            each(share * C, R * C, lambda i: f_copy(i).start())
            xrecv[y] = gsend[p]
            end_from_side()

        @when(jnp.logical_not(hub))
        def _():
            end_from_side()

    @when(t == 0)
    def _():
        each(0, half, z_wait, jnp.where(hub, y, half))

    @when(t == 1)
    def _():
        each(0, half, x_wait, jnp.where(hub, y, half))
        each(0, half, f_wait)

    total = xrecv[0] + xrecv[1]
    ends = product(total[both:], end_hi[...], end_lo[...], dot_nn)
    coefficients[0] = ends[:, :nb]
    coefficients[1] = ends[:, nb:2 * nb]
    projected[0] = total[:nvec] - ends[:, 2 * nb:2 * nb + rows]
    projected[1] = total[nvec:both] - ends[:, 2 * nb + rows:]

    @when(side)
    def _():
        for i in range(steps):
            g_copy(i).wait_send()
        each(1, C, lambda cc: h_copy(cc).wait_send())

        @when(t == 1)
        def _():
            m_near().wait_send()

    @when((c >= per) & (t == 0))
    def _():
        m_far().wait_send()

    @when(main)
    def _():
        @when(jnp.logical_not(hub))
        def _():
            u_copy().wait_send()

        @when(t == 0)
        def _():
            each(0, half, lambda i: t_copy(i).wait_send(), jnp.where(hub, y, half))
            each(0, jnp.where(hub, half - 1, half), lambda i: a_copy(i).wait_send())

            @when(hub)
            def _():
                for i in range(share):
                    y_copy(i).wait_send()

        @when(t == 1)
        def _():
            o_copy().wait_send()
            each(0, jnp.where(hub, half - 1, half), lambda i: d_copy(i).wait_send())

        @when(hub)
        def _():
            @when(t == 1)
            def _():
                each(0, share * C, lambda i: x_copy(i).wait_send(), p * C + c)
                for i in range(per * half):
                    e_copy(i).wait_send()

            @when(t == 0)
            def _():
                each(0, share * C, lambda i: z_copy(i).wait_send(), p * C + c)
                each(share * C, R * C, lambda i: f_copy(i).wait_send())


def hub_call(R, C, factor, lower, upper, krylov, basis):
    tile, rows = lower.shape[1], lower.shape[2]
    width = factor.shape[2]
    nvec, nb = krylov.shape[1], basis.shape[1]
    share, per = tile // rows, tile // width
    half = share // 2
    steps = R.bit_length() - 1
    dma = pltpu.SemaphoreType.DMA
    vmem = pl.BlockSpec(memory_space=pltpu.VMEM)
    block = (2 * nvec, rows)
    f32 = lambda *shape: pltpu.VMEM(shape, F32)
    bf16 = lambda *shape: [pltpu.VMEM(shape, BF16)] * 2
    return pl.pallas_call(
        functools.partial(hub_kernel, R, C),
        out_shape=(pltpu.VMEM(krylov.shape, F32), pltpu.VMEM((2, nvec, nb), F32)),
        in_specs=[pl.BlockSpec(memory_space=pl.ANY)] * 5,
        out_specs=(vmem, vmem),
        scratch_shapes=[
            f32(*factor.shape), f32(*lower.shape), f32(*upper.shape), f32(*krylov.shape), f32(*basis.shape),
            f32(*upper.shape), f32(2, per, *factor.shape),
            *bf16(tile, 2 * rows), *bf16(tile, 4 * rows), *bf16(2 * rows + nb, 2 * tile),
            *bf16(2 * nb, 2 * rows), *bf16(2 * nb, 2 * nb + 2 * rows),
            f32(share, *basis.shape), f32(2, *basis.shape),
            f32(half, 2, *block), f32(share, 2, *block), f32(2, *block), f32(half, 2, *block),
            f32(half, 2, *block), f32(share, 2, *block), f32(share, *block), f32(2, share, *block),
            f32(share, 3 * nvec, rows), f32(half, 3 * nvec, rows),
            f32(steps + 1, nb, 2 * nb), f32(steps + 1, nb, 2 * nb),
            dma((5,)), dma((half,)), dma((share,)), dma((share,)), dma((half,)),
            dma((half,)), dma((share,)), dma((per * half,)), dma((per * half,)),
            dma((share * C,)), dma((half,)), dma((R * C,)), dma((half,)),
            dma((1,)), dma((1,)), dma((1,)), dma((2 * per,)), dma((half,)), dma((share,)), dma((1,)), dma((2,)),
            dma((steps,)), dma((steps,)), dma((C,)), dma((1,)),
            pltpu.SemaphoreType.REGULAR, pltpu.SemaphoreType.REGULAR,
        ],
        compiler_params=pltpu.CompilerParams(collective_id=0, has_side_effects=True),
        name="krylov_hubs",
    )(factor, lower, upper, krylov, basis)


def finish(projected, turned, projected_out, turned_out, sems):
    copies = [
        pltpu.make_async_copy(projected, projected_out, sems.at[0]),
        pltpu.make_async_copy(turned, turned_out, sems.at[1]),
    ]
    for copy in copies:
        copy.start()
    for copy in copies:
        copy.wait()


def general_call(R, C, factor, lower, upper, krylov, basis):
    tile, rows = lower.shape[1], lower.shape[2]
    width = factor.shape[2]
    nvec, nb = krylov.shape[1], basis.shape[1]
    share, per, pieces = tile // rows, tile // width, width // rows
    steps = R.bit_length() - 1
    dma = pltpu.SemaphoreType.DMA
    vmem = pl.BlockSpec(memory_space=pltpu.VMEM)
    block = (2 * nvec, rows)
    return pl.pallas_call(
        functools.partial(kernel, R, C),
        out_shape=(
            jax.ShapeDtypeStruct(krylov.shape, F32),
            jax.ShapeDtypeStruct((2, nvec, nb), F32),
        ),
        in_specs=[vmem] * 5,
        out_specs=(vmem, vmem),
        scratch_shapes=[
            pltpu.VMEM((2, tile, 2 * rows), BF16),
            pltpu.VMEM((2, tile, 2 * rows), BF16),
            pltpu.VMEM((rows, 2 * width), BF16),
            pltpu.VMEM((rows, 2 * width), BF16),
            pltpu.VMEM((2 * nb, 2 * rows), BF16),
            pltpu.VMEM((2 * nb, 2 * rows), BF16),
            pltpu.VMEM((2 * nb, 2 * nb + 2 * rows), BF16),
            pltpu.VMEM((2 * nb, 2 * nb + 2 * rows), BF16),
            pltpu.VMEM((2 * nb, 2 * rows), BF16),
            pltpu.VMEM((2 * nb, 2 * rows), BF16),
            pltpu.VMEM((share, 2, nb, rows), F32),
            pltpu.VMEM((2, share) + block, F32),
            pltpu.VMEM((2, share) + block, F32),
            pltpu.VMEM(block, F32),
            pltpu.VMEM(block, F32),
            pltpu.VMEM((pieces,) + block, F32),
            pltpu.VMEM(block, F32),
            pltpu.VMEM((C,) + block, F32),
            pltpu.VMEM((nvec, 2 * nb), F32),
            pltpu.VMEM((R, nvec, 2 * nb), F32),
            pltpu.VMEM((steps + 1, nb, 2 * nb), F32),
            pltpu.VMEM((steps, nb, 2 * nb), F32),
            dma((2, share)),
            dma((2, share)),
            dma((R,)),
            dma((pieces,)),
            dma((C,)),
            dma((C,)),
            dma((C // per,)),
            dma((1,)),
            dma((R,)),
            dma((R,)),
            dma((steps,)),
            dma((steps,)),
            dma((share,)),
            dma((share,)),
            dma((C // per,)),
            dma((1,)),
            pltpu.SemaphoreType.REGULAR,
        ],
        compiler_params=pltpu.CompilerParams(collective_id=0, has_side_effects=True),
        name="krylov_step",
    )(factor, lower, upper, krylov, basis)


def local(R, C, factor, lower, upper, krylov, basis):
    tile, rows = lower.shape[1], lower.shape[2]
    share, per = tile // rows, tile // factor.shape[2]
    vmem = pl.BlockSpec(memory_space=pltpu.VMEM)
    paired = R == 2 * share and C == 2 * per and share == 4 and per == 2
    call = hub_call if paired else general_call
    projected, turned = call(R, C, factor, lower, upper, krylov, basis)
    if paired:
        projected, turned = [pltpu.with_memory_space_constraint(x, pltpu.VMEM) for x in (projected, turned)]
    projected, turned = pl.pallas_call(
        finish,
        out_shape=(jax.ShapeDtypeStruct(projected.shape, F32), jax.ShapeDtypeStruct(turned.shape, F32)),
        in_specs=[vmem] * 2,
        out_specs=[pl.BlockSpec(memory_space=pl.ANY)] * 2,
        scratch_shapes=[pltpu.SemaphoreType.DMA((2,))],
        name="finish",
    )(projected, turned)
    return projected, turned.transpose(0, 2, 1)


def solution(mesh):
    in_specs = (
        P(None, "row", "col"),
        P(None, None, "row"),
        P(None, None, "row"),
        P(None, None, "row"),
        P(None, None, "row"),
    )
    out_specs = (P(None, None, "row"), P())
    body = functools.partial(local, mesh.shape["row"], mesh.shape["col"])
    return jax.shard_map(body, mesh=mesh, in_specs=in_specs, out_specs=out_specs, check_vma=False)
```

```python
import functools

import jax
import jax.numpy as jnp
from jax import lax
from jax.experimental import pallas as pl
from jax.experimental.pallas import tpu as pltpu
from jax.sharding import PartitionSpec as P

MESH = pl.DeviceIdType.MESH
F32 = jnp.float32
BF16 = jnp.bfloat16


def split(value):
    high = value.astype(BF16)
    low = (value - high.astype(F32)).astype(BF16)
    return high, low


def dot_nt(left, right):
    return lax.dot_general(left, right, (((1,), (1,)), ((), ())), preferred_element_type=F32)


def dot_nn(left, right):
    return lax.dot_general(left, right, (((1,), (0,)), ((), ())), preferred_element_type=F32)


def product(left, high, low, dot):
    rows = left.shape[0]
    left_high, left_low = split(left)
    both = dot(jnp.concatenate([left_high, left_low], 0), high)
    return both[:rows] + (both[rows:] + dot(left_high, low))


def complex_left(pieces, nvec):
    re = [x[:nvec] for x in pieces]
    im = [x[nvec:] for x in pieces]
    top = jnp.concatenate(re + [-x for x in im], 1)
    bottom = jnp.concatenate(im + re, 1)
    return jnp.concatenate([top, bottom], 0)


def kernel(
    R, C, factor, lower, upper, krylov, basis, projected, coefficients,
    inv_hi, inv_lo, fac_hi, fac_lo, bas_hi, bas_lo,
    end_hi, end_lo, lead_hi, lead_lo, gather,
    psend, precv, ybuf, xbuf, bcast, vbuf, vrecv, fsend, frecv, gacc, grecv,
    psend_sem, precv_sem, bsend_sem, brecv_sem, vsend_sem, vrecv_sem, xsend_sem, xrecv_sem,
    fsend_sem, frecv_sem, gsend_sem, grecv_sem, tsend_sem, trecv_sem, ysend_sem, yrecv_sem,
    ready_sem,
):
    tile, rows = lower.shape[1], lower.shape[2]
    width = factor.shape[2]
    nvec = krylov.shape[1]
    nb = basis.shape[1]
    share = tile // rows
    per = tile // width
    pieces = width // rows
    steps = R.bit_length() - 1
    r = lax.axis_index("row")
    c = lax.axis_index("col")
    t, p = r // share, r % share
    j, h = c // per, c % per
    solver = j == t

    barrier = pltpu.get_barrier_semaphore()

    def greet_mate(i, carry):
        pl.semaphore_signal(barrier, inc=1, device_id=(t * share + (p + 1 + i) % share, c), device_id_type=MESH)
        return carry

    def greet_tile(i, carry):
        pl.semaphore_signal(barrier, inc=1, device_id=((r + (1 + i) * share) % R, c), device_id_type=MESH)
        return carry

    def greet_col(i, carry):
        pl.semaphore_signal(barrier, inc=1, device_id=(r, (c + 1 + i) % C), device_id_type=MESH)
        return carry

    lax.fori_loop(0, share - 1, greet_mate, 0)
    lax.fori_loop(0, R // share - 1, greet_tile, 0)
    lax.fori_loop(0, C - 1, greet_col, 0)

    def prepare(ref, slot):
        high, low = split(jnp.concatenate([ref[0], ref[1]], 1))
        inv_hi[slot] = high
        inv_lo[slot] = low

    @pl.when(solver)
    def _():
        prepare(lower, 0)

    @pl.when(jnp.logical_not(solver))
    def _():
        high, low = split(jnp.concatenate([factor[0], factor[1]], 1))
        fac_hi[...] = high
        fac_lo[...] = low

    def prepare_basis():
        top = jnp.concatenate([basis[0], basis[1]], 1)
        bottom = jnp.concatenate([-basis[1], basis[0]], 1)
        high, low = split(jnp.concatenate([top, bottom], 0))
        bas_hi[...] = high
        bas_lo[...] = low
        gacc[0] = product(top, high, low, dot_nt)

    def remote(src, dst, send, recv, dest):
        return pltpu.make_async_remote_copy(
            src_ref=src, dst_ref=dst, send_sem=send, recv_sem=recv, device_id=dest, device_id_type=MESH
        )

    def each(first_index, last_index, act):
        def body(i, carry):
            act(i)
            return carry

        lax.fori_loop(first_index, last_index, body, 0)

    def gram_copy(i):
        other = r + (1 << i) * (1 - 2 * ((r // (1 << i)) % 2))
        return remote(gacc.at[i], grecv.at[i], gsend_sem.at[i], grecv_sem.at[i], (other, c))

    def gram_all():
        for i in range(steps):
            copy = gram_copy(i)
            copy.start()
            copy.wait_recv()
            gacc[i + 1] = gacc[i] + grecv[i]
        top = gacc[steps]
        gram = jnp.concatenate([top, jnp.concatenate([-top[:, nb:], top[:, :nb]], 1)], 0)
        row_id = lax.broadcasted_iota(jnp.int32, gram.shape, 0)
        col_id = lax.broadcasted_iota(jnp.int32, gram.shape, 1)
        twice = jnp.where(row_id == col_id, 2.0, 0.0) - gram
        spread = product(twice, bas_hi[...], bas_lo[...], dot_nn)
        high, low = split(jnp.concatenate([twice, spread], 1))
        end_hi[...] = high
        end_lo[...] = low

    def t_copy(d):
        q = (p + d) % share
        return remote(basis, gather.at[p], tsend_sem.at[d], trecv_sem.at[p], (t * share + q, c))

    def lead_send():
        for d in range(1, share):
            t_copy(d).start()
        gather[p] = basis[...]

    def lead_all():
        for d in range(1, share):
            q = (p + d) % share
            remote(basis, gather.at[q], tsend_sem.at[d], trecv_sem.at[q], (t * share + q, c)).wait_recv()
        left = jnp.concatenate(
            [jnp.concatenate([gather[q, i] for q in range(share)], 1) for i in range(2)], 0
        )
        out = product(left, inv_hi[1], inv_lo[1], dot_nn)
        one = out[:nb, :rows] + out[nb:, rows:]
        two = out[nb:, :rows] - out[:nb, rows:]
        whole = jnp.concatenate([jnp.concatenate([one, two], 1), jnp.concatenate([-two, one], 1)], 0)
        high, low = split(whole)
        lead_hi[...] = high
        lead_lo[...] = low

    def side_work():
        gram_all()

        @pl.when(t == 0)
        def _():
            lead_send()
            lead_all()

    def part_copy(sweep, d):
        q = (p + d) % share
        return remote(
            psend.at[sweep, q], precv.at[sweep, p], psend_sem.at[sweep, q], precv_sem.at[sweep, p], (t * share + q, c)
        )

    def part_arrival(sweep, d):
        q = (p + d) % share
        return remote(
            psend.at[sweep, q], precv.at[sweep, q], psend_sem.at[sweep, q], precv_sem.at[sweep, q], (t * share + q, c)
        ), q

    def v_copy(cc):
        return remote(vbuf, vrecv.at[c], vsend_sem.at[cc], vrecv_sem.at[c], (r, cc))

    def v_each(act):
        @pl.when(t > 0)
        def _():
            for hh in range(per):
                act(v_copy(t * per + hh))

        @pl.when(t == 0)
        def _():
            each(1, C, lambda d: act(v_copy((c + d) % C)))

    def v_sum(first_col, last_col, value):
        def body(cc, total):
            @pl.when(cc != c)
            def _():
                remote(vbuf, vrecv.at[cc], vsend_sem.at[0], vrecv_sem.at[cc], (r, cc)).wait_recv()

            return total - vrecv[cc]

        return lax.fori_loop(first_col, last_col, body, value)

    def f_copy(d):
        return remote(fsend, frecv.at[r], fsend_sem.at[d], frecv_sem.at[r], ((r + d) % R, c))

    def send_first(value, high, low):
        wide_value = jnp.concatenate([value[:nvec], value[nvec:]], 1)
        fsend[...] = product(wide_value, high, low, dot_nt)
        each(1, R, lambda d: f_copy(d).start())

    def multiply(sweep, g):
        out = product(complex_left([g], nvec), inv_hi[sweep], inv_lo[sweep], dot_nt)
        for q in range(share):
            psend[sweep, q] = out[:, q * rows:(q + 1) * rows]

    def solve(sweep, g):
        multiply(sweep, g)
        return exchange(sweep)

    def exchange(sweep):
        for d in range(1, share):
            part_copy(sweep, d).start()
        total = psend[sweep, p]
        for d in range(1, share):
            arrival, q = part_arrival(sweep, d)
            arrival.wait_recv()
            total = total + precv[sweep, q]
        return total

    def b_copy(buf, rr):
        return remote(buf, bcast.at[p % pieces], bsend_sem.at[rr], brecv_sem.at[p % pieces], (rr, c))

    def x_copy(tt):
        cc = tt * per + h
        return remote(xbuf, xbuf, xsend_sem.at[tt], xrecv_sem.at[0], (r, cc))

    def y_copy(tt):
        return remote(ybuf, ybuf, ysend_sem.at[tt], yrecv_sem.at[0], (r, tt * per + h))

    speaks = p // pieces == h

    @pl.when(solver != (t == 0))
    def _():
        prepare(upper, 1)

    @pl.when(j > 0)
    def _():
        prepare_basis()

    @pl.when(jnp.logical_and(solver, t == 0))
    def _():
        multiply(0, jnp.concatenate([krylov[0], krylov[1]], 0))

    pl.semaphore_wait(barrier, share - 1 + R // share - 1 + C - 1)
    for d in range(1, share):
        pl.semaphore_signal(
            ready_sem, inc=1, device_id=(t * share + (p + d) % share, c), device_id_type=MESH
        )

    @pl.when(j > 0)
    def _():
        side_work()

    @pl.when(solver)
    def _():
        @pl.when(t > 0)
        def _():
            b = jnp.concatenate([krylov[0], krylov[1]], 0)
            multiply(0, v_sum(0, t * per, b))

        ybuf[...] = exchange(0)
        pl.semaphore_wait(ready_sem, share - 1)

        @pl.when(speaks)
        def _():
            each((t + 1) * share, R, lambda rr: b_copy(ybuf, rr).start())

        @pl.when(t == 0)
        def _():
            each(1, C // per, lambda tt: y_copy(tt).start())
            prepare(upper, 1)

    @pl.when(jnp.logical_not(solver))
    def _():
        pl.semaphore_wait(ready_sem, share - 1)
        got = []
        for i in range(pieces):
            remote(ybuf, bcast.at[i], bsend_sem.at[0], brecv_sem.at[i], (r, t * per)).wait_recv()
            got.append(bcast[i])
        value = product(complex_left(got, nvec), fac_hi[...], fac_lo[...], dot_nt)
        vbuf[...] = value
        v_each(lambda copy: copy.start())
        vrecv[c] = value

    @pl.when(j == 0)
    def _():
        prepare_basis()
        side_work()

    @pl.when(t == 0)
    def _():
        @pl.when(jnp.logical_not(solver))
        def _():
            remote(ybuf, ybuf, ysend_sem.at[0], yrecv_sem.at[0], (r, h)).wait_recv()

        g = v_sum(per, C, ybuf[...])
        send_first(g, lead_hi[...], lead_lo[...])
        xbuf[...] = solve(1, g)

    @pl.when(t > 0)
    def _():
        @pl.when(solver)
        def _():
            xbuf[...] = solve(1, v_sum((t + 1) * per, C, ybuf[...]))

            @pl.when(speaks)
            def _():
                each(0, t * share, lambda rr: b_copy(xbuf, rr).start())

            each(0, t, lambda tt: x_copy(tt).start())
            each(t + 1, C // per, lambda tt: x_copy(tt).start())

        @pl.when(jnp.logical_not(solver))
        def _():
            remote(ybuf, xbuf, xsend_sem.at[0], xrecv_sem.at[0], (r, t * per)).wait_recv()

        send_first(xbuf[...], bas_hi[...], bas_lo[...])

    frecv[r] = fsend[...]

    def f_wait(d):
        q = (r + d) % R
        remote(fsend, frecv.at[q], fsend_sem.at[d], frecv_sem.at[q], (q, c)).wait_recv()

    each(1, R, f_wait)
    first = frecv[0]
    for i in range(1, R):
        first = first + frecv[i]
    ends = product(first, end_hi[...], end_lo[...], dot_nn)
    coefficients[0] = ends[:, :nb]
    coefficients[1] = ends[:, nb:2 * nb]
    projected[0] = xbuf[:nvec] - ends[:, 2 * nb:2 * nb + rows]
    projected[1] = xbuf[nvec:] - ends[:, 2 * nb + rows:]

    each(1, R, lambda d: f_copy(d).wait_send())
    for i in range(steps):
        gram_copy(i).wait_send()

    def parts_sent(sweep):
        for d in range(1, share):
            part_copy(sweep, d).wait_send()

    @pl.when(t == 0)
    def _():
        parts_sent(1)
        for d in range(1, share):
            t_copy(d).wait_send()

    @pl.when(solver)
    def _():
        parts_sent(0)

        @pl.when(speaks)
        def _():
            each((t + 1) * share, R, lambda rr: b_copy(ybuf, rr).wait_send())

        @pl.when(t == 0)
        def _():
            each(1, C // per, lambda tt: y_copy(tt).wait_send())

        @pl.when(t > 0)
        def _():
            parts_sent(1)

            @pl.when(speaks)
            def _():
                each(0, t * share, lambda rr: b_copy(xbuf, rr).wait_send())

            each(0, t, lambda tt: x_copy(tt).wait_send())
            each(t + 1, C // per, lambda tt: x_copy(tt).wait_send())

    @pl.when(jnp.logical_not(solver))
    def _():
        v_each(lambda copy: copy.wait_send())


def hub_kernel(
    R, C, factor, lower, upper, krylov, basis, projected, coefficients,
    fac_in, f_first, up_in, bas_in, up_recv, f_recv,
    low_hi, low_lo, up_hi, up_lo, fac_hi, fac_lo,
    bas_hi, bas_lo, end_hi, end_lo, gather, gather_one,
    asend, arecv, ybuf, yrecv, dsend, drecv, esend, erecv, gsend, xrecv, gacc, grecv,
    load_sem, send_sem, recv_sem, next_sem, all_sem,
):
    tile, rows = lower.shape[1], lower.shape[2]
    width = factor.shape[2]
    nvec = krylov.shape[1]
    nb = basis.shape[1]
    share = tile // rows
    per = tile // width
    half = share // 2
    steps = R.bit_length() - 1
    r = lax.axis_index("row")
    c = lax.axis_index("col")
    me = r * C + c
    t, p = r // share, r % share
    y, z = p % half, p // half
    lead = per - 1
    main = c == lead
    hub = main & (z == 1 - t)
    side = c == 0

    def partner(i):
        return r + (1 << i) * (1 - 2 * ((r // (1 << i)) % 2))

    def remote(src, dst, send, recv, dest):
        return pltpu.make_async_remote_copy(
            src_ref=src, dst_ref=dst, send_sem=send, recv_sem=recv, device_id=dest, device_id_type=MESH
        )

    low_in, kry_in = f_first.at[:, pl.ds(0, tile)], f_first.at[:, pl.ds(tile, nvec)]

    def load(i, src, dst):
        return pltpu.make_async_copy(src, dst, load_sem.at[i])

    @pl.when(main)
    def _():
        load(0, lower, low_in).start()
        load(0, krylov, kry_in).start()

        @pl.when(t == 1)
        def _():
            load(1, factor, fac_in).start()

        @pl.when(hub)
        def _():
            load(2, upper, up_in).start()

    load(3, basis, bas_in).start()

    barrier = pltpu.get_barrier_semaphore()
    guide = (c == per) & (t == 1) & (z == 0)
    far = (c >= per) & (t == 0)
    parted = far & (z == 0) & (c == per)
    aid = (c == C - 1) & (t == 1) & (z == 1)

    def greet(rr, cc):
        pl.semaphore_signal(barrier, inc=1, device_id=(rr, cc), device_id_type=MESH)

    @pl.when(main)
    def _():
        @pl.when(hub)
        def _():
            for d in range(1, share):
                greet(t * share + (p + d) % share, c)

        greet(r, 0)

        @pl.when(t == 1)
        def _():
            for i in range(half):
                greet(half + i, 0)

        @pl.when(hub & (t == 0))
        def _():
            for cc in range(per, C):
                greet(r, cc)
                greet(y, cc)

        @pl.when(hub & (t == 1))
        def _():
            greet(share + half + y, C - 1)

        @pl.when((t == 0) & (z == 0))
        def _():
            greet(r, per)

    @pl.when(side)
    def _():
        for i in range(steps):
            greet(partner(i), c)

    @pl.when(c >= per)
    def _():
        greet(r, 0)

    for i in range(half):
        @pl.when(jnp.logical_not(guide & (y == i)))
        def _():
            greet(share + i, per)

    def arrive():
        count = jnp.where(main, jnp.where(hub, half - 1, half), jnp.where(
            side, steps + 1 + C - per + jnp.where((t == 0) & (z == 1), share, 0),
            jnp.where(guide, R * C - 1, jnp.where(parted, 2, 1)),
        ))
        @pl.when(main | side | far | guide | aid)
        def _():
            pl.semaphore_wait(barrier, count)

        @pl.when(side & (t == 0) & (z == 1))
        def _():
            pl.semaphore_signal(next_sem, inc=1, device_id=(r, lead), device_id_type=MESH)

        @pl.when(guide)
        def _():
            for i in range(2):
                pl.semaphore_signal(all_sem, inc=1, device_id=(half * (i + 1) + y, lead), device_id_type=MESH)

    def when(cond):
        return pl.when(cond)

    def pair(ref, axis=1):
        return jnp.concatenate([ref[0], ref[1]], axis)

    block, wave, bas, fac, ups, gram = 2 * nvec, 3 * nvec, 2 * nb, 2 * width, 2 * tile, 2 * nb * nb // rows
    AD, US, MS, XS, YE, ES, TS, OS, GS = range(9)

    def take(sem, count):
        if count > ups:
            ref = f_recv.at[:, :, :, pl.ds(0, count * rows // (4 * per * width))]
        else:
            ref = up_recv.at[:, pl.ds(0, count // 2)]
        remote(ref, ref, send_sem.at[0], sem, ((r + 1) % R, c)).wait_recv()

    def send(src, dst, recv, dest, way=0):
        return remote(src, dst, send_sem.at[way], recv_sem.at[recv], dest)

    def a_copy(i):
        i = (y + 1 + i) % half
        return send(asend.at[i], arecv.at[p], AD, (half + i, c))

    def y_copy(i):
        i = (1 - i // half) * half + (y + 1 + i) % half
        return send(ybuf, yrecv.at[y], YE, (share + i, c))

    def u_copy(first, count):
        at = pl.ds(first * (tile // 2), count * (tile // 2))
        return send(upper.at[:, at], up_recv.at[:, at], US, (t * share + (1 - z) * half + y, lead))

    def m_near():
        return send(factor, f_recv.at[0, 0], MS, (r, lead))

    def m_far():
        return send(factor, f_recv.at[z, c % per], MS, (half + y, lead))

    def m_part(i):
        return send(factor.at[i], f_recv.at[0, 0, i], MS, (half * (1 - i) + y, lead))

    def m_relay():
        return send(f_recv.at[0, 0, 1], f_recv.at[0, 0, 1], MS, (half + y, lead))

    def t_copy(i):
        return send(basis, gather.at[p], TS, (half + i, lead))

    def o_copy():
        return send(basis, gather_one.at[z], OS, (half + y, lead))

    def d_copy(i):
        i = (y + 1 + i) % half
        return send(dsend.at[i], drecv.at[p], AD, (share + i, c))

    def e_copy(i):
        h, k = i // half, (y + 1 + i) % half
        at = pl.ds(h * half, half)
        return send(esend.at[at], erecv.at[y, at], YE + h, (half + k, c))

    def x_copy(i):
        k, cc = i // C, i % C
        return send(esend.at[k], xrecv.at[y, pl.ds(0, block)], XS, (t * share + k, cc))

    def f_copy(i):
        at = pl.ds(block, nvec)
        return send(gsend.at[0, at], xrecv.at[y, at], XS, (i // C, i % C), 1)

    def z_copy(i):
        k, cc = i // C, i % C
        return send(gsend.at[k], xrecv.at[y], XS, (k, cc), 1)

    def g_copy(i):
        return send(gacc.at[i], grecv.at[i], GS + i, (partner(i), c))

    def h_copy(cc):
        return send(gacc.at[steps], grecv.at[steps], GS, (r, cc))

    def each(first_index, last_index, act, skip=None):
        def body(i, carry):
            if skip is None:
                act(i)
            else:
                @pl.when(i != skip)
                def _():
                    act(i)
            return carry

        lax.fori_loop(first_index, last_index, body, 0)

    def store(hi, lo, index, value):
        high, low = split(value)
        hi[index] = high
        lo[index] = low

    def wide(value):
        return jnp.concatenate([value[:nvec], value[nvec:]], 1)

    def start_sends():
        @when(side & (t == 1))
        def _():
            m_near().start()

        @when(far & jnp.logical_not(parted))
        def _():
            m_far().start()

        @when(parted)
        def _():
            for i in range(2):
                m_part(1 - i).start()

        @when(main & (t == 1) & (z == 1))
        def _():
            u_copy(0, 1).start()

        @when(aid)
        def _():
            u_copy(1, 1).start()

    def put_slices(ref, out):
        for k in range(share):
            ref[k] = out[:, k * rows:(k + 1) * rows]

    def put_pairs(ref, out):
        for i in range(half):
            for k in range(2):
                ref[i, k] = out[:, (k * half + i) * rows:(k * half + i + 1) * rows]

    def inverse_times(hi, lo, values):
        left = jnp.concatenate([complex_left([v], nvec) for v in values], 1)
        return product(left, hi, lo, dot_nt)

    def factor_times(values, count):
        left = jnp.concatenate(
            [complex_left(values[h * half:(h + 1) * half], nvec) for h in range(per)], 1
        )
        return product(left, fac_hi[:count], fac_lo[:count], dot_nt)

    def first_loads():
        at = pl.ds(0, tile + nvec)
        pltpu.make_async_copy(f_first.at[:, at], f_first.at[:, at], load_sem.at[0]).wait()

    span = 2 * rows
    broad = 2 * width

    @when(main & (t == 0))
    def _():
        first_loads()
        store(low_hi, low_lo, ..., pair(low_in))
        put_pairs(asend, inverse_times(low_hi[...], low_lo[...], [pair(kry_in, 0)]))

    arrive()

    @when(main & (t == 0))
    def _():
        each(0, jnp.where(hub, half - 1, half), lambda i: a_copy(i).start())

    start_sends()

    @when(main & (t == 0))
    def _():
        @when(hub)
        def _():
            arecv[p] = asend[y]
            take(recv_sem.at[AD], (share - 1) * 2 * block)
            parts = [arecv[q] for q in range(share)]
            ybuf[...] = (parts[0] + parts[1]) + (parts[2] + parts[3])
            pl.semaphore_wait(next_sem, 1)
            for i in range(share):
                y_copy(i).start()

        each(0, half, lambda i: t_copy(i).start(), jnp.where(hub, y, half))

        @when(jnp.logical_not(hub))
        def _():
            u_copy(0, 2).start()
            take(recv_sem.at[MS], fac // 2)
            m_relay().start()

    load(3, basis, bas_in).wait()

    def prepare_basis():
        top = pair(bas_in)
        bottom = jnp.concatenate([-bas_in[1], bas_in[0]], 1)
        store(bas_hi, bas_lo, ..., jnp.concatenate([top, bottom], 0))
        return top

    def prepare_end(top):
        gram = jnp.concatenate([top, jnp.concatenate([-top[:, nb:], top[:, :nb]], 1)], 0)
        row_id = lax.broadcasted_iota(jnp.int32, gram.shape, 0)
        col_id = lax.broadcasted_iota(jnp.int32, gram.shape, 1)
        twice = jnp.where(row_id == col_id, 2.0, 0.0) - gram
        spread = product(twice, bas_hi[...], bas_lo[...], dot_nn)
        store(end_hi, end_lo, ..., jnp.concatenate([twice, spread], 1))

    def end_from_side():
        prepare_basis()
        take(recv_sem.at[GS], gram)
        prepare_end(grecv[steps])

    @when(side)
    def _():
        gacc[0] = product(prepare_basis(), bas_hi[...], bas_lo[...], dot_nt)
        for i in range(steps):
            g_copy(i).start()
            take(recv_sem.at[GS + i], gram)
            gacc[i + 1] = gacc[i] + grecv[i]
        each(1, C, lambda cc: h_copy(cc).start())
        prepare_end(gacc[steps])

    @when(c > lead)
    def _():
        end_from_side()

    @when(main & (t == 1))
    def _():
        first_loads()
        load(1, factor, fac_in).wait()
        store(low_hi, low_lo, ..., pair(low_in))
        store(fac_hi, fac_lo, (slice(0, rows), slice(broad, 2 * broad)), pair(fac_in))
        take(recv_sem.at[MS], fac)
        store(fac_hi, fac_lo, (slice(0, rows), slice(0, broad)), pair(f_recv.at[0, 0]))

        @when(hub)
        def _():
            load(2, upper, up_in).wait()
            store(up_hi, up_lo, (slice(None), slice(0, span)), pair(up_in))

        take(recv_sem.at[YE], half * 2 * block)
        g = pair(kry_in, 0) - factor_times([yrecv[q % half, q // half] for q in range(share)], rows)
        put_pairs(dsend, inverse_times(low_hi[...], low_lo[...], [g]))
        each(0, jnp.where(hub, half - 1, half), lambda i: d_copy(i).start())
        o_copy().start()

        @when(hub)
        def _():
            drecv[p] = dsend[y]
            take(recv_sem.at[US], ups)
            store(up_hi, up_lo, (slice(None), slice(span, 2 * span)), pair(up_recv))

            take(recv_sem.at[AD], (share - 1) * 2 * block)
            parts = [drecv[q] for q in range(share)]
            total = (parts[0] + parts[1]) + (parts[2] + parts[3])
            put_slices(esend, inverse_times(up_hi[...], up_lo[...], [total[0], total[1]]))
            for i in range(per * half):
                e_copy(i).start()
            pl.semaphore_wait(all_sem, 1)
            each(0, share * C, lambda i: x_copy(i).start(), p * C + c)
            xrecv[y, :block] = esend[p]

        end_from_side()

    @when(main & (t == 0))
    def _():
        @when(hub)
        def _():
            load(2, upper, up_in).wait()
            store(up_hi, up_lo, (slice(None), slice(span, 2 * span)), pair(up_in))
            gather[p] = bas_in[...]
            take(recv_sem.at[TS], (share - 1) * bas)
            stacked = jnp.concatenate(
                [jnp.concatenate([gather[q, i] for q in range(share)], 1) for i in range(2)], 0
            )
            take(recv_sem.at[US], ups)
            store(up_hi, up_lo, (slice(None), slice(0, span)), pair(up_recv))
            real, imag = [], []
            for k in range(2):
                at = slice(k * span, (k + 1) * span)
                out = product(stacked, up_hi[:, at], up_lo[:, at], dot_nn)
                real.append(out[:nb, :rows] + out[nb:, rows:])
                imag.append(out[:nb, rows:] - out[nb:, :rows])
            real, imag = jnp.concatenate(real, 1), jnp.concatenate(imag, 1)
            high, low = split(jnp.concatenate([real, imag], 1))
            known = product(complex_left([ybuf[0], ybuf[1]], nvec), high, low, dot_nt)
            take(recv_sem.at[MS], 2 * per * fac)
            for h in range(per):
                for k in range(2):
                    store(
                        fac_hi, fac_lo, (slice(k * rows, (k + 1) * rows), slice(h * broad, (h + 1) * broad)),
                        pair(f_recv.at[k, h]),
                    )
            take(recv_sem.at[OS], 2 * bas)
            empty = jnp.zeros((nb, rows), F32)
            for h in range(per):
                at = slice(h * broad, (h + 1) * broad)
                out = product(
                    jnp.concatenate([real, imag], 0), fac_hi[:span, at], fac_lo[:span, at], dot_nn
                )
                one = gather_one[h]
                own_re = jnp.where(y == 0, jnp.concatenate([one[0], empty], 1), jnp.concatenate([empty, one[0]], 1))
                own_im = jnp.where(y == 0, jnp.concatenate([one[1], empty], 1), jnp.concatenate([empty, one[1]], 1))
                store(fac_hi, fac_lo, (slice(span, span + nb), at), jnp.concatenate([
                    own_re - (out[:nb, :width] - out[nb:, width:]),
                    -own_im - (out[:nb, width:] + out[nb:, :width]),
                ], 1))
            pl.semaphore_wait(all_sem, 1)

            out = 0.0
            for h in range(per):
                take(recv_sem.at[YE + h], half * half * block)
                x = [erecv[0, h * half + k] + erecv[1, h * half + k] for k in range(half)]
                at = slice(h * broad, (h + 1) * broad)
                out = out + product(complex_left(x, nvec), fac_hi[:, at], fac_lo[:, at], dot_nt)
            w = [ybuf[k] - out[:, k * rows:(k + 1) * rows] for k in range(2)]
            first = wide(known + out[:, span:])
            for k in range(share):
                gsend[k, block:] = first
            out = inverse_times(up_hi[...], up_lo[...], w)
            for k in range(share):
                gsend[k, :block] = out[:, k * rows:(k + 1) * rows]
            each(0, share * C, lambda i: z_copy(i).start(), p * C + c)
            each(share * C, R * C, lambda i: f_copy(i).start())
            xrecv[y] = gsend[p]
            end_from_side()

        @when(jnp.logical_not(hub))
        def _():
            end_from_side()

    @when(jnp.logical_not(hub))
    def _():
        take(recv_sem.at[XS], 2 * wave)

    for i in range(2):
        @when(hub & (t == i))
        def _():
            take(recv_sem.at[XS], wave + i * nvec)

    total = xrecv[0] + xrecv[1]
    ends = product(total[block:], end_hi[...], end_lo[...], dot_nn)
    coefficients[0] = ends[:, :nb]
    coefficients[1] = ends[:, nb:2 * nb]
    projected[0] = total[:nvec] - ends[:, 2 * nb:2 * nb + rows]
    projected[1] = total[nvec:block] - ends[:, 2 * nb + rows:]

    def sent(cond, count, way=0):
        @when(cond)
        def _():
            take(send_sem.at[way], count)

    others = share * C - 1
    sent(main & (t == 0) & (z == 0), half * (2 * block + bas) + ups + fac // 2)
    sent(hub & (t == 0), (half - 1) * (2 * block + bas) + share * 2 * block)
    sent(hub & (t == 0), others * wave + share * C * nvec, 1)
    sent(main & (t == 1) & (z == 1), half * 2 * block + bas + ups // 2)
    sent(hub & (t == 1), (half - 1) * 2 * block + bas + half * share * block + others * block)
    sent(side & (t == 0), (steps + C - 1) * gram)
    sent(side & (t == 1), (steps + C - 1) * gram + fac)
    sent(far, fac)
    sent(aid, ups // 2)


def hub_call(R, C, factor, lower, upper, krylov, basis):
    tile, rows = lower.shape[1], lower.shape[2]
    width = factor.shape[2]
    nvec, nb = krylov.shape[1], basis.shape[1]
    share, per = tile // rows, tile // width
    half = share // 2
    steps = R.bit_length() - 1
    dma = pltpu.SemaphoreType.DMA
    vmem = pl.BlockSpec(memory_space=pltpu.VMEM)
    block = (2 * nvec, rows)
    f32 = lambda *shape: pltpu.VMEM(shape, F32)
    bf16 = lambda *shape: [pltpu.VMEM(shape, BF16)] * 2
    return pl.pallas_call(
        functools.partial(hub_kernel, R, C),
        out_shape=(pltpu.VMEM(krylov.shape, F32), pltpu.VMEM((2, nvec, nb), F32)),
        in_specs=[pl.BlockSpec(memory_space=pl.ANY)] * 5,
        out_specs=(vmem, vmem),
        scratch_shapes=[
            f32(*factor.shape), f32(2, tile + nvec, rows), f32(*upper.shape), f32(*basis.shape),
            f32(*upper.shape), f32(2, per, *factor.shape),
            *bf16(tile, 2 * rows), *bf16(tile, 4 * rows), *bf16(2 * rows + nb, 2 * tile),
            *bf16(2 * nb, 2 * rows), *bf16(2 * nb, 2 * nb + 2 * rows),
            f32(share, *basis.shape), f32(2, *basis.shape),
            f32(half, 2, *block), f32(share, 2, *block), f32(2, *block), f32(half, 2, *block),
            f32(half, 2, *block), f32(share, 2, *block), f32(share, *block), f32(2, share, *block),
            f32(share, 3 * nvec, rows), f32(half, 3 * nvec, rows),
            f32(steps + 1, nb, 2 * nb), f32(steps + 1, nb, 2 * nb),
            dma((4,)), dma((2,)), dma((8 + steps,)),
            pltpu.SemaphoreType.REGULAR, pltpu.SemaphoreType.REGULAR,
        ],
        compiler_params=pltpu.CompilerParams(collective_id=0, has_side_effects=True),
        name="krylov_hubs",
    )(factor, lower, upper, krylov, basis)


def finish(projected, turned, projected_out, turned_out, sems):
    copies = [
        pltpu.make_async_copy(projected, projected_out, sems.at[0]),
        pltpu.make_async_copy(turned, turned_out, sems.at[1]),
    ]
    for copy in copies:
        copy.start()
    for copy in copies:
        copy.wait()


def general_call(R, C, factor, lower, upper, krylov, basis):
    tile, rows = lower.shape[1], lower.shape[2]
    width = factor.shape[2]
    nvec, nb = krylov.shape[1], basis.shape[1]
    share, per, pieces = tile // rows, tile // width, width // rows
    steps = R.bit_length() - 1
    dma = pltpu.SemaphoreType.DMA
    vmem = pl.BlockSpec(memory_space=pltpu.VMEM)
    block = (2 * nvec, rows)
    return pl.pallas_call(
        functools.partial(kernel, R, C),
        out_shape=(
            jax.ShapeDtypeStruct(krylov.shape, F32),
            jax.ShapeDtypeStruct((2, nvec, nb), F32),
        ),
        in_specs=[vmem] * 5,
        out_specs=(vmem, vmem),
        scratch_shapes=[
            pltpu.VMEM((2, tile, 2 * rows), BF16),
            pltpu.VMEM((2, tile, 2 * rows), BF16),
            pltpu.VMEM((rows, 2 * width), BF16),
            pltpu.VMEM((rows, 2 * width), BF16),
            pltpu.VMEM((2 * nb, 2 * rows), BF16),
            pltpu.VMEM((2 * nb, 2 * rows), BF16),
            pltpu.VMEM((2 * nb, 2 * nb + 2 * rows), BF16),
            pltpu.VMEM((2 * nb, 2 * nb + 2 * rows), BF16),
            pltpu.VMEM((2 * nb, 2 * rows), BF16),
            pltpu.VMEM((2 * nb, 2 * rows), BF16),
            pltpu.VMEM((share, 2, nb, rows), F32),
            pltpu.VMEM((2, share) + block, F32),
            pltpu.VMEM((2, share) + block, F32),
            pltpu.VMEM(block, F32),
            pltpu.VMEM(block, F32),
            pltpu.VMEM((pieces,) + block, F32),
            pltpu.VMEM(block, F32),
            pltpu.VMEM((C,) + block, F32),
            pltpu.VMEM((nvec, 2 * nb), F32),
            pltpu.VMEM((R, nvec, 2 * nb), F32),
            pltpu.VMEM((steps + 1, nb, 2 * nb), F32),
            pltpu.VMEM((steps, nb, 2 * nb), F32),
            dma((2, share)),
            dma((2, share)),
            dma((R,)),
            dma((pieces,)),
            dma((C,)),
            dma((C,)),
            dma((C // per,)),
            dma((1,)),
            dma((R,)),
            dma((R,)),
            dma((steps,)),
            dma((steps,)),
            dma((share,)),
            dma((share,)),
            dma((C // per,)),
            dma((1,)),
            pltpu.SemaphoreType.REGULAR,
        ],
        compiler_params=pltpu.CompilerParams(collective_id=0, has_side_effects=True),
        name="krylov_step",
    )(factor, lower, upper, krylov, basis)


def local(R, C, factor, lower, upper, krylov, basis):
    tile, rows = lower.shape[1], lower.shape[2]
    share, per = tile // rows, tile // factor.shape[2]
    vmem = pl.BlockSpec(memory_space=pltpu.VMEM)
    paired = R == 2 * share and C == 2 * per and share == 4 and per == 2
    call = hub_call if paired else general_call
    projected, turned = call(R, C, factor, lower, upper, krylov, basis)
    if paired:
        projected, turned = [pltpu.with_memory_space_constraint(x, pltpu.VMEM) for x in (projected, turned)]
    projected, turned = pl.pallas_call(
        finish,
        out_shape=(jax.ShapeDtypeStruct(projected.shape, F32), jax.ShapeDtypeStruct(turned.shape, F32)),
        in_specs=[vmem] * 2,
        out_specs=[pl.BlockSpec(memory_space=pl.ANY)] * 2,
        scratch_shapes=[pltpu.SemaphoreType.DMA((2,))],
        name="finish",
    )(projected, turned)
    return projected, turned.transpose(0, 2, 1)


def solution(mesh):
    in_specs = (
        P(None, "row", "col"),
        P(None, None, "row"),
        P(None, None, "row"),
        P(None, None, "row"),
        P(None, None, "row"),
    )
    out_specs = (P(None, None, "row"), P())
    body = functools.partial(local, mesh.shape["row"], mesh.shape["col"])
    return jax.shard_map(body, mesh=mesh, in_specs=in_specs, out_specs=out_specs, check_vma=False)
```

```python
import functools

import jax
import jax.numpy as jnp
from jax import lax
from jax.experimental import pallas as pl
from jax.experimental.pallas import tpu as pltpu
from jax.sharding import PartitionSpec as P

MESH = pl.DeviceIdType.MESH
F32 = jnp.float32
BF16 = jnp.bfloat16


def split(value):
    high = value.astype(BF16)
    low = (value - high.astype(F32)).astype(BF16)
    return high, low


def dot_nt(left, right):
    return lax.dot_general(left, right, (((1,), (1,)), ((), ())), preferred_element_type=F32)


def dot_nn(left, right):
    return lax.dot_general(left, right, (((1,), (0,)), ((), ())), preferred_element_type=F32)


def product(left, high, low, dot):
    rows = left.shape[0]
    left_high, left_low = split(left)
    both = dot(jnp.concatenate([left_high, left_low], 0), high)
    return both[:rows] + (both[rows:] + dot(left_high, low))


def complex_left(pieces, nvec):
    re = [x[:nvec] for x in pieces]
    im = [x[nvec:] for x in pieces]
    top = jnp.concatenate(re + [-x for x in im], 1)
    bottom = jnp.concatenate(im + re, 1)
    return jnp.concatenate([top, bottom], 0)


def kernel(
    R, C, factor, lower, upper, krylov, basis, projected, coefficients,
    inv_hi, inv_lo, fac_hi, fac_lo, bas_hi, bas_lo,
    end_hi, end_lo, lead_hi, lead_lo, gather,
    psend, precv, ybuf, xbuf, bcast, vbuf, vrecv, fsend, frecv, gacc, grecv,
    psend_sem, precv_sem, bsend_sem, brecv_sem, vsend_sem, vrecv_sem, xsend_sem, xrecv_sem,
    fsend_sem, frecv_sem, gsend_sem, grecv_sem, tsend_sem, trecv_sem, ysend_sem, yrecv_sem,
    ready_sem,
):
    tile, rows = lower.shape[1], lower.shape[2]
    width = factor.shape[2]
    nvec = krylov.shape[1]
    nb = basis.shape[1]
    share = tile // rows
    per = tile // width
    pieces = width // rows
    steps = R.bit_length() - 1
    r = lax.axis_index("row")
    c = lax.axis_index("col")
    t, p = r // share, r % share
    j, h = c // per, c % per
    solver = j == t

    barrier = pltpu.get_barrier_semaphore()

    def greet_mate(i, carry):
        pl.semaphore_signal(barrier, inc=1, device_id=(t * share + (p + 1 + i) % share, c), device_id_type=MESH)
        return carry

    def greet_tile(i, carry):
        pl.semaphore_signal(barrier, inc=1, device_id=((r + (1 + i) * share) % R, c), device_id_type=MESH)
        return carry

    def greet_col(i, carry):
        pl.semaphore_signal(barrier, inc=1, device_id=(r, (c + 1 + i) % C), device_id_type=MESH)
        return carry

    lax.fori_loop(0, share - 1, greet_mate, 0)
    lax.fori_loop(0, R // share - 1, greet_tile, 0)
    lax.fori_loop(0, C - 1, greet_col, 0)

    def prepare(ref, slot):
        high, low = split(jnp.concatenate([ref[0], ref[1]], 1))
        inv_hi[slot] = high
        inv_lo[slot] = low

    @pl.when(solver)
    def _():
        prepare(lower, 0)

    @pl.when(jnp.logical_not(solver))
    def _():
        high, low = split(jnp.concatenate([factor[0], factor[1]], 1))
        fac_hi[...] = high
        fac_lo[...] = low

    def prepare_basis():
        top = jnp.concatenate([basis[0], basis[1]], 1)
        bottom = jnp.concatenate([-basis[1], basis[0]], 1)
        high, low = split(jnp.concatenate([top, bottom], 0))
        bas_hi[...] = high
        bas_lo[...] = low
        gacc[0] = product(top, high, low, dot_nt)

    def remote(src, dst, send, recv, dest):
        return pltpu.make_async_remote_copy(
            src_ref=src, dst_ref=dst, send_sem=send, recv_sem=recv, device_id=dest, device_id_type=MESH
        )

    def each(first_index, last_index, act):
        def body(i, carry):
            act(i)
            return carry

        lax.fori_loop(first_index, last_index, body, 0)

    def gram_copy(i):
        other = r + (1 << i) * (1 - 2 * ((r // (1 << i)) % 2))
        return remote(gacc.at[i], grecv.at[i], gsend_sem.at[i], grecv_sem.at[i], (other, c))

    def gram_all():
        for i in range(steps):
            copy = gram_copy(i)
            copy.start()
            copy.wait_recv()
            gacc[i + 1] = gacc[i] + grecv[i]
        top = gacc[steps]
        gram = jnp.concatenate([top, jnp.concatenate([-top[:, nb:], top[:, :nb]], 1)], 0)
        row_id = lax.broadcasted_iota(jnp.int32, gram.shape, 0)
        col_id = lax.broadcasted_iota(jnp.int32, gram.shape, 1)
        twice = jnp.where(row_id == col_id, 2.0, 0.0) - gram
        spread = product(twice, bas_hi[...], bas_lo[...], dot_nn)
        high, low = split(jnp.concatenate([twice, spread], 1))
        end_hi[...] = high
        end_lo[...] = low

    def t_copy(d):
        q = (p + d) % share
        return remote(basis, gather.at[p], tsend_sem.at[d], trecv_sem.at[p], (t * share + q, c))

    def lead_send():
        for d in range(1, share):
            t_copy(d).start()
        gather[p] = basis[...]

    def lead_all():
        for d in range(1, share):
            q = (p + d) % share
            remote(basis, gather.at[q], tsend_sem.at[d], trecv_sem.at[q], (t * share + q, c)).wait_recv()
        left = jnp.concatenate(
            [jnp.concatenate([gather[q, i] for q in range(share)], 1) for i in range(2)], 0
        )
        out = product(left, inv_hi[1], inv_lo[1], dot_nn)
        one = out[:nb, :rows] + out[nb:, rows:]
        two = out[nb:, :rows] - out[:nb, rows:]
        whole = jnp.concatenate([jnp.concatenate([one, two], 1), jnp.concatenate([-two, one], 1)], 0)
        high, low = split(whole)
        lead_hi[...] = high
        lead_lo[...] = low

    def side_work():
        gram_all()

        @pl.when(t == 0)
        def _():
            lead_send()
            lead_all()

    def part_copy(sweep, d):
        q = (p + d) % share
        return remote(
            psend.at[sweep, q], precv.at[sweep, p], psend_sem.at[sweep, q], precv_sem.at[sweep, p], (t * share + q, c)
        )

    def part_arrival(sweep, d):
        q = (p + d) % share
        return remote(
            psend.at[sweep, q], precv.at[sweep, q], psend_sem.at[sweep, q], precv_sem.at[sweep, q], (t * share + q, c)
        ), q

    def v_copy(cc):
        return remote(vbuf, vrecv.at[c], vsend_sem.at[cc], vrecv_sem.at[c], (r, cc))

    def v_each(act):
        @pl.when(t > 0)
        def _():
            for hh in range(per):
                act(v_copy(t * per + hh))

        @pl.when(t == 0)
        def _():
            each(1, C, lambda d: act(v_copy((c + d) % C)))

    def v_sum(first_col, last_col, value):
        def body(cc, total):
            @pl.when(cc != c)
            def _():
                remote(vbuf, vrecv.at[cc], vsend_sem.at[0], vrecv_sem.at[cc], (r, cc)).wait_recv()

            return total - vrecv[cc]

        return lax.fori_loop(first_col, last_col, body, value)

    def f_copy(d):
        return remote(fsend, frecv.at[r], fsend_sem.at[d], frecv_sem.at[r], ((r + d) % R, c))

    def send_first(value, high, low):
        wide_value = jnp.concatenate([value[:nvec], value[nvec:]], 1)
        fsend[...] = product(wide_value, high, low, dot_nt)
        each(1, R, lambda d: f_copy(d).start())

    def multiply(sweep, g):
        out = product(complex_left([g], nvec), inv_hi[sweep], inv_lo[sweep], dot_nt)
        for q in range(share):
            psend[sweep, q] = out[:, q * rows:(q + 1) * rows]

    def solve(sweep, g):
        multiply(sweep, g)
        return exchange(sweep)

    def exchange(sweep):
        for d in range(1, share):
            part_copy(sweep, d).start()
        total = psend[sweep, p]
        for d in range(1, share):
            arrival, q = part_arrival(sweep, d)
            arrival.wait_recv()
            total = total + precv[sweep, q]
        return total

    def b_copy(buf, rr):
        return remote(buf, bcast.at[p % pieces], bsend_sem.at[rr], brecv_sem.at[p % pieces], (rr, c))

    def x_copy(tt):
        cc = tt * per + h
        return remote(xbuf, xbuf, xsend_sem.at[tt], xrecv_sem.at[0], (r, cc))

    def y_copy(tt):
        return remote(ybuf, ybuf, ysend_sem.at[tt], yrecv_sem.at[0], (r, tt * per + h))

    speaks = p // pieces == h

    @pl.when(solver != (t == 0))
    def _():
        prepare(upper, 1)

    @pl.when(j > 0)
    def _():
        prepare_basis()

    @pl.when(jnp.logical_and(solver, t == 0))
    def _():
        multiply(0, jnp.concatenate([krylov[0], krylov[1]], 0))

    pl.semaphore_wait(barrier, share - 1 + R // share - 1 + C - 1)
    for d in range(1, share):
        pl.semaphore_signal(
            ready_sem, inc=1, device_id=(t * share + (p + d) % share, c), device_id_type=MESH
        )

    @pl.when(j > 0)
    def _():
        side_work()

    @pl.when(solver)
    def _():
        @pl.when(t > 0)
        def _():
            b = jnp.concatenate([krylov[0], krylov[1]], 0)
            multiply(0, v_sum(0, t * per, b))

        ybuf[...] = exchange(0)
        pl.semaphore_wait(ready_sem, share - 1)

        @pl.when(speaks)
        def _():
            each((t + 1) * share, R, lambda rr: b_copy(ybuf, rr).start())

        @pl.when(t == 0)
        def _():
            each(1, C // per, lambda tt: y_copy(tt).start())
            prepare(upper, 1)

    @pl.when(jnp.logical_not(solver))
    def _():
        pl.semaphore_wait(ready_sem, share - 1)
        got = []
        for i in range(pieces):
            remote(ybuf, bcast.at[i], bsend_sem.at[0], brecv_sem.at[i], (r, t * per)).wait_recv()
            got.append(bcast[i])
        value = product(complex_left(got, nvec), fac_hi[...], fac_lo[...], dot_nt)
        vbuf[...] = value
        v_each(lambda copy: copy.start())
        vrecv[c] = value

    @pl.when(j == 0)
    def _():
        prepare_basis()
        side_work()

    @pl.when(t == 0)
    def _():
        @pl.when(jnp.logical_not(solver))
        def _():
            remote(ybuf, ybuf, ysend_sem.at[0], yrecv_sem.at[0], (r, h)).wait_recv()

        g = v_sum(per, C, ybuf[...])
        send_first(g, lead_hi[...], lead_lo[...])
        xbuf[...] = solve(1, g)

    @pl.when(t > 0)
    def _():
        @pl.when(solver)
        def _():
            xbuf[...] = solve(1, v_sum((t + 1) * per, C, ybuf[...]))

            @pl.when(speaks)
            def _():
                each(0, t * share, lambda rr: b_copy(xbuf, rr).start())

            each(0, t, lambda tt: x_copy(tt).start())
            each(t + 1, C // per, lambda tt: x_copy(tt).start())

        @pl.when(jnp.logical_not(solver))
        def _():
            remote(ybuf, xbuf, xsend_sem.at[0], xrecv_sem.at[0], (r, t * per)).wait_recv()

        send_first(xbuf[...], bas_hi[...], bas_lo[...])

    frecv[r] = fsend[...]

    def f_wait(d):
        q = (r + d) % R
        remote(fsend, frecv.at[q], fsend_sem.at[d], frecv_sem.at[q], (q, c)).wait_recv()

    each(1, R, f_wait)
    first = frecv[0]
    for i in range(1, R):
        first = first + frecv[i]
    ends = product(first, end_hi[...], end_lo[...], dot_nn)
    coefficients[0] = ends[:, :nb]
    coefficients[1] = ends[:, nb:2 * nb]
    projected[0] = xbuf[:nvec] - ends[:, 2 * nb:2 * nb + rows]
    projected[1] = xbuf[nvec:] - ends[:, 2 * nb + rows:]

    each(1, R, lambda d: f_copy(d).wait_send())
    for i in range(steps):
        gram_copy(i).wait_send()

    def parts_sent(sweep):
        for d in range(1, share):
            part_copy(sweep, d).wait_send()

    @pl.when(t == 0)
    def _():
        parts_sent(1)
        for d in range(1, share):
            t_copy(d).wait_send()

    @pl.when(solver)
    def _():
        parts_sent(0)

        @pl.when(speaks)
        def _():
            each((t + 1) * share, R, lambda rr: b_copy(ybuf, rr).wait_send())

        @pl.when(t == 0)
        def _():
            each(1, C // per, lambda tt: y_copy(tt).wait_send())

        @pl.when(t > 0)
        def _():
            parts_sent(1)

            @pl.when(speaks)
            def _():
                each(0, t * share, lambda rr: b_copy(xbuf, rr).wait_send())

            each(0, t, lambda tt: x_copy(tt).wait_send())
            each(t + 1, C // per, lambda tt: x_copy(tt).wait_send())

    @pl.when(jnp.logical_not(solver))
    def _():
        v_each(lambda copy: copy.wait_send())


def hub_kernel(
    R, C, factor, lower, upper, krylov, basis, projected, coefficients,
    fac_in, f_first, up_in, bas_in, up_recv, f_recv,
    low_hi, low_lo, up_hi, up_lo, fac_hi, fac_lo,
    bas_hi, bas_lo, end_hi, end_lo, gather, gather_one,
    asend, arecv, ybuf, yrecv, dsend, drecv, esend, erecv, gsend, xrecv, gacc, grecv,
    load_sem, send_sem, recv_sem, next_sem, all_sem,
):
    tile, rows = lower.shape[1], lower.shape[2]
    width = factor.shape[2]
    nvec = krylov.shape[1]
    nb = basis.shape[1]
    share = tile // rows
    per = tile // width
    half = share // 2
    steps = R.bit_length() - 1
    r = lax.axis_index("row")
    c = lax.axis_index("col")
    me = r * C + c
    t, p = r // share, r % share
    y, z = p % half, p // half
    lead = per - 1
    main = c == lead
    hub = main & (z == 1 - t)
    side = c == 0

    def partner(i):
        return r + (1 << i) * (1 - 2 * ((r // (1 << i)) % 2))

    def remote(src, dst, send, recv, dest):
        return pltpu.make_async_remote_copy(
            src_ref=src, dst_ref=dst, send_sem=send, recv_sem=recv, device_id=dest, device_id_type=MESH
        )

    low_in, kry_in = f_first.at[:, pl.ds(0, tile)], f_first.at[:, pl.ds(tile, nvec)]

    def load(i, src, dst):
        return pltpu.make_async_copy(src, dst, load_sem.at[i])

    @pl.when(main)
    def _():
        load(0, lower, low_in).start()
        load(0, krylov, kry_in).start()

        @pl.when(t == 1)
        def _():
            load(1, factor, fac_in).start()

        @pl.when(hub)
        def _():
            load(2, upper, up_in).start()

    load(3, basis, bas_in).start()

    barrier = pltpu.get_barrier_semaphore()
    guide = (c == per) & (t == 1) & (z == 0)
    far = (c >= per) & (t == 0)
    parted = far & (z == 0) & (c == per)
    aid = (c == C - 1) & (t == 1) & (z == 1)

    def greet(rr, cc):
        pl.semaphore_signal(barrier, inc=1, device_id=(rr, cc), device_id_type=MESH)

    @pl.when(main)
    def _():
        @pl.when(hub)
        def _():
            for d in range(1, share):
                greet(t * share + (p + d) % share, c)

        greet(r, 0)

        @pl.when(t == 1)
        def _():
            for i in range(half):
                greet(half + i, 0)

        @pl.when(hub & (t == 0))
        def _():
            for cc in range(per, C):
                greet(r, cc)
                greet(y, cc)

        @pl.when(hub & (t == 1))
        def _():
            greet(share + half + y, C - 1)

        @pl.when((t == 0) & (z == 0))
        def _():
            greet(r, per)

    @pl.when(side)
    def _():
        for i in range(steps):
            greet(partner(i), c)

    @pl.when(c >= per)
    def _():
        greet(r, 0)

    for i in range(half):
        @pl.when(jnp.logical_not(guide & (y == i)))
        def _():
            greet(share + i, per)

    def arrive():
        count = jnp.where(main, jnp.where(hub, half - 1, half), jnp.where(
            side, steps + 1 + C - per + jnp.where((t == 0) & (z == 1), share, 0),
            jnp.where(guide, R * C - 1, jnp.where(parted, 2, 1)),
        ))
        @pl.when(main | side | far | guide | aid)
        def _():
            pl.semaphore_wait(barrier, count)

        @pl.when(side & (t == 0) & (z == 1))
        def _():
            pl.semaphore_signal(next_sem, inc=1, device_id=(r, lead), device_id_type=MESH)

        @pl.when(guide)
        def _():
            for i in range(2):
                pl.semaphore_signal(all_sem, inc=1, device_id=(half * (i + 1) + y, lead), device_id_type=MESH)

    def when(cond):
        return pl.when(cond)

    def pair(ref, axis=1):
        return jnp.concatenate([ref[0], ref[1]], axis)

    block, wave, bas, fac, ups, gram = 2 * nvec, 3 * nvec, 2 * nb, 2 * width, 2 * tile, 2 * nb * nb // rows
    AD, US, XS, YE, ES, TS, VS, OS, GS = range(9)
    MS = GS + steps

    def take(sem, count):
        if count > ups:
            ref = f_recv.at[:, :, :, pl.ds(0, count * rows // (4 * per * width))]
        else:
            ref = up_recv.at[:, pl.ds(0, count // 2)]
        remote(ref, ref, send_sem.at[0], sem, ((r + 1) % R, c)).wait_recv()

    def send(src, dst, recv, dest, way=0):
        return remote(src, dst, send_sem.at[way], recv_sem.at[recv], dest)

    def a_copy(i):
        i = (y + 1 + i) % half
        return send(asend.at[i], arecv.at[p], AD, (half + i, c))

    def y_copy(i):
        i = (1 - i // half) * half + (y + 1 + i) % half
        return send(ybuf, yrecv.at[y], YE, (share + i, c))

    def u_copy(first, count):
        at = pl.ds(first * (tile // 2), count * (tile // 2))
        return send(upper.at[:, at], up_recv.at[:, at], US, (t * share + (1 - z) * half + y, lead))

    def m_near():
        return send(factor, f_recv.at[0, 0], MS, (r, lead))

    def m_far():
        return send(factor, f_recv.at[z, c % per], MS + z * per + c % per, (half + y, lead))

    def m_part(i):
        return send(factor.at[i], f_recv.at[0, 0, i], MS, (half * (1 - i) + y, lead))

    def m_relay():
        return send(f_recv.at[0, 0, 1], f_recv.at[0, 0, 1], MS, (half + y, lead))

    def t_copy():
        return send(basis, gather.at[p], TS, (half + y, lead))

    def v_copy(i):
        if i == 0:
            return send(basis, gather.at[p], VS, (half + (y + 1) % half, lead))
        return send(gather.at[y], gather.at[y], VS, (half + (y + 1) % half, lead))

    def o_copy():
        return send(basis, gather_one.at[z], OS, (half + y, lead))

    def d_copy(i):
        i = (y + 1 + i) % half
        return send(dsend.at[i], drecv.at[p], AD, (share + i, c))

    def e_copy(i):
        h, k = i // half, (y + 1 + i) % half
        at = pl.ds(h * half, half)
        return send(esend.at[at], erecv.at[y, at], YE + h, (half + k, c))

    def x_copy(i):
        k, cc = i // C, i % C
        return send(esend.at[k], xrecv.at[y, pl.ds(0, block)], XS, (t * share + k, cc))

    def f_copy(i):
        at = pl.ds(block, nvec)
        return send(gsend.at[0, at], xrecv.at[y, at], XS, (i // C, i % C), 1)

    def z_copy(i):
        k, cc = i // C, i % C
        return send(gsend.at[k], xrecv.at[y], XS, (k, cc), 1)

    def g_copy(i):
        return send(gacc.at[i], grecv.at[i], GS + i, (partner(i), c))

    def h_copy(cc):
        return send(gacc.at[steps], grecv.at[steps], GS, (r, cc))

    def each(first_index, last_index, act, skip=None):
        def body(i, carry):
            if skip is None:
                act(i)
            else:
                @pl.when(i != skip)
                def _():
                    act(i)
            return carry

        lax.fori_loop(first_index, last_index, body, 0)

    def store(hi, lo, index, value):
        high, low = split(value)
        hi[index] = high
        lo[index] = low

    def wide(value):
        return jnp.concatenate([value[:nvec], value[nvec:]], 1)

    def start_sends():
        @when(side & (t == 1))
        def _():
            m_near().start()

        @when(far & jnp.logical_not(parted))
        def _():
            m_far().start()

        @when(parted)
        def _():
            for i in range(2):
                m_part(1 - i).start()

        @when(main & (t == 1) & (z == 1))
        def _():
            u_copy(0, 1).start()

        @when(aid)
        def _():
            u_copy(1, 1).start()

    def put_pairs(ref, out):
        for i in range(half):
            for k in range(2):
                ref[i, k] = out[:, (k * half + i) * rows:(k * half + i + 1) * rows]

    def inverse_times(hi, lo, values):
        left = jnp.concatenate([complex_left([v], nvec) for v in values], 1)
        return product(left, hi, lo, dot_nt)

    def factor_times(values, count):
        left = jnp.concatenate(
            [complex_left(values[h * half:(h + 1) * half], nvec) for h in range(per)], 1
        )
        return product(left, fac_hi[:count], fac_lo[:count], dot_nt)

    def first_loads():
        at = pl.ds(0, tile + nvec)
        pltpu.make_async_copy(f_first.at[:, at], f_first.at[:, at], load_sem.at[0]).wait()

    span = 2 * rows
    broad = 2 * width

    @when(main & (t == 0))
    def _():
        first_loads()
        store(low_hi, low_lo, ..., pair(low_in))
        put_pairs(asend, inverse_times(low_hi[...], low_lo[...], [pair(kry_in, 0)]))

    arrive()

    @when(main & (t == 0))
    def _():
        each(0, jnp.where(hub, half - 1, half), lambda i: a_copy(i).start())

    start_sends()

    @when(main & (t == 0))
    def _():
        @when(hub)
        def _():
            arecv[p] = asend[y]
            take(recv_sem.at[AD], (share - 1) * 2 * block)
            parts = [arecv[q] for q in range(share)]
            ybuf[...] = (parts[0] + parts[1]) + (parts[2] + parts[3])
            pl.semaphore_wait(next_sem, 1)
            for i in range(share):
                y_copy(i).start()

        @when(hub)
        def _():
            v_copy(0).start()

        @when(jnp.logical_not(hub))
        def _():
            t_copy().start()
            u_copy(0, 2).start()
            take(recv_sem.at[MS], fac // 2)
            m_relay().start()

    load(3, basis, bas_in).wait()

    def prepare_basis():
        top = pair(bas_in)
        bottom = jnp.concatenate([-bas_in[1], bas_in[0]], 1)
        store(bas_hi, bas_lo, ..., jnp.concatenate([top, bottom], 0))
        return top

    def prepare_end(top):
        gram = jnp.concatenate([top, jnp.concatenate([-top[:, nb:], top[:, :nb]], 1)], 0)
        row_id = lax.broadcasted_iota(jnp.int32, gram.shape, 0)
        col_id = lax.broadcasted_iota(jnp.int32, gram.shape, 1)
        twice = jnp.where(row_id == col_id, 2.0, 0.0) - gram
        spread = product(twice, bas_hi[...], bas_lo[...], dot_nn)
        store(end_hi, end_lo, ..., jnp.concatenate([twice, spread], 1))

    def end_from_side():
        prepare_basis()
        take(recv_sem.at[GS], gram)
        prepare_end(grecv[steps])

    @when(side)
    def _():
        gacc[0] = product(prepare_basis(), bas_hi[...], bas_lo[...], dot_nt)
        for i in range(steps):
            g_copy(i).start()
            take(recv_sem.at[GS + i], gram)
            gacc[i + 1] = gacc[i] + grecv[i]
        each(1, C, lambda cc: h_copy(cc).start())
        prepare_end(gacc[steps])

    @when(c > lead)
    def _():
        end_from_side()

    @when(main & (t == 1))
    def _():
        first_loads()
        load(1, factor, fac_in).wait()
        store(low_hi, low_lo, ..., pair(low_in))
        store(fac_hi, fac_lo, (slice(0, rows), slice(broad, 2 * broad)), pair(fac_in))
        take(recv_sem.at[MS], fac)
        store(fac_hi, fac_lo, (slice(0, rows), slice(0, broad)), pair(f_recv.at[0, 0]))

        @when(hub)
        def _():
            load(2, upper, up_in).wait()
            store(up_hi, up_lo, (slice(0, tile), slice(0, span)), pair(up_in))

        take(recv_sem.at[YE], half * 2 * block)
        g = pair(kry_in, 0) - factor_times([yrecv[q % half, q // half] for q in range(share)], rows)
        put_pairs(dsend, inverse_times(low_hi[...], low_lo[...], [g]))
        each(0, jnp.where(hub, half - 1, half), lambda i: d_copy(i).start())
        o_copy().start()

        @when(hub)
        def _():
            drecv[p] = dsend[y]
            take(recv_sem.at[US], ups)
            store(up_hi, up_lo, (slice(0, tile), slice(span, 2 * span)), pair(up_recv))

            take(recv_sem.at[AD], (share - 1) * 2 * block)
            parts = [drecv[q] for q in range(share)]
            total = (parts[0] + parts[1]) + (parts[2] + parts[3])
            out = inverse_times(up_hi[:tile], up_lo[:tile], [total[0], total[1]])
            for h in range(per):
                for k in range(half):
                    esend[h * half + k] = out[:, (h * half + k) * rows:(h * half + k + 1) * rows]
                for k in range(half):
                    e_copy(h * half + k).start()
            pl.semaphore_wait(all_sem, 1)
            each(0, share * C, lambda i: x_copy(i).start(), p * C + c)
            xrecv[y, :block] = esend[p]

        end_from_side()

    @when(main & (t == 0))
    def _():
        @when(hub)
        def _():
            load(2, upper, up_in).wait()
            store(up_hi, up_lo, (slice(0, tile), slice(span, 2 * span)), pair(up_in))
            gather[p] = bas_in[...]
            take(recv_sem.at[TS], bas)
            v_copy(1).start()
            take(recv_sem.at[VS], 2 * bas)
            stacked = jnp.concatenate(
                [jnp.concatenate([gather[q, i] for q in range(share)], 1) for i in range(2)], 0
            )
            take(recv_sem.at[US], ups)
            store(up_hi, up_lo, (slice(0, tile), slice(0, span)), pair(up_recv))
            for k in range(2):
                at = slice(k * span, (k + 1) * span)
                out = product(stacked, up_hi[:tile, at], up_lo[:tile, at], dot_nn)
                store(up_hi, up_lo, (slice(tile, tile + nb), at), jnp.concatenate(
                    [out[:nb, :rows] + out[nb:, rows:], out[:nb, rows:] - out[nb:, :rows]], 1
                ))
            take(recv_sem.at[OS], 2 * bas)
            empty = jnp.zeros((nb, rows), F32)
            for h in range(per):
                at = slice(h * broad, (h + 1) * broad)
                one = gather_one[h]
                own_re = jnp.where(y == 0, jnp.concatenate([one[0], empty], 1), jnp.concatenate([empty, one[0]], 1))
                own_im = jnp.where(y == 0, jnp.concatenate([one[1], empty], 1), jnp.concatenate([empty, one[1]], 1))
                store(fac_hi, fac_lo, (slice(span, span + nb), at), jnp.concatenate([own_re, -own_im], 1))
            pl.semaphore_wait(all_sem, 1)
            for h in range(per):
                for k in range(2):
                    take(recv_sem.at[MS + k * per + h], fac)
                    store(
                        fac_hi, fac_lo, (slice(k * rows, (k + 1) * rows), slice(h * broad, (h + 1) * broad)),
                        pair(f_recv.at[k, h]),
                    )
            out = 0.0
            for h in range(per):
                take(recv_sem.at[YE + h], half * half * block)
                x = [erecv[0, h * half + k] + erecv[1, h * half + k] for k in range(half)]
                at = slice(h * broad, (h + 1) * broad)
                out = out + product(complex_left(x, nvec), fac_hi[:, at], fac_lo[:, at], dot_nt)
            w = [ybuf[k] - out[:, k * rows:(k + 1) * rows] for k in range(2)]
            more = inverse_times(up_hi[...], up_lo[...], w)
            first = wide(out[:, span:] + more[:, tile:])
            for k in range(share):
                gsend[k, block:] = first
            for h in range(per):
                for k in range(h * half, (h + 1) * half):
                    gsend[k, :block] = more[:, k * rows:(k + 1) * rows]
                each(h * half * C, (h + 1) * half * C, lambda i: z_copy(i).start(), p * C + c)
            each(share * C, R * C, lambda i: f_copy(i).start())
            xrecv[y] = gsend[p]
            end_from_side()

        @when(jnp.logical_not(hub))
        def _():
            end_from_side()

    @when(jnp.logical_not(hub))
    def _():
        take(recv_sem.at[XS], 2 * wave)

    for i in range(2):
        @when(hub & (t == i))
        def _():
            take(recv_sem.at[XS], wave + i * nvec)

    total = xrecv[0] + xrecv[1]
    ends = product(total[block:], end_hi[...], end_lo[...], dot_nn)
    coefficients[0] = ends[:, :nb]
    coefficients[1] = ends[:, nb:2 * nb]
    projected[0] = total[:nvec] - ends[:, 2 * nb:2 * nb + rows]
    projected[1] = total[nvec:block] - ends[:, 2 * nb + rows:]

    def sent(cond, count, way=0):
        @when(cond)
        def _():
            take(send_sem.at[way], count)

    others = share * C - 1
    sent(main & (t == 0) & (z == 0), half * 2 * block + bas + ups + fac // 2)
    sent(hub & (t == 0), (half - 1) * 2 * block + 2 * bas + share * 2 * block)
    sent(hub & (t == 0), others * wave + share * C * nvec, 1)
    sent(main & (t == 1) & (z == 1), half * 2 * block + bas + ups // 2)
    sent(hub & (t == 1), (half - 1) * 2 * block + bas + half * share * block + others * block)
    sent(side & (t == 0), (steps + C - 1) * gram)
    sent(side & (t == 1), (steps + C - 1) * gram + fac)
    sent(far, fac)
    sent(aid, ups // 2)


def hub_call(R, C, factor, lower, upper, krylov, basis):
    tile, rows = lower.shape[1], lower.shape[2]
    width = factor.shape[2]
    nvec, nb = krylov.shape[1], basis.shape[1]
    share, per = tile // rows, tile // width
    half = share // 2
    steps = R.bit_length() - 1
    dma = pltpu.SemaphoreType.DMA
    vmem = pl.BlockSpec(memory_space=pltpu.VMEM)
    block = (2 * nvec, rows)
    f32 = lambda *shape: pltpu.VMEM(shape, F32)
    bf16 = lambda *shape: [pltpu.VMEM(shape, BF16)] * 2
    return pl.pallas_call(
        functools.partial(hub_kernel, R, C),
        out_shape=(pltpu.VMEM(krylov.shape, F32), pltpu.VMEM((2, nvec, nb), F32)),
        in_specs=[pl.BlockSpec(memory_space=pl.ANY)] * 5,
        out_specs=(vmem, vmem),
        scratch_shapes=[
            f32(*factor.shape), f32(2, tile + nvec, rows), f32(*upper.shape), f32(*basis.shape),
            f32(*upper.shape), f32(2, per, *factor.shape),
            *bf16(tile, 2 * rows), *bf16(tile + nb, 4 * rows), *bf16(2 * rows + nb, 2 * tile),
            *bf16(2 * nb, 2 * rows), *bf16(2 * nb, 2 * nb + 2 * rows),
            f32(share, *basis.shape), f32(2, *basis.shape),
            f32(half, 2, *block), f32(share, 2, *block), f32(2, *block), f32(half, 2, *block),
            f32(half, 2, *block), f32(share, 2, *block), f32(share, *block), f32(2, share, *block),
            f32(share, 3 * nvec, rows), f32(half, 3 * nvec, rows),
            f32(steps + 1, nb, 2 * nb), f32(steps + 1, nb, 2 * nb),
            dma((4,)), dma((2,)), dma((8 + steps + 2 * per,)),
            pltpu.SemaphoreType.REGULAR, pltpu.SemaphoreType.REGULAR,
        ],
        compiler_params=pltpu.CompilerParams(collective_id=0, has_side_effects=True),
        name="krylov_hubs",
    )(factor, lower, upper, krylov, basis)


def finish(projected, turned, projected_out, turned_out, sems):
    copies = [
        pltpu.make_async_copy(projected, projected_out, sems.at[0]),
        pltpu.make_async_copy(turned, turned_out, sems.at[1]),
    ]
    for copy in copies:
        copy.start()
    for copy in copies:
        copy.wait()


def general_call(R, C, factor, lower, upper, krylov, basis):
    tile, rows = lower.shape[1], lower.shape[2]
    width = factor.shape[2]
    nvec, nb = krylov.shape[1], basis.shape[1]
    share, per, pieces = tile // rows, tile // width, width // rows
    steps = R.bit_length() - 1
    dma = pltpu.SemaphoreType.DMA
    vmem = pl.BlockSpec(memory_space=pltpu.VMEM)
    block = (2 * nvec, rows)
    return pl.pallas_call(
        functools.partial(kernel, R, C),
        out_shape=(
            jax.ShapeDtypeStruct(krylov.shape, F32),
            jax.ShapeDtypeStruct((2, nvec, nb), F32),
        ),
        in_specs=[vmem] * 5,
        out_specs=(vmem, vmem),
        scratch_shapes=[
            pltpu.VMEM((2, tile, 2 * rows), BF16),
            pltpu.VMEM((2, tile, 2 * rows), BF16),
            pltpu.VMEM((rows, 2 * width), BF16),
            pltpu.VMEM((rows, 2 * width), BF16),
            pltpu.VMEM((2 * nb, 2 * rows), BF16),
            pltpu.VMEM((2 * nb, 2 * rows), BF16),
            pltpu.VMEM((2 * nb, 2 * nb + 2 * rows), BF16),
            pltpu.VMEM((2 * nb, 2 * nb + 2 * rows), BF16),
            pltpu.VMEM((2 * nb, 2 * rows), BF16),
            pltpu.VMEM((2 * nb, 2 * rows), BF16),
            pltpu.VMEM((share, 2, nb, rows), F32),
            pltpu.VMEM((2, share) + block, F32),
            pltpu.VMEM((2, share) + block, F32),
            pltpu.VMEM(block, F32),
            pltpu.VMEM(block, F32),
            pltpu.VMEM((pieces,) + block, F32),
            pltpu.VMEM(block, F32),
            pltpu.VMEM((C,) + block, F32),
            pltpu.VMEM((nvec, 2 * nb), F32),
            pltpu.VMEM((R, nvec, 2 * nb), F32),
            pltpu.VMEM((steps + 1, nb, 2 * nb), F32),
            pltpu.VMEM((steps, nb, 2 * nb), F32),
            dma((2, share)),
            dma((2, share)),
            dma((R,)),
            dma((pieces,)),
            dma((C,)),
            dma((C,)),
            dma((C // per,)),
            dma((1,)),
            dma((R,)),
            dma((R,)),
            dma((steps,)),
            dma((steps,)),
            dma((share,)),
            dma((share,)),
            dma((C // per,)),
            dma((1,)),
            pltpu.SemaphoreType.REGULAR,
        ],
        compiler_params=pltpu.CompilerParams(collective_id=0, has_side_effects=True),
        name="krylov_step",
    )(factor, lower, upper, krylov, basis)


def local(R, C, factor, lower, upper, krylov, basis):
    tile, rows = lower.shape[1], lower.shape[2]
    share, per = tile // rows, tile // factor.shape[2]
    vmem = pl.BlockSpec(memory_space=pltpu.VMEM)
    paired = R == 2 * share and C == 2 * per and share == 4 and per == 2
    call = hub_call if paired else general_call
    projected, turned = call(R, C, factor, lower, upper, krylov, basis)
    if paired:
        projected, turned = [pltpu.with_memory_space_constraint(x, pltpu.VMEM) for x in (projected, turned)]
    projected, turned = pl.pallas_call(
        finish,
        out_shape=(jax.ShapeDtypeStruct(projected.shape, F32), jax.ShapeDtypeStruct(turned.shape, F32)),
        in_specs=[vmem] * 2,
        out_specs=[pl.BlockSpec(memory_space=pl.ANY)] * 2,
        scratch_shapes=[pltpu.SemaphoreType.DMA((2,))],
        name="finish",
    )(projected, turned)
    return projected, turned.transpose(0, 2, 1)


def solution(mesh):
    in_specs = (
        P(None, "row", "col"),
        P(None, None, "row"),
        P(None, None, "row"),
        P(None, None, "row"),
        P(None, None, "row"),
    )
    out_specs = (P(None, None, "row"), P())
    body = functools.partial(local, mesh.shape["row"], mesh.shape["col"])
    return jax.shard_map(body, mesh=mesh, in_specs=in_specs, out_specs=out_specs, check_vma=False)
```

```python
import functools

import jax
import jax.numpy as jnp
from jax import lax
from jax.experimental import pallas as pl
from jax.experimental.pallas import tpu as pltpu
from jax.sharding import PartitionSpec as P

MESH = pl.DeviceIdType.MESH
F32 = jnp.float32
BF16 = jnp.bfloat16


def split(value):
    high = value.astype(BF16)
    low = (value - high.astype(F32)).astype(BF16)
    return high, low


def dot_nt(left, right):
    return lax.dot_general(left, right, (((1,), (1,)), ((), ())), preferred_element_type=F32)


def dot_nn(left, right):
    return lax.dot_general(left, right, (((1,), (0,)), ((), ())), preferred_element_type=F32)


def product(left, high, low, dot):
    rows = left.shape[0]
    left_high, left_low = split(left)
    both = dot(jnp.concatenate([left_high, left_low], 0), high)
    return both[:rows] + (both[rows:] + dot(left_high, low))


def complex_left(pieces, nvec):
    re = [x[:nvec] for x in pieces]
    im = [x[nvec:] for x in pieces]
    top = jnp.concatenate(re + [-x for x in im], 1)
    bottom = jnp.concatenate(im + re, 1)
    return jnp.concatenate([top, bottom], 0)


def kernel(
    R, C, factor, lower, upper, krylov, basis, projected, coefficients,
    inv_hi, inv_lo, fac_hi, fac_lo, bas_hi, bas_lo,
    end_hi, end_lo, lead_hi, lead_lo, gather,
    psend, precv, ybuf, xbuf, bcast, vbuf, vrecv, fsend, frecv, gacc, grecv,
    psend_sem, precv_sem, bsend_sem, brecv_sem, vsend_sem, vrecv_sem, xsend_sem, xrecv_sem,
    fsend_sem, frecv_sem, gsend_sem, grecv_sem, tsend_sem, trecv_sem, ysend_sem, yrecv_sem,
    ready_sem,
):
    tile, rows = lower.shape[1], lower.shape[2]
    width = factor.shape[2]
    nvec = krylov.shape[1]
    nb = basis.shape[1]
    share = tile // rows
    per = tile // width
    pieces = width // rows
    steps = R.bit_length() - 1
    r = lax.axis_index("row")
    c = lax.axis_index("col")
    t, p = r // share, r % share
    j, h = c // per, c % per
    solver = j == t

    barrier = pltpu.get_barrier_semaphore()

    def greet_mate(i, carry):
        pl.semaphore_signal(barrier, inc=1, device_id=(t * share + (p + 1 + i) % share, c), device_id_type=MESH)
        return carry

    def greet_tile(i, carry):
        pl.semaphore_signal(barrier, inc=1, device_id=((r + (1 + i) * share) % R, c), device_id_type=MESH)
        return carry

    def greet_col(i, carry):
        pl.semaphore_signal(barrier, inc=1, device_id=(r, (c + 1 + i) % C), device_id_type=MESH)
        return carry

    lax.fori_loop(0, share - 1, greet_mate, 0)
    lax.fori_loop(0, R // share - 1, greet_tile, 0)
    lax.fori_loop(0, C - 1, greet_col, 0)

    def prepare(ref, slot):
        high, low = split(jnp.concatenate([ref[0], ref[1]], 1))
        inv_hi[slot] = high
        inv_lo[slot] = low

    @pl.when(solver)
    def _():
        prepare(lower, 0)

    @pl.when(jnp.logical_not(solver))
    def _():
        high, low = split(jnp.concatenate([factor[0], factor[1]], 1))
        fac_hi[...] = high
        fac_lo[...] = low

    def prepare_basis():
        top = jnp.concatenate([basis[0], basis[1]], 1)
        bottom = jnp.concatenate([-basis[1], basis[0]], 1)
        high, low = split(jnp.concatenate([top, bottom], 0))
        bas_hi[...] = high
        bas_lo[...] = low
        gacc[0] = product(top, high, low, dot_nt)

    def remote(src, dst, send, recv, dest):
        return pltpu.make_async_remote_copy(
            src_ref=src, dst_ref=dst, send_sem=send, recv_sem=recv, device_id=dest, device_id_type=MESH
        )

    def each(first_index, last_index, act):
        def body(i, carry):
            act(i)
            return carry

        lax.fori_loop(first_index, last_index, body, 0)

    def gram_copy(i):
        other = r + (1 << i) * (1 - 2 * ((r // (1 << i)) % 2))
        return remote(gacc.at[i], grecv.at[i], gsend_sem.at[i], grecv_sem.at[i], (other, c))

    def gram_all():
        for i in range(steps):
            copy = gram_copy(i)
            copy.start()
            copy.wait_recv()
            gacc[i + 1] = gacc[i] + grecv[i]
        top = gacc[steps]
        gram = jnp.concatenate([top, jnp.concatenate([-top[:, nb:], top[:, :nb]], 1)], 0)
        row_id = lax.broadcasted_iota(jnp.int32, gram.shape, 0)
        col_id = lax.broadcasted_iota(jnp.int32, gram.shape, 1)
        twice = jnp.where(row_id == col_id, 2.0, 0.0) - gram
        spread = product(twice, bas_hi[...], bas_lo[...], dot_nn)
        high, low = split(jnp.concatenate([twice, spread], 1))
        end_hi[...] = high
        end_lo[...] = low

    def t_copy(d):
        q = (p + d) % share
        return remote(basis, gather.at[p], tsend_sem.at[d], trecv_sem.at[p], (t * share + q, c))

    def lead_send():
        for d in range(1, share):
            t_copy(d).start()
        gather[p] = basis[...]

    def lead_all():
        for d in range(1, share):
            q = (p + d) % share
            remote(basis, gather.at[q], tsend_sem.at[d], trecv_sem.at[q], (t * share + q, c)).wait_recv()
        left = jnp.concatenate(
            [jnp.concatenate([gather[q, i] for q in range(share)], 1) for i in range(2)], 0
        )
        out = product(left, inv_hi[1], inv_lo[1], dot_nn)
        one = out[:nb, :rows] + out[nb:, rows:]
        two = out[nb:, :rows] - out[:nb, rows:]
        whole = jnp.concatenate([jnp.concatenate([one, two], 1), jnp.concatenate([-two, one], 1)], 0)
        high, low = split(whole)
        lead_hi[...] = high
        lead_lo[...] = low

    def side_work():
        gram_all()

        @pl.when(t == 0)
        def _():
            lead_send()
            lead_all()

    def part_copy(sweep, d):
        q = (p + d) % share
        return remote(
            psend.at[sweep, q], precv.at[sweep, p], psend_sem.at[sweep, q], precv_sem.at[sweep, p], (t * share + q, c)
        )

    def part_arrival(sweep, d):
        q = (p + d) % share
        return remote(
            psend.at[sweep, q], precv.at[sweep, q], psend_sem.at[sweep, q], precv_sem.at[sweep, q], (t * share + q, c)
        ), q

    def v_copy(cc):
        return remote(vbuf, vrecv.at[c], vsend_sem.at[cc], vrecv_sem.at[c], (r, cc))

    def v_each(act):
        @pl.when(t > 0)
        def _():
            for hh in range(per):
                act(v_copy(t * per + hh))

        @pl.when(t == 0)
        def _():
            each(1, C, lambda d: act(v_copy((c + d) % C)))

    def v_sum(first_col, last_col, value):
        def body(cc, total):
            @pl.when(cc != c)
            def _():
                remote(vbuf, vrecv.at[cc], vsend_sem.at[0], vrecv_sem.at[cc], (r, cc)).wait_recv()

            return total - vrecv[cc]

        return lax.fori_loop(first_col, last_col, body, value)

    def f_copy(d):
        return remote(fsend, frecv.at[r], fsend_sem.at[d], frecv_sem.at[r], ((r + d) % R, c))

    def send_first(value, high, low):
        wide_value = jnp.concatenate([value[:nvec], value[nvec:]], 1)
        fsend[...] = product(wide_value, high, low, dot_nt)
        each(1, R, lambda d: f_copy(d).start())

    def multiply(sweep, g):
        out = product(complex_left([g], nvec), inv_hi[sweep], inv_lo[sweep], dot_nt)
        for q in range(share):
            psend[sweep, q] = out[:, q * rows:(q + 1) * rows]

    def solve(sweep, g):
        multiply(sweep, g)
        return exchange(sweep)

    def exchange(sweep):
        for d in range(1, share):
            part_copy(sweep, d).start()
        total = psend[sweep, p]
        for d in range(1, share):
            arrival, q = part_arrival(sweep, d)
            arrival.wait_recv()
            total = total + precv[sweep, q]
        return total

    def b_copy(buf, rr):
        return remote(buf, bcast.at[p % pieces], bsend_sem.at[rr], brecv_sem.at[p % pieces], (rr, c))

    def x_copy(tt):
        cc = tt * per + h
        return remote(xbuf, xbuf, xsend_sem.at[tt], xrecv_sem.at[0], (r, cc))

    def y_copy(tt):
        return remote(ybuf, ybuf, ysend_sem.at[tt], yrecv_sem.at[0], (r, tt * per + h))

    speaks = p // pieces == h

    @pl.when(solver != (t == 0))
    def _():
        prepare(upper, 1)

    @pl.when(j > 0)
    def _():
        prepare_basis()

    @pl.when(jnp.logical_and(solver, t == 0))
    def _():
        multiply(0, jnp.concatenate([krylov[0], krylov[1]], 0))

    pl.semaphore_wait(barrier, share - 1 + R // share - 1 + C - 1)
    for d in range(1, share):
        pl.semaphore_signal(
            ready_sem, inc=1, device_id=(t * share + (p + d) % share, c), device_id_type=MESH
        )

    @pl.when(j > 0)
    def _():
        side_work()

    @pl.when(solver)
    def _():
        @pl.when(t > 0)
        def _():
            b = jnp.concatenate([krylov[0], krylov[1]], 0)
            multiply(0, v_sum(0, t * per, b))

        ybuf[...] = exchange(0)
        pl.semaphore_wait(ready_sem, share - 1)

        @pl.when(speaks)
        def _():
            each((t + 1) * share, R, lambda rr: b_copy(ybuf, rr).start())

        @pl.when(t == 0)
        def _():
            each(1, C // per, lambda tt: y_copy(tt).start())
            prepare(upper, 1)

    @pl.when(jnp.logical_not(solver))
    def _():
        pl.semaphore_wait(ready_sem, share - 1)
        got = []
        for i in range(pieces):
            remote(ybuf, bcast.at[i], bsend_sem.at[0], brecv_sem.at[i], (r, t * per)).wait_recv()
            got.append(bcast[i])
        value = product(complex_left(got, nvec), fac_hi[...], fac_lo[...], dot_nt)
        vbuf[...] = value
        v_each(lambda copy: copy.start())
        vrecv[c] = value

    @pl.when(j == 0)
    def _():
        prepare_basis()
        side_work()

    @pl.when(t == 0)
    def _():
        @pl.when(jnp.logical_not(solver))
        def _():
            remote(ybuf, ybuf, ysend_sem.at[0], yrecv_sem.at[0], (r, h)).wait_recv()

        g = v_sum(per, C, ybuf[...])
        send_first(g, lead_hi[...], lead_lo[...])
        xbuf[...] = solve(1, g)

    @pl.when(t > 0)
    def _():
        @pl.when(solver)
        def _():
            xbuf[...] = solve(1, v_sum((t + 1) * per, C, ybuf[...]))

            @pl.when(speaks)
            def _():
                each(0, t * share, lambda rr: b_copy(xbuf, rr).start())

            each(0, t, lambda tt: x_copy(tt).start())
            each(t + 1, C // per, lambda tt: x_copy(tt).start())

        @pl.when(jnp.logical_not(solver))
        def _():
            remote(ybuf, xbuf, xsend_sem.at[0], xrecv_sem.at[0], (r, t * per)).wait_recv()

        send_first(xbuf[...], bas_hi[...], bas_lo[...])

    frecv[r] = fsend[...]

    def f_wait(d):
        q = (r + d) % R
        remote(fsend, frecv.at[q], fsend_sem.at[d], frecv_sem.at[q], (q, c)).wait_recv()

    each(1, R, f_wait)
    first = frecv[0]
    for i in range(1, R):
        first = first + frecv[i]
    ends = product(first, end_hi[...], end_lo[...], dot_nn)
    coefficients[0] = ends[:, :nb]
    coefficients[1] = ends[:, nb:2 * nb]
    projected[0] = xbuf[:nvec] - ends[:, 2 * nb:2 * nb + rows]
    projected[1] = xbuf[nvec:] - ends[:, 2 * nb + rows:]

    each(1, R, lambda d: f_copy(d).wait_send())
    for i in range(steps):
        gram_copy(i).wait_send()

    def parts_sent(sweep):
        for d in range(1, share):
            part_copy(sweep, d).wait_send()

    @pl.when(t == 0)
    def _():
        parts_sent(1)
        for d in range(1, share):
            t_copy(d).wait_send()

    @pl.when(solver)
    def _():
        parts_sent(0)

        @pl.when(speaks)
        def _():
            each((t + 1) * share, R, lambda rr: b_copy(ybuf, rr).wait_send())

        @pl.when(t == 0)
        def _():
            each(1, C // per, lambda tt: y_copy(tt).wait_send())

        @pl.when(t > 0)
        def _():
            parts_sent(1)

            @pl.when(speaks)
            def _():
                each(0, t * share, lambda rr: b_copy(xbuf, rr).wait_send())

            each(0, t, lambda tt: x_copy(tt).wait_send())
            each(t + 1, C // per, lambda tt: x_copy(tt).wait_send())

    @pl.when(jnp.logical_not(solver))
    def _():
        v_each(lambda copy: copy.wait_send())


def hub_kernel(
    R, C, factor, lower, upper, krylov, basis, projected, coefficients,
    fac_in, f_first, up_in, bas_in, up_recv, f_recv,
    low_hi, low_lo, up_hi, up_lo, fac_hi, fac_lo, turn_hi, turn_lo,
    bas_hi, bas_lo, end_hi, end_lo, gather, gather_one,
    asend, arecv, ybuf, yrecv, dsend, drecv, esend, erecv, gsend, xrecv, gacc, grecv,
    load_sem, send_sem, recv_sem, next_sem, all_sem,
):
    tile, rows = lower.shape[1], lower.shape[2]
    width = factor.shape[2]
    nvec = krylov.shape[1]
    nb = basis.shape[1]
    share = tile // rows
    per = tile // width
    half = share // 2
    steps = R.bit_length() - 1
    r = lax.axis_index("row")
    c = lax.axis_index("col")
    me = r * C + c
    t, p = r // share, r % share
    y, z = p % half, p // half
    lead = per - 1
    main = c == lead
    hub = main & (z == 1 - t)
    side = c == 0

    def partner(i):
        return r + (1 << i) * (1 - 2 * ((r // (1 << i)) % 2))

    def remote(src, dst, send, recv, dest):
        return pltpu.make_async_remote_copy(
            src_ref=src, dst_ref=dst, send_sem=send, recv_sem=recv, device_id=dest, device_id_type=MESH
        )

    low_in, kry_in = f_first.at[:, pl.ds(0, tile)], f_first.at[:, pl.ds(tile, nvec)]

    def load(i, src, dst):
        return pltpu.make_async_copy(src, dst, load_sem.at[i])

    @pl.when(main)
    def _():
        load(0, lower, low_in).start()
        load(0, krylov, kry_in).start()

        @pl.when(t == 1)
        def _():
            load(1, factor, fac_in).start()

        @pl.when(hub)
        def _():
            load(2, upper, up_in).start()

    load(3, basis, bas_in).start()

    barrier = pltpu.get_barrier_semaphore()
    guide = (c == per) & (t == 1) & (z == 0)
    far = (c >= per) & (t == 0)
    parted = far & (z == 0) & (c == per)
    aid = (c == C - 1) & (t == 1) & (z == 1)

    def greet(rr, cc):
        pl.semaphore_signal(barrier, inc=1, device_id=(rr, cc), device_id_type=MESH)

    @pl.when(main)
    def _():
        @pl.when(hub)
        def _():
            for d in range(1, share):
                greet(t * share + (p + d) % share, c)

        greet(r, 0)

        @pl.when(t == 1)
        def _():
            for i in range(half):
                greet(half + i, 0)

        @pl.when(hub & (t == 0))
        def _():
            for cc in range(per, C):
                greet(r, cc)
                greet(y, cc)

        @pl.when(hub & (t == 1))
        def _():
            greet(share + half + y, C - 1)

        @pl.when((t == 0) & (z == 0))
        def _():
            greet(r, per)

    @pl.when(side)
    def _():
        for i in range(steps):
            greet(partner(i), c)

    @pl.when(c >= per)
    def _():
        greet(r, 0)

    for i in range(half):
        @pl.when(jnp.logical_not(guide & (y == i)))
        def _():
            greet(share + i, per)

    def arrive():
        count = jnp.where(main, jnp.where(hub, half - 1, half), jnp.where(
            side, steps + 1 + C - per + jnp.where((t == 0) & (z == 1), share, 0),
            jnp.where(guide, R * C - 1, jnp.where(parted, 2, 1)),
        ))
        @pl.when(main | side | far | guide | aid)
        def _():
            pl.semaphore_wait(barrier, count)

        @pl.when(side & (t == 0) & (z == 1))
        def _():
            pl.semaphore_signal(next_sem, inc=1, device_id=(r, lead), device_id_type=MESH)

        @pl.when(guide)
        def _():
            for i in range(2):
                pl.semaphore_signal(all_sem, inc=1, device_id=(half * (i + 1) + y, lead), device_id_type=MESH)

    def when(cond):
        return pl.when(cond)

    def pair(ref, axis=1):
        return jnp.concatenate([ref[0], ref[1]], axis)

    block, wave, bas, fac, ups, gram = 2 * nvec, 3 * nvec, 2 * nb, 2 * width, 2 * tile, 2 * nb * nb // rows
    AD, US, XS, YE, ES, TS, VS, OS, GS = range(9)
    MS = GS + steps

    def take(sem, count):
        if count > ups:
            ref = f_recv.at[:, :, :, pl.ds(0, count * rows // (4 * per * width))]
        else:
            ref = up_recv.at[:, pl.ds(0, count // 2)]
        remote(ref, ref, send_sem.at[0], sem, ((r + 1) % R, c)).wait_recv()

    def send(src, dst, recv, dest, way=0):
        return remote(src, dst, send_sem.at[way], recv_sem.at[recv], dest)

    def a_copy(i):
        i = (y + 1 + i) % half
        return send(asend.at[i], arecv.at[p], AD, (half + i, c))

    def y_copy(i):
        i = (1 - i // half) * half + (y + 1 + i) % half
        return send(ybuf, yrecv.at[y], YE, (share + i, c))

    def u_copy(first, count):
        at = pl.ds(first * (tile // 2), count * (tile // 2))
        return send(upper.at[:, at], up_recv.at[:, at], US, (t * share + (1 - z) * half + y, lead))

    def m_near():
        return send(factor, f_recv.at[0, 0], MS, (r, lead))

    def m_far():
        return send(factor, f_recv.at[z, c % per], MS + z * per + c % per, (half + y, lead))

    def m_part(i):
        return send(factor.at[i], f_recv.at[0, 0, i], MS, (half * (1 - i) + y, lead))

    def m_relay():
        return send(f_recv.at[0, 0, 1], f_recv.at[0, 0, 1], MS, (half + y, lead))

    def t_copy():
        return send(basis, gather.at[p], TS, (half + y, lead))

    def v_copy(i):
        if i == 0:
            return send(basis, gather.at[p], VS, (half + (y + 1) % half, lead))
        return send(gather.at[y], gather.at[y], VS, (half + (y + 1) % half, lead))

    def o_copy():
        return send(basis, gather_one.at[z], OS, (half + y, lead))

    def d_copy(i):
        i = (y + 1 + i) % half
        return send(dsend.at[i], drecv.at[p], AD, (share + i, c))

    def e_copy(i):
        h, k = i // half, (y + 1 + i) % half
        at = pl.ds(h * half, half)
        return send(esend.at[at], erecv.at[y, at], YE + h, (half + k, c))

    def x_copy(i):
        k, cc = i // C, i % C
        return send(esend.at[k], xrecv.at[y, pl.ds(0, block)], XS, (t * share + k, cc))

    def f_copy(i):
        at = pl.ds(block, nvec)
        return send(gsend.at[0, at], xrecv.at[y, at], XS, (i // C, i % C), 1)

    def z_copy(i):
        k, cc = i // C, i % C
        return send(gsend.at[k], xrecv.at[y], XS, (k, cc), 1)

    def g_copy(i):
        return send(gacc.at[i], grecv.at[i], GS + i, (partner(i), c))

    def h_copy(cc):
        return send(gacc.at[steps], grecv.at[steps], GS, (r, cc))

    def each(first_index, last_index, act, skip=None):
        def body(i, carry):
            if skip is None:
                act(i)
            else:
                @pl.when(i != skip)
                def _():
                    act(i)
            return carry

        lax.fori_loop(first_index, last_index, body, 0)

    def store(hi, lo, index, value):
        high, low = split(value)
        hi[index] = high
        lo[index] = low

    def wide(value):
        return jnp.concatenate([value[:nvec], value[nvec:]], 1)

    def start_sends():
        @when(side & (t == 1))
        def _():
            m_near().start()

        @when(far & jnp.logical_not(parted))
        def _():
            m_far().start()

        @when(parted)
        def _():
            for i in range(2):
                m_part(1 - i).start()

        @when(main & (t == 1) & (z == 1))
        def _():
            u_copy(0, 1).start()

        @when(aid)
        def _():
            u_copy(1, 1).start()

    def put_pairs(ref, out):
        for i in range(half):
            for k in range(2):
                ref[i, k] = out[:, (k * half + i) * rows:(k * half + i + 1) * rows]

    def times(values, high, low):
        left = jnp.concatenate([complex_left(v, nvec) for v in values], 1)
        return product(left, high, low, dot_nn)

    def turn(hi, lo, row, col, value):
        high, low = split(value.T)
        at = (slice(row, row + value.shape[1]), slice(col, col + value.shape[0]))
        hi[at] = high
        lo[at] = low

    def turn_pair(hi, lo, row, col, ref):
        for i in range(2):
            turn(hi, lo, row + i * ref.shape[2], col, ref[i])

    def first_loads():
        at = pl.ds(0, tile + nvec)
        pltpu.make_async_copy(f_first.at[:, at], f_first.at[:, at], load_sem.at[0]).wait()

    span = 2 * rows
    broad = 2 * width

    @when(main & (t == 0))
    def _():
        first_loads()
        store(low_hi, low_lo, ..., pair(low_in))
        left = complex_left([pair(kry_in, 0)], nvec)
        put_pairs(asend, product(left, low_hi[...], low_lo[...], dot_nt))

    arrive()

    @when(main & (t == 0))
    def _():
        each(0, jnp.where(hub, half - 1, half), lambda i: a_copy(i).start())

    start_sends()

    @when(main & (t == 0))
    def _():
        @when(hub)
        def _():
            arecv[p] = asend[y]
            take(recv_sem.at[AD], (share - 1) * 2 * block)
            parts = [arecv[q] for q in range(share)]
            ybuf[...] = (parts[0] + parts[1]) + (parts[2] + parts[3])
            pl.semaphore_wait(next_sem, 1)
            for i in range(share):
                y_copy(i).start()

        @when(hub)
        def _():
            v_copy(0).start()

        @when(jnp.logical_not(hub))
        def _():
            t_copy().start()
            u_copy(0, 2).start()
            take(recv_sem.at[MS], fac // 2)
            m_relay().start()

    load(3, basis, bas_in).wait()

    def prepare_basis():
        top = pair(bas_in)
        bottom = jnp.concatenate([-bas_in[1], bas_in[0]], 1)
        store(bas_hi, bas_lo, ..., jnp.concatenate([top, bottom], 0))
        return top

    def prepare_end(top):
        gram = jnp.concatenate([top, jnp.concatenate([-top[:, nb:], top[:, :nb]], 1)], 0)
        row_id = lax.broadcasted_iota(jnp.int32, gram.shape, 0)
        col_id = lax.broadcasted_iota(jnp.int32, gram.shape, 1)
        twice = jnp.where(row_id == col_id, 2.0, 0.0) - gram
        spread = product(twice, bas_hi[...], bas_lo[...], dot_nn)
        store(end_hi, end_lo, ..., jnp.concatenate([twice, spread], 1))

    def end_from_side():
        prepare_basis()
        take(recv_sem.at[GS], gram)
        prepare_end(grecv[steps])

    @when(side)
    def _():
        gacc[0] = product(prepare_basis(), bas_hi[...], bas_lo[...], dot_nt)
        for i in range(steps):
            g_copy(i).start()
            take(recv_sem.at[GS + i], gram)
            gacc[i + 1] = gacc[i] + grecv[i]
        each(1, C, lambda cc: h_copy(cc).start())
        prepare_end(gacc[steps])

    @when(c > lead)
    def _():
        end_from_side()

    @when(main & (t == 1))
    def _():
        first_loads()
        load(1, factor, fac_in).wait()
        turn_pair(turn_hi, turn_lo, 0, 0, low_in)
        turn_pair(fac_hi, fac_lo, broad, 0, fac_in)
        take(recv_sem.at[MS], fac)
        turn_pair(fac_hi, fac_lo, 0, 0, f_recv.at[0, 0])

        @when(hub)
        def _():
            load(2, upper, up_in).wait()
            turn_pair(up_hi, up_lo, 0, 0, up_in)

        take(recv_sem.at[YE], half * 2 * block)
        parts = [[yrecv[i, h] for i in range(half)] for h in range(per)]
        g = pair(kry_in, 0) - times(parts, fac_hi[:, :rows], fac_lo[:, :rows])
        ybuf[0] = g

        @when(main)
        def _():
            put_pairs(dsend, times([[ybuf[0]]], turn_hi[...], turn_lo[...]))

        each(0, jnp.where(hub, half - 1, half), lambda i: d_copy(i).start())
        o_copy().start()

        @when(hub)
        def _():
            drecv[p] = dsend[y]
            take(recv_sem.at[US], ups)
            turn_pair(up_hi, up_lo, span, 0, up_recv)

            take(recv_sem.at[AD], (share - 1) * 2 * block)
            parts = [drecv[q] for q in range(share)]
            total = (parts[0] + parts[1]) + (parts[2] + parts[3])
            out = times([[total[0]], [total[1]]], up_hi[:, :tile], up_lo[:, :tile])
            for h in range(per):
                for k in range(half):
                    esend[h * half + k] = out[:, (h * half + k) * rows:(h * half + k + 1) * rows]
                for k in range(half):
                    e_copy(h * half + k).start()
            pl.semaphore_wait(all_sem, 1)
            each(0, share * C, lambda i: x_copy(i).start(), p * C + c)
            xrecv[y, :block] = esend[p]

        end_from_side()

    @when(main & (t == 0))
    def _():
        @when(hub)
        def _():
            load(2, upper, up_in).wait()
            turn_pair(up_hi, up_lo, span, 0, up_in)
            gather[p] = bas_in[...]
            take(recv_sem.at[TS], bas)
            v_copy(1).start()
            take(recv_sem.at[VS], 2 * bas)
            stacked = jnp.concatenate(
                [jnp.concatenate([gather[q, i] for q in range(share)], 1) for i in range(2)], 0
            )
            take(recv_sem.at[US], ups)
            turn_pair(up_hi, up_lo, 0, 0, up_recv)
            for k in range(2):
                at = slice(k * span, (k + 1) * span)
                out = product(stacked, up_hi[at, :tile], up_lo[at, :tile], dot_nt)
                turn(up_hi, up_lo, k * span, tile, out[:nb, :rows] + out[nb:, rows:])
                turn(up_hi, up_lo, k * span + rows, tile, out[:nb, rows:] - out[nb:, :rows])
            take(recv_sem.at[OS], 2 * bas)
            empty = jnp.zeros((nb, rows), F32)
            for h in range(per):
                one = gather_one[h]
                for i in range(2):
                    own = (1 - 2 * i) * one[i]
                    own = jnp.where(y == 0, jnp.concatenate([own, empty], 1), jnp.concatenate([empty, own], 1))
                    turn(fac_hi, fac_lo, h * broad + i * width, span, own)
            pl.semaphore_wait(all_sem, 1)
            for h in range(per):
                for k in range(2):
                    take(recv_sem.at[MS + k * per + h], fac)
                    turn_pair(fac_hi, fac_lo, h * broad, k * rows, f_recv.at[k, h])
            out = 0.0
            for h in range(per):
                take(recv_sem.at[YE + h], half * half * block)
                x = [erecv[0, h * half + k] + erecv[1, h * half + k] for k in range(half)]
                at = slice(h * broad, (h + 1) * broad)
                out = out + times([x], fac_hi[at], fac_lo[at])
            for k in range(2):
                yrecv[0, k] = ybuf[k] - out[:, k * rows:(k + 1) * rows]
            gsend[0, :, :nb] = jnp.concatenate([out[:, span:], out[:nvec, span:]], 0)

            @when(main)
            def _():
                more = times([[yrecv[0, 0]], [yrecv[0, 1]]], up_hi[...], up_lo[...])
                first = wide(gsend[0, :block, :nb] + more[:, tile:])
                for k in range(share):
                    gsend[k, block:] = first
                    gsend[k, :block] = more[:, k * rows:(k + 1) * rows]
                    for cc in range(C):
                        if k < half or cc != lead:
                            z_copy(k * C + cc).start()
                        else:
                            @when(p != k)
                            def _():
                                z_copy(k * C + cc).start()

            each(share * C, R * C, lambda i: f_copy(i).start())
            xrecv[y] = gsend[p]
            end_from_side()

        @when(jnp.logical_not(hub))
        def _():
            end_from_side()

    @when(jnp.logical_not(hub))
    def _():
        take(recv_sem.at[XS], 2 * wave)

    for i in range(2):
        @when(hub & (t == i))
        def _():
            take(recv_sem.at[XS], wave + i * nvec)

    total = xrecv[0] + xrecv[1]
    ends = product(total[block:], end_hi[...], end_lo[...], dot_nn)
    coefficients[0] = ends[:, :nb]
    coefficients[1] = ends[:, nb:2 * nb]
    projected[0] = total[:nvec] - ends[:, 2 * nb:2 * nb + rows]
    projected[1] = total[nvec:block] - ends[:, 2 * nb + rows:]

    def sent(cond, count, way=0):
        @when(cond)
        def _():
            take(send_sem.at[way], count)

    others = share * C - 1
    sent(main & (t == 0) & (z == 0), half * 2 * block + bas + ups + fac // 2)
    sent(hub & (t == 0), (half - 1) * 2 * block + 2 * bas + share * 2 * block)
    sent(hub & (t == 0), others * wave + share * C * nvec, 1)
    sent(main & (t == 1) & (z == 1), half * 2 * block + bas + ups // 2)
    sent(hub & (t == 1), (half - 1) * 2 * block + bas + half * share * block + others * block)
    sent(side & (t == 0), (steps + C - 1) * gram)
    sent(side & (t == 1), (steps + C - 1) * gram + fac)
    sent(far, fac)
    sent(aid, ups // 2)


def hub_call(R, C, factor, lower, upper, krylov, basis):
    tile, rows = lower.shape[1], lower.shape[2]
    width = factor.shape[2]
    nvec, nb = krylov.shape[1], basis.shape[1]
    share, per = tile // rows, tile // width
    half = share // 2
    steps = R.bit_length() - 1
    dma = pltpu.SemaphoreType.DMA
    vmem = pl.BlockSpec(memory_space=pltpu.VMEM)
    block = (2 * nvec, rows)
    f32 = lambda *shape: pltpu.VMEM(shape, F32)
    bf16 = lambda *shape: [pltpu.VMEM(shape, BF16)] * 2
    return pl.pallas_call(
        functools.partial(hub_kernel, R, C),
        out_shape=(pltpu.VMEM(krylov.shape, F32), pltpu.VMEM((2, nvec, nb), F32)),
        in_specs=[pl.BlockSpec(memory_space=pl.ANY)] * 5,
        out_specs=(vmem, vmem),
        scratch_shapes=[
            f32(*factor.shape), f32(2, tile + nvec, rows), f32(*upper.shape), f32(*basis.shape),
            f32(*upper.shape), f32(2, per, *factor.shape),
            *bf16(tile, 2 * rows), *bf16(4 * rows, tile + nb), *bf16(2 * tile, 2 * rows + nb), *bf16(2 * rows, tile),
            *bf16(2 * nb, 2 * rows), *bf16(2 * nb, 2 * nb + 2 * rows),
            f32(share, *basis.shape), f32(2, *basis.shape),
            f32(half, 2, *block), f32(share, 2, *block), f32(2, *block), f32(half, 2, *block),
            f32(half, 2, *block), f32(share, 2, *block), f32(share, *block), f32(2, share, *block),
            f32(share, 3 * nvec, rows), f32(half, 3 * nvec, rows),
            f32(steps + 1, nb, 2 * nb), f32(steps + 1, nb, 2 * nb),
            dma((4,)), dma((2,)), dma((8 + steps + 2 * per,)),
            pltpu.SemaphoreType.REGULAR, pltpu.SemaphoreType.REGULAR,
        ],
        compiler_params=pltpu.CompilerParams(collective_id=0, has_side_effects=True),
        name="krylov_hubs",
    )(factor, lower, upper, krylov, basis)


def finish(projected, turned, projected_out, turned_out, sems):
    copies = [
        pltpu.make_async_copy(projected, projected_out, sems.at[0]),
        pltpu.make_async_copy(turned, turned_out, sems.at[1]),
    ]
    for copy in copies:
        copy.start()
    for copy in copies:
        copy.wait()


def general_call(R, C, factor, lower, upper, krylov, basis):
    tile, rows = lower.shape[1], lower.shape[2]
    width = factor.shape[2]
    nvec, nb = krylov.shape[1], basis.shape[1]
    share, per, pieces = tile // rows, tile // width, width // rows
    steps = R.bit_length() - 1
    dma = pltpu.SemaphoreType.DMA
    vmem = pl.BlockSpec(memory_space=pltpu.VMEM)
    block = (2 * nvec, rows)
    return pl.pallas_call(
        functools.partial(kernel, R, C),
        out_shape=(
            jax.ShapeDtypeStruct(krylov.shape, F32),
            jax.ShapeDtypeStruct((2, nvec, nb), F32),
        ),
        in_specs=[vmem] * 5,
        out_specs=(vmem, vmem),
        scratch_shapes=[
            pltpu.VMEM((2, tile, 2 * rows), BF16),
            pltpu.VMEM((2, tile, 2 * rows), BF16),
            pltpu.VMEM((rows, 2 * width), BF16),
            pltpu.VMEM((rows, 2 * width), BF16),
            pltpu.VMEM((2 * nb, 2 * rows), BF16),
            pltpu.VMEM((2 * nb, 2 * rows), BF16),
            pltpu.VMEM((2 * nb, 2 * nb + 2 * rows), BF16),
            pltpu.VMEM((2 * nb, 2 * nb + 2 * rows), BF16),
            pltpu.VMEM((2 * nb, 2 * rows), BF16),
            pltpu.VMEM((2 * nb, 2 * rows), BF16),
            pltpu.VMEM((share, 2, nb, rows), F32),
            pltpu.VMEM((2, share) + block, F32),
            pltpu.VMEM((2, share) + block, F32),
            pltpu.VMEM(block, F32),
            pltpu.VMEM(block, F32),
            pltpu.VMEM((pieces,) + block, F32),
            pltpu.VMEM(block, F32),
            pltpu.VMEM((C,) + block, F32),
            pltpu.VMEM((nvec, 2 * nb), F32),
            pltpu.VMEM((R, nvec, 2 * nb), F32),
            pltpu.VMEM((steps + 1, nb, 2 * nb), F32),
            pltpu.VMEM((steps, nb, 2 * nb), F32),
            dma((2, share)),
            dma((2, share)),
            dma((R,)),
            dma((pieces,)),
            dma((C,)),
            dma((C,)),
            dma((C // per,)),
            dma((1,)),
            dma((R,)),
            dma((R,)),
            dma((steps,)),
            dma((steps,)),
            dma((share,)),
            dma((share,)),
            dma((C // per,)),
            dma((1,)),
            pltpu.SemaphoreType.REGULAR,
        ],
        compiler_params=pltpu.CompilerParams(collective_id=0, has_side_effects=True),
        name="krylov_step",
    )(factor, lower, upper, krylov, basis)


def local(R, C, factor, lower, upper, krylov, basis):
    tile, rows = lower.shape[1], lower.shape[2]
    share, per = tile // rows, tile // factor.shape[2]
    vmem = pl.BlockSpec(memory_space=pltpu.VMEM)
    paired = R == 2 * share and C == 2 * per and share == 4 and per == 2
    call = hub_call if paired else general_call
    projected, turned = call(R, C, factor, lower, upper, krylov, basis)
    if paired:
        projected, turned = [pltpu.with_memory_space_constraint(x, pltpu.VMEM) for x in (projected, turned)]
    projected, turned = pl.pallas_call(
        finish,
        out_shape=(jax.ShapeDtypeStruct(projected.shape, F32), jax.ShapeDtypeStruct(turned.shape, F32)),
        in_specs=[vmem] * 2,
        out_specs=[pl.BlockSpec(memory_space=pl.ANY)] * 2,
        scratch_shapes=[pltpu.SemaphoreType.DMA((2,))],
        name="finish",
    )(projected, turned)
    return projected, turned.transpose(0, 2, 1)


def solution(mesh):
    in_specs = (
        P(None, "row", "col"),
        P(None, None, "row"),
        P(None, None, "row"),
        P(None, None, "row"),
        P(None, None, "row"),
    )
    out_specs = (P(None, None, "row"), P())
    body = functools.partial(local, mesh.shape["row"], mesh.shape["col"])
    return jax.shard_map(body, mesh=mesh, in_specs=in_specs, out_specs=out_specs, check_vma=False)
```

```python
import functools

import jax
import jax.numpy as jnp
from jax import lax
from jax.experimental import pallas as pl
from jax.experimental.pallas import tpu as pltpu
from jax.sharding import PartitionSpec as P

MESH = pl.DeviceIdType.MESH
F32 = jnp.float32
BF16 = jnp.bfloat16


def split(value):
    high = value.astype(BF16)
    low = (value - high.astype(F32)).astype(BF16)
    return high, low


def dot_nt(left, right):
    return lax.dot_general(left, right, (((1,), (1,)), ((), ())), preferred_element_type=F32)


def dot_nn(left, right):
    return lax.dot_general(left, right, (((1,), (0,)), ((), ())), preferred_element_type=F32)


def product(left, high, low, dot):
    rows = left.shape[0]
    left_high, left_low = split(left)
    both = dot(jnp.concatenate([left_high, left_low], 0), high)
    return both[:rows] + (both[rows:] + dot(left_high, low))


def complex_left(pieces, nvec):
    re = [x[:nvec] for x in pieces]
    im = [x[nvec:] for x in pieces]
    top = jnp.concatenate(re + [-x for x in im], 1)
    bottom = jnp.concatenate(im + re, 1)
    return jnp.concatenate([top, bottom], 0)


def kernel(
    R, C, factor, lower, upper, krylov, basis, projected, coefficients,
    inv_hi, inv_lo, fac_hi, fac_lo, bas_hi, bas_lo,
    end_hi, end_lo, lead_hi, lead_lo, gather,
    psend, precv, ybuf, xbuf, bcast, vbuf, vrecv, fsend, frecv, gacc, grecv,
    psend_sem, precv_sem, bsend_sem, brecv_sem, vsend_sem, vrecv_sem, xsend_sem, xrecv_sem,
    fsend_sem, frecv_sem, gsend_sem, grecv_sem, tsend_sem, trecv_sem, ysend_sem, yrecv_sem,
    ready_sem,
):
    tile, rows = lower.shape[1], lower.shape[2]
    width = factor.shape[2]
    nvec = krylov.shape[1]
    nb = basis.shape[1]
    share = tile // rows
    per = tile // width
    pieces = width // rows
    steps = R.bit_length() - 1
    r = lax.axis_index("row")
    c = lax.axis_index("col")
    t, p = r // share, r % share
    j, h = c // per, c % per
    solver = j == t

    barrier = pltpu.get_barrier_semaphore()

    def greet_mate(i, carry):
        pl.semaphore_signal(barrier, inc=1, device_id=(t * share + (p + 1 + i) % share, c), device_id_type=MESH)
        return carry

    def greet_tile(i, carry):
        pl.semaphore_signal(barrier, inc=1, device_id=((r + (1 + i) * share) % R, c), device_id_type=MESH)
        return carry

    def greet_col(i, carry):
        pl.semaphore_signal(barrier, inc=1, device_id=(r, (c + 1 + i) % C), device_id_type=MESH)
        return carry

    lax.fori_loop(0, share - 1, greet_mate, 0)
    lax.fori_loop(0, R // share - 1, greet_tile, 0)
    lax.fori_loop(0, C - 1, greet_col, 0)

    def prepare(ref, slot):
        high, low = split(jnp.concatenate([ref[0], ref[1]], 1))
        inv_hi[slot] = high
        inv_lo[slot] = low

    @pl.when(solver)
    def _():
        prepare(lower, 0)

    @pl.when(jnp.logical_not(solver))
    def _():
        high, low = split(jnp.concatenate([factor[0], factor[1]], 1))
        fac_hi[...] = high
        fac_lo[...] = low

    def prepare_basis():
        top = jnp.concatenate([basis[0], basis[1]], 1)
        bottom = jnp.concatenate([-basis[1], basis[0]], 1)
        high, low = split(jnp.concatenate([top, bottom], 0))
        bas_hi[...] = high
        bas_lo[...] = low
        gacc[0] = product(top, high, low, dot_nt)

    def remote(src, dst, send, recv, dest):
        return pltpu.make_async_remote_copy(
            src_ref=src, dst_ref=dst, send_sem=send, recv_sem=recv, device_id=dest, device_id_type=MESH
        )

    def each(first_index, last_index, act):
        def body(i, carry):
            act(i)
            return carry

        lax.fori_loop(first_index, last_index, body, 0)

    def gram_copy(i):
        other = r + (1 << i) * (1 - 2 * ((r // (1 << i)) % 2))
        return remote(gacc.at[i], grecv.at[i], gsend_sem.at[i], grecv_sem.at[i], (other, c))

    def gram_all():
        for i in range(steps):
            copy = gram_copy(i)
            copy.start()
            copy.wait_recv()
            gacc[i + 1] = gacc[i] + grecv[i]
        top = gacc[steps]
        gram = jnp.concatenate([top, jnp.concatenate([-top[:, nb:], top[:, :nb]], 1)], 0)
        row_id = lax.broadcasted_iota(jnp.int32, gram.shape, 0)
        col_id = lax.broadcasted_iota(jnp.int32, gram.shape, 1)
        twice = jnp.where(row_id == col_id, 2.0, 0.0) - gram
        spread = product(twice, bas_hi[...], bas_lo[...], dot_nn)
        high, low = split(jnp.concatenate([twice, spread], 1))
        end_hi[...] = high
        end_lo[...] = low

    def t_copy(d):
        q = (p + d) % share
        return remote(basis, gather.at[p], tsend_sem.at[d], trecv_sem.at[p], (t * share + q, c))

    def lead_send():
        for d in range(1, share):
            t_copy(d).start()
        gather[p] = basis[...]

    def lead_all():
        for d in range(1, share):
            q = (p + d) % share
            remote(basis, gather.at[q], tsend_sem.at[d], trecv_sem.at[q], (t * share + q, c)).wait_recv()
        left = jnp.concatenate(
            [jnp.concatenate([gather[q, i] for q in range(share)], 1) for i in range(2)], 0
        )
        out = product(left, inv_hi[1], inv_lo[1], dot_nn)
        one = out[:nb, :rows] + out[nb:, rows:]
        two = out[nb:, :rows] - out[:nb, rows:]
        whole = jnp.concatenate([jnp.concatenate([one, two], 1), jnp.concatenate([-two, one], 1)], 0)
        high, low = split(whole)
        lead_hi[...] = high
        lead_lo[...] = low

    def side_work():
        gram_all()

        @pl.when(t == 0)
        def _():
            lead_send()
            lead_all()

    def part_copy(sweep, d):
        q = (p + d) % share
        return remote(
            psend.at[sweep, q], precv.at[sweep, p], psend_sem.at[sweep, q], precv_sem.at[sweep, p], (t * share + q, c)
        )

    def part_arrival(sweep, d):
        q = (p + d) % share
        return remote(
            psend.at[sweep, q], precv.at[sweep, q], psend_sem.at[sweep, q], precv_sem.at[sweep, q], (t * share + q, c)
        ), q

    def v_copy(cc):
        return remote(vbuf, vrecv.at[c], vsend_sem.at[cc], vrecv_sem.at[c], (r, cc))

    def v_each(act):
        @pl.when(t > 0)
        def _():
            for hh in range(per):
                act(v_copy(t * per + hh))

        @pl.when(t == 0)
        def _():
            each(1, C, lambda d: act(v_copy((c + d) % C)))

    def v_sum(first_col, last_col, value):
        def body(cc, total):
            @pl.when(cc != c)
            def _():
                remote(vbuf, vrecv.at[cc], vsend_sem.at[0], vrecv_sem.at[cc], (r, cc)).wait_recv()

            return total - vrecv[cc]

        return lax.fori_loop(first_col, last_col, body, value)

    def f_copy(d):
        return remote(fsend, frecv.at[r], fsend_sem.at[d], frecv_sem.at[r], ((r + d) % R, c))

    def send_first(value, high, low):
        wide_value = jnp.concatenate([value[:nvec], value[nvec:]], 1)
        fsend[...] = product(wide_value, high, low, dot_nt)
        each(1, R, lambda d: f_copy(d).start())

    def multiply(sweep, g):
        out = product(complex_left([g], nvec), inv_hi[sweep], inv_lo[sweep], dot_nt)
        for q in range(share):
            psend[sweep, q] = out[:, q * rows:(q + 1) * rows]

    def solve(sweep, g):
        multiply(sweep, g)
        return exchange(sweep)

    def exchange(sweep):
        for d in range(1, share):
            part_copy(sweep, d).start()
        total = psend[sweep, p]
        for d in range(1, share):
            arrival, q = part_arrival(sweep, d)
            arrival.wait_recv()
            total = total + precv[sweep, q]
        return total

    def b_copy(buf, rr):
        return remote(buf, bcast.at[p % pieces], bsend_sem.at[rr], brecv_sem.at[p % pieces], (rr, c))

    def x_copy(tt):
        cc = tt * per + h
        return remote(xbuf, xbuf, xsend_sem.at[tt], xrecv_sem.at[0], (r, cc))

    def y_copy(tt):
        return remote(ybuf, ybuf, ysend_sem.at[tt], yrecv_sem.at[0], (r, tt * per + h))

    speaks = p // pieces == h

    @pl.when(solver != (t == 0))
    def _():
        prepare(upper, 1)

    @pl.when(j > 0)
    def _():
        prepare_basis()

    @pl.when(jnp.logical_and(solver, t == 0))
    def _():
        multiply(0, jnp.concatenate([krylov[0], krylov[1]], 0))

    pl.semaphore_wait(barrier, share - 1 + R // share - 1 + C - 1)
    for d in range(1, share):
        pl.semaphore_signal(
            ready_sem, inc=1, device_id=(t * share + (p + d) % share, c), device_id_type=MESH
        )

    @pl.when(j > 0)
    def _():
        side_work()

    @pl.when(solver)
    def _():
        @pl.when(t > 0)
        def _():
            b = jnp.concatenate([krylov[0], krylov[1]], 0)
            multiply(0, v_sum(0, t * per, b))

        ybuf[...] = exchange(0)
        pl.semaphore_wait(ready_sem, share - 1)

        @pl.when(speaks)
        def _():
            each((t + 1) * share, R, lambda rr: b_copy(ybuf, rr).start())

        @pl.when(t == 0)
        def _():
            each(1, C // per, lambda tt: y_copy(tt).start())
            prepare(upper, 1)

    @pl.when(jnp.logical_not(solver))
    def _():
        pl.semaphore_wait(ready_sem, share - 1)
        got = []
        for i in range(pieces):
            remote(ybuf, bcast.at[i], bsend_sem.at[0], brecv_sem.at[i], (r, t * per)).wait_recv()
            got.append(bcast[i])
        value = product(complex_left(got, nvec), fac_hi[...], fac_lo[...], dot_nt)
        vbuf[...] = value
        v_each(lambda copy: copy.start())
        vrecv[c] = value

    @pl.when(j == 0)
    def _():
        prepare_basis()
        side_work()

    @pl.when(t == 0)
    def _():
        @pl.when(jnp.logical_not(solver))
        def _():
            remote(ybuf, ybuf, ysend_sem.at[0], yrecv_sem.at[0], (r, h)).wait_recv()

        g = v_sum(per, C, ybuf[...])
        send_first(g, lead_hi[...], lead_lo[...])
        xbuf[...] = solve(1, g)

    @pl.when(t > 0)
    def _():
        @pl.when(solver)
        def _():
            xbuf[...] = solve(1, v_sum((t + 1) * per, C, ybuf[...]))

            @pl.when(speaks)
            def _():
                each(0, t * share, lambda rr: b_copy(xbuf, rr).start())

            each(0, t, lambda tt: x_copy(tt).start())
            each(t + 1, C // per, lambda tt: x_copy(tt).start())

        @pl.when(jnp.logical_not(solver))
        def _():
            remote(ybuf, xbuf, xsend_sem.at[0], xrecv_sem.at[0], (r, t * per)).wait_recv()

        send_first(xbuf[...], bas_hi[...], bas_lo[...])

    frecv[r] = fsend[...]

    def f_wait(d):
        q = (r + d) % R
        remote(fsend, frecv.at[q], fsend_sem.at[d], frecv_sem.at[q], (q, c)).wait_recv()

    each(1, R, f_wait)
    first = frecv[0]
    for i in range(1, R):
        first = first + frecv[i]
    ends = product(first, end_hi[...], end_lo[...], dot_nn)
    coefficients[0] = ends[:, :nb]
    coefficients[1] = ends[:, nb:2 * nb]
    projected[0] = xbuf[:nvec] - ends[:, 2 * nb:2 * nb + rows]
    projected[1] = xbuf[nvec:] - ends[:, 2 * nb + rows:]

    each(1, R, lambda d: f_copy(d).wait_send())
    for i in range(steps):
        gram_copy(i).wait_send()

    def parts_sent(sweep):
        for d in range(1, share):
            part_copy(sweep, d).wait_send()

    @pl.when(t == 0)
    def _():
        parts_sent(1)
        for d in range(1, share):
            t_copy(d).wait_send()

    @pl.when(solver)
    def _():
        parts_sent(0)

        @pl.when(speaks)
        def _():
            each((t + 1) * share, R, lambda rr: b_copy(ybuf, rr).wait_send())

        @pl.when(t == 0)
        def _():
            each(1, C // per, lambda tt: y_copy(tt).wait_send())

        @pl.when(t > 0)
        def _():
            parts_sent(1)

            @pl.when(speaks)
            def _():
                each(0, t * share, lambda rr: b_copy(xbuf, rr).wait_send())

            each(0, t, lambda tt: x_copy(tt).wait_send())
            each(t + 1, C // per, lambda tt: x_copy(tt).wait_send())

    @pl.when(jnp.logical_not(solver))
    def _():
        v_each(lambda copy: copy.wait_send())


def hub_kernel(
    R, C, factor, lower, upper, krylov, basis, projected, coefficients,
    fac_in, f_first, up_in, bas_in, up_recv, f_recv,
    low_hi, low_lo, up_hi, up_lo, fac_hi, fac_lo, turn_hi, turn_lo,
    bas_hi, bas_lo, end_hi, end_lo, gather, gather_one,
    asend, arecv, ybuf, yrecv, dsend, drecv, esend, erecv, gsend, xrecv, gacc, grecv,
    load_sem, send_sem, recv_sem, next_sem, all_sem,
):
    tile, rows = lower.shape[1], lower.shape[2]
    width = factor.shape[2]
    nvec = krylov.shape[1]
    nb = basis.shape[1]
    share = tile // rows
    per = tile // width
    half = share // 2
    steps = R.bit_length() - 1
    r = lax.axis_index("row")
    c = lax.axis_index("col")
    me = r * C + c
    t, p = r // share, r % share
    y, z = p % half, p // half
    lead = per - 1
    main = c == lead
    hub = main & (z == 1 - t)
    side = c == 0

    def partner(i):
        return r + (1 << i) * (1 - 2 * ((r // (1 << i)) % 2))

    def remote(src, dst, send, recv, dest):
        return pltpu.make_async_remote_copy(
            src_ref=src, dst_ref=dst, send_sem=send, recv_sem=recv, device_id=dest, device_id_type=MESH
        )

    low_in, kry_in = f_first.at[:, pl.ds(0, tile)], f_first.at[:, pl.ds(tile, nvec)]

    def load(i, src, dst):
        return pltpu.make_async_copy(src, dst, load_sem.at[i])

    barrier = pltpu.get_barrier_semaphore()
    guide = (c == per) & (t == 1) & (z == 0)
    far = (c >= per) & (t == 0)
    parted = far & (z == 0) & (c == per)
    aid = (c == C - 1) & (t == 1) & (z == 1)

    def greet(rr, cc):
        pl.semaphore_signal(barrier, inc=1, device_id=(rr, cc), device_id_type=MESH)

    @pl.when(main)
    def _():
        @pl.when(hub)
        def _():
            for d in range(1, share):
                greet(t * share + (p + d) % share, c)

        greet(r, 0)

        @pl.when(t == 1)
        def _():
            for i in range(half):
                greet(half + i, 0)

        @pl.when(hub & (t == 0))
        def _():
            for cc in range(per, C):
                greet(r, cc)
                greet(y, cc)

        @pl.when(hub & (t == 1))
        def _():
            greet(share + half + y, C - 1)

        @pl.when((t == 0) & (z == 0))
        def _():
            greet(r, per)

    @pl.when(side)
    def _():
        for i in range(steps):
            greet(partner(i), c)

    @pl.when(c >= per)
    def _():
        greet(r, 0)

    for i in range(half):
        @pl.when(jnp.logical_not(guide & (y == i)))
        def _():
            greet(share + i, per)

    @pl.when(main)
    def _():
        load(0, lower, low_in).start()
        load(0, krylov, kry_in).start()

        @pl.when(t == 1)
        def _():
            load(1, factor, fac_in).start()

        @pl.when(hub)
        def _():
            load(2, upper, up_in).start()

    load(3, basis, bas_in).start()

    def arrive():
        count = jnp.where(main, jnp.where(hub, half - 1, half), jnp.where(
            side, steps + 1 + C - per + jnp.where((t == 0) & (z == 1), share, 0),
            jnp.where(guide, R * C - 1, jnp.where(parted, 2, 1)),
        ))
        @pl.when(main | side | far | guide | aid)
        def _():
            pl.semaphore_wait(barrier, count)

        @pl.when(side & (t == 0) & (z == 1))
        def _():
            pl.semaphore_signal(next_sem, inc=1, device_id=(r, lead), device_id_type=MESH)

        @pl.when(guide)
        def _():
            for i in range(2):
                pl.semaphore_signal(all_sem, inc=1, device_id=(half * (i + 1) + y, lead), device_id_type=MESH)

    def when(cond):
        return pl.when(cond)

    def pair(ref, axis=1):
        return jnp.concatenate([ref[0], ref[1]], axis)

    block, wave, bas, fac, ups, gram = 2 * nvec, 3 * nvec, 2 * nb, 2 * width, 2 * tile, 2 * nb * nb // rows
    AD, US, XS, YE, ES, TS, VS, OS, GS = range(9)
    MS = GS + steps

    def take(sem, count):
        if count > ups:
            ref = f_recv.at[:, :, :, pl.ds(0, count * rows // (4 * per * width))]
        else:
            ref = up_recv.at[:, pl.ds(0, count // 2)]
        remote(ref, ref, send_sem.at[0], sem, ((r + 1) % R, c)).wait_recv()

    def send(src, dst, recv, dest, way=0):
        return remote(src, dst, send_sem.at[way], recv_sem.at[recv], dest)

    def a_copy(i):
        i = (y + 1 + i) % half
        return send(asend.at[i], arecv.at[p], AD, (half + i, c))

    def y_copy(i):
        i = (1 - i // half) * half + (y + 1 + i) % half
        return send(ybuf, yrecv.at[y], YE, (share + i, c))

    def u_copy(first, count):
        at = pl.ds(first * (tile // 2), count * (tile // 2))
        return send(upper.at[:, at], up_recv.at[:, at], US, (t * share + (1 - z) * half + y, lead))

    def m_near():
        return send(factor, f_recv.at[0, 0], MS, (r, lead))

    def m_far():
        return send(factor, f_recv.at[z, c % per], MS + z * per + c % per, (half + y, lead))

    def m_part(i):
        return send(factor.at[i], f_recv.at[0, 0, i], MS, (half * (1 - i) + y, lead))

    def m_relay():
        return send(f_recv.at[0, 0, 1], f_recv.at[0, 0, 1], MS, (half + y, lead))

    def t_copy():
        return send(basis, gather.at[p], TS, (half + y, lead))

    def v_copy(i):
        if i == 0:
            return send(basis, gather.at[p], VS, (half + (y + 1) % half, lead))
        return send(gather.at[y], gather.at[y], VS, (half + (y + 1) % half, lead))

    def o_copy():
        return send(basis, gather_one.at[z], OS, (half + y, lead))

    def d_copy(i):
        i = (y + 1 + i) % half
        return send(dsend.at[i], drecv.at[p], AD, (share + i, c))

    def e_copy(i):
        h, k = i // half, (y + 1 + i) % half
        at = pl.ds(h * half, half)
        return send(esend.at[at], erecv.at[y, at], YE + h, (half + k, c))

    def x_copy(i):
        k, cc = i // C, i % C
        return send(esend.at[k], xrecv.at[y, pl.ds(0, block)], XS, (t * share + k, cc))

    def f_copy(i):
        at = pl.ds(block, nvec)
        return send(gsend.at[0, at], xrecv.at[y, at], XS, (i // C, i % C), 1)

    def z_copy(i):
        k, cc = i // C, i % C
        return send(gsend.at[k], xrecv.at[y], XS, (k, cc), 1)

    def g_copy(i):
        return send(gacc.at[i], grecv.at[i], GS + i, (partner(i), c))

    def h_copy(cc):
        return send(gacc.at[steps], grecv.at[steps], GS, (r, cc))

    def each(first_index, last_index, act, skip=None):
        def body(i, carry):
            if skip is None:
                act(i)
            else:
                @pl.when(i != skip)
                def _():
                    act(i)
            return carry

        lax.fori_loop(first_index, last_index, body, 0)

    def store(hi, lo, index, value):
        high, low = split(value)
        hi[index] = high
        lo[index] = low

    def wide(value):
        return jnp.concatenate([value[:nvec], value[nvec:]], 1)

    def start_sends():
        @when(side & (t == 1))
        def _():
            m_near().start()

        @when(far & jnp.logical_not(parted))
        def _():
            m_far().start()

        @when(parted)
        def _():
            for i in range(2):
                m_part(1 - i).start()

        @when(main & (t == 1) & (z == 1))
        def _():
            u_copy(0, 1).start()

        @when(aid)
        def _():
            u_copy(1, 1).start()

    def put_pairs(ref, out):
        for i in range(half):
            for k in range(2):
                ref[i, k] = out[:, (k * half + i) * rows:(k * half + i + 1) * rows]

    def times(values, high, low):
        left = jnp.concatenate([complex_left(v, nvec) for v in values], 1)
        return product(left, high, low, dot_nn)

    def turn(hi, lo, row, col, value):
        high, low = split(value.T)
        at = (slice(row, row + value.shape[1]), slice(col, col + value.shape[0]))
        hi[at] = high
        lo[at] = low

    def turn_pair(hi, lo, row, col, ref):
        for i in range(2):
            turn(hi, lo, row + i * ref.shape[2], col, ref[i])

    def turn_parts(row, ref):
        for i in range(2):
            for h in range(2):
                turn(up_hi, up_lo, row + i * rows, h * gap, ref[i, h * width:(h + 1) * width])

    def first_loads():
        at = pl.ds(0, tile + nvec)
        pltpu.make_async_copy(f_first.at[:, at], f_first.at[:, at], load_sem.at[0]).wait()

    span = 2 * rows
    gap = width + rows
    broad = 2 * width

    @when(main & (t == 0))
    def _():
        first_loads()
        store(low_hi, low_lo, ..., pair(low_in))
        left = complex_left([pair(kry_in, 0)], nvec)
        put_pairs(asend, product(left, low_hi[...], low_lo[...], dot_nt))

    arrive()

    @when(main & (t == 0))
    def _():
        each(0, jnp.where(hub, half - 1, half), lambda i: a_copy(i).start())

    start_sends()

    @when(main & (t == 0))
    def _():
        @when(hub)
        def _():
            arecv[p] = asend[y]
            take(recv_sem.at[AD], (share - 1) * 2 * block)
            parts = [arecv[q] for q in range(share)]
            ybuf[...] = (parts[0] + parts[1]) + (parts[2] + parts[3])
            pl.semaphore_wait(next_sem, 1)
            for i in range(share):
                y_copy(i).start()

        @when(hub)
        def _():
            v_copy(0).start()

        @when(jnp.logical_not(hub))
        def _():
            t_copy().start()
            u_copy(0, 2).start()
            take(recv_sem.at[MS], fac // 2)
            m_relay().start()

    load(3, basis, bas_in).wait()

    def prepare_basis():
        top = pair(bas_in)
        bottom = jnp.concatenate([-bas_in[1], bas_in[0]], 1)
        store(bas_hi, bas_lo, ..., jnp.concatenate([top, bottom], 0))
        return top

    def prepare_end(top):
        gram = jnp.concatenate([top, jnp.concatenate([-top[:, nb:], top[:, :nb]], 1)], 0)
        row_id = lax.broadcasted_iota(jnp.int32, gram.shape, 0)
        col_id = lax.broadcasted_iota(jnp.int32, gram.shape, 1)
        twice = jnp.where(row_id == col_id, 2.0, 0.0) - gram
        spread = product(twice, bas_hi[...], bas_lo[...], dot_nn)
        store(end_hi, end_lo, ..., jnp.concatenate([twice, spread], 1))

    def end_from_side():
        prepare_basis()
        take(recv_sem.at[GS], gram)
        prepare_end(grecv[steps])

    @when(side)
    def _():
        gacc[0] = product(prepare_basis(), bas_hi[...], bas_lo[...], dot_nt)
        for i in range(steps):
            g_copy(i).start()
            take(recv_sem.at[GS + i], gram)
            gacc[i + 1] = gacc[i] + grecv[i]
        each(1, C, lambda cc: h_copy(cc).start())
        prepare_end(gacc[steps])

    @when(c > lead)
    def _():
        end_from_side()

    @when(main & (t == 1))
    def _():
        first_loads()
        load(1, factor, fac_in).wait()
        turn_pair(turn_hi, turn_lo, 0, 0, low_in)
        turn_pair(fac_hi, fac_lo, broad, 0, fac_in)
        take(recv_sem.at[MS], fac)
        turn_pair(fac_hi, fac_lo, 0, 0, f_recv.at[0, 0])

        @when(hub)
        def _():
            load(2, upper, up_in).wait()
            turn_pair(up_hi, up_lo, 0, 0, up_in)

        take(recv_sem.at[YE], half * 2 * block)
        parts = [[yrecv[i, h] for i in range(half)] for h in range(per)]
        g = pair(kry_in, 0) - times(parts, fac_hi[:, :rows], fac_lo[:, :rows])
        ybuf[0] = g

        @when(main)
        def _():
            put_pairs(dsend, times([[ybuf[0]]], turn_hi[...], turn_lo[...]))

        each(0, jnp.where(hub, half - 1, half), lambda i: d_copy(i).start())
        o_copy().start()

        @when(hub)
        def _():
            drecv[p] = dsend[y]
            take(recv_sem.at[US], ups)
            turn_pair(up_hi, up_lo, span, 0, up_recv)

            take(recv_sem.at[AD], (share - 1) * 2 * block)
            parts = [drecv[q] for q in range(share)]
            total = (parts[0] + parts[1]) + (parts[2] + parts[3])
            out = times([[total[0]], [total[1]]], up_hi[:, :tile], up_lo[:, :tile])
            for h in range(per):
                for k in range(half):
                    esend[h * half + k] = out[:, (h * half + k) * rows:(h * half + k + 1) * rows]
                for k in range(half):
                    e_copy(h * half + k).start()
            pl.semaphore_wait(all_sem, 1)
            each(0, share * C, lambda i: x_copy(i).start(), p * C + c)
            xrecv[y, :block] = esend[p]

        end_from_side()

    @when(main & (t == 0))
    def _():
        @when(hub)
        def _():
            load(2, upper, up_in).wait()
            turn_parts(span, up_in)
            gather[p] = bas_in[...]
            take(recv_sem.at[TS], bas)
            v_copy(1).start()
            take(recv_sem.at[VS], 2 * bas)
            stacked = jnp.concatenate(
                [jnp.concatenate([gather[q, i] for q in range(share)], 1) for i in range(2)], 0
            )
            take(recv_sem.at[US], ups)
            turn_parts(0, up_recv)
            for k in range(2):
                at = slice(k * span, (k + 1) * span)
                high = jnp.concatenate([up_hi[at, :width], up_hi[at, gap:]], 1)
                low = jnp.concatenate([up_lo[at, :width], up_lo[at, gap:]], 1)
                out = product(stacked, high, low, dot_nt)
                turn(up_hi, up_lo, k * span, width, out[:nb, :rows] + out[nb:, rows:])
                turn(up_hi, up_lo, k * span + rows, width, out[:nb, rows:] - out[nb:, :rows])
            take(recv_sem.at[OS], 2 * bas)
            empty = jnp.zeros((nb, rows), F32)
            for h in range(per):
                one = gather_one[h]
                for i in range(2):
                    own = (1 - 2 * i) * one[i]
                    own = jnp.where(y == 0, jnp.concatenate([own, empty], 1), jnp.concatenate([empty, own], 1))
                    turn(fac_hi, fac_lo, h * broad + i * width, span, own)
            pl.semaphore_wait(all_sem, 1)
            for h in range(per):
                for k in range(2):
                    take(recv_sem.at[MS + k * per + h], fac)
                    turn_pair(fac_hi, fac_lo, h * broad, k * rows, f_recv.at[k, h])
            out = 0.0
            for h in range(per):
                take(recv_sem.at[YE + h], half * half * block)
                x = [erecv[0, h * half + k] + erecv[1, h * half + k] for k in range(half)]
                at = slice(h * broad, (h + 1) * broad)
                out = out + times([x], fac_hi[at], fac_lo[at])
            for k in range(2):
                yrecv[0, k] = ybuf[k] - out[:, k * rows:(k + 1) * rows]
            gsend[0, :, :nb] = jnp.concatenate([out[:, span:], out[:nvec, span:]], 0)

            @when(main)
            def _():
                w = [[yrecv[0, 0]], [yrecv[0, 1]]]
                more = times(w, up_hi[:, :width + nb], up_lo[:, :width + nb])
                first = wide(gsend[0, :block, :nb] + more[:, width:])
                for k in range(share):
                    if k == half:
                        more = times(w, up_hi[:, gap:], up_lo[:, gap:])
                    gsend[k, block:] = first
                    gsend[k, :block] = more[:, (k % half) * rows:(k % half + 1) * rows]
                    for cc in range(C):
                        if k < half or cc != lead:
                            z_copy(k * C + cc).start()
                        else:
                            @when(p != k)
                            def _():
                                z_copy(k * C + cc).start()

            each(share * C, R * C, lambda i: f_copy(i).start())
            xrecv[y] = gsend[p]
            end_from_side()

        @when(jnp.logical_not(hub))
        def _():
            end_from_side()

    @when(jnp.logical_not(hub))
    def _():
        take(recv_sem.at[XS], 2 * wave)

    for i in range(2):
        @when(hub & (t == i))
        def _():
            take(recv_sem.at[XS], wave + i * nvec)

    total = xrecv[0] + xrecv[1]
    ends = product(total[block:], end_hi[...], end_lo[...], dot_nn)
    coefficients[0] = ends[:, :nb]
    coefficients[1] = ends[:, nb:2 * nb]
    projected[0] = total[:nvec] - ends[:, 2 * nb:2 * nb + rows]
    projected[1] = total[nvec:block] - ends[:, 2 * nb + rows:]

    def sent(cond, count, way=0):
        @when(cond)
        def _():
            take(send_sem.at[way], count)

    others = share * C - 1
    sent(main & (t == 0) & (z == 0), half * 2 * block + bas + ups + fac // 2)
    sent(hub & (t == 0), (half - 1) * 2 * block + 2 * bas + share * 2 * block)
    sent(hub & (t == 0), others * wave + share * C * nvec, 1)
    sent(main & (t == 1) & (z == 1), half * 2 * block + bas + ups // 2)
    sent(hub & (t == 1), (half - 1) * 2 * block + bas + half * share * block + others * block)
    sent(side & (t == 0), (steps + C - 1) * gram)
    sent(side & (t == 1), (steps + C - 1) * gram + fac)
    sent(far, fac)
    sent(aid, ups // 2)


def hub_call(R, C, factor, lower, upper, krylov, basis):
    tile, rows = lower.shape[1], lower.shape[2]
    width = factor.shape[2]
    nvec, nb = krylov.shape[1], basis.shape[1]
    share, per = tile // rows, tile // width
    half = share // 2
    steps = R.bit_length() - 1
    dma = pltpu.SemaphoreType.DMA
    vmem = pl.BlockSpec(memory_space=pltpu.VMEM)
    block = (2 * nvec, rows)
    f32 = lambda *shape: pltpu.VMEM(shape, F32)
    bf16 = lambda *shape: [pltpu.VMEM(shape, BF16)] * 2
    return pl.pallas_call(
        functools.partial(hub_kernel, R, C),
        out_shape=(pltpu.VMEM(krylov.shape, F32), pltpu.VMEM((2, nvec, nb), F32)),
        in_specs=[pl.BlockSpec(memory_space=pl.ANY)] * 5,
        out_specs=(vmem, vmem),
        scratch_shapes=[
            f32(*factor.shape), f32(2, tile + nvec, rows), f32(*upper.shape), f32(*basis.shape),
            f32(*upper.shape), f32(2, per, *factor.shape),
            *bf16(tile, 2 * rows), *bf16(4 * rows, tile + rows), *bf16(2 * tile, 2 * rows + nb), *bf16(2 * rows, tile),
            *bf16(2 * nb, 2 * rows), *bf16(2 * nb, 2 * nb + 2 * rows),
            f32(share, *basis.shape), f32(2, *basis.shape),
            f32(half, 2, *block), f32(share, 2, *block), f32(2, *block), f32(half, 2, *block),
            f32(half, 2, *block), f32(share, 2, *block), f32(share, *block), f32(2, share, *block),
            f32(share, 3 * nvec, rows), f32(half, 3 * nvec, rows),
            f32(steps + 1, nb, 2 * nb), f32(steps + 1, nb, 2 * nb),
            dma((4,)), dma((2,)), dma((8 + steps + 2 * per,)),
            pltpu.SemaphoreType.REGULAR, pltpu.SemaphoreType.REGULAR,
        ],
        compiler_params=pltpu.CompilerParams(collective_id=0, has_side_effects=True),
        name="krylov_hubs",
    )(factor, lower, upper, krylov, basis)


def finish(projected, turned, projected_out, turned_out, sems):
    copies = [
        pltpu.make_async_copy(projected, projected_out, sems.at[0]),
        pltpu.make_async_copy(turned, turned_out, sems.at[1]),
    ]
    for copy in copies:
        copy.start()
    for copy in copies:
        copy.wait()


def general_call(R, C, factor, lower, upper, krylov, basis):
    tile, rows = lower.shape[1], lower.shape[2]
    width = factor.shape[2]
    nvec, nb = krylov.shape[1], basis.shape[1]
    share, per, pieces = tile // rows, tile // width, width // rows
    steps = R.bit_length() - 1
    dma = pltpu.SemaphoreType.DMA
    vmem = pl.BlockSpec(memory_space=pltpu.VMEM)
    block = (2 * nvec, rows)
    return pl.pallas_call(
        functools.partial(kernel, R, C),
        out_shape=(
            jax.ShapeDtypeStruct(krylov.shape, F32),
            jax.ShapeDtypeStruct((2, nvec, nb), F32),
        ),
        in_specs=[vmem] * 5,
        out_specs=(vmem, vmem),
        scratch_shapes=[
            pltpu.VMEM((2, tile, 2 * rows), BF16),
            pltpu.VMEM((2, tile, 2 * rows), BF16),
            pltpu.VMEM((rows, 2 * width), BF16),
            pltpu.VMEM((rows, 2 * width), BF16),
            pltpu.VMEM((2 * nb, 2 * rows), BF16),
            pltpu.VMEM((2 * nb, 2 * rows), BF16),
            pltpu.VMEM((2 * nb, 2 * nb + 2 * rows), BF16),
            pltpu.VMEM((2 * nb, 2 * nb + 2 * rows), BF16),
            pltpu.VMEM((2 * nb, 2 * rows), BF16),
            pltpu.VMEM((2 * nb, 2 * rows), BF16),
            pltpu.VMEM((share, 2, nb, rows), F32),
            pltpu.VMEM((2, share) + block, F32),
            pltpu.VMEM((2, share) + block, F32),
            pltpu.VMEM(block, F32),
            pltpu.VMEM(block, F32),
            pltpu.VMEM((pieces,) + block, F32),
            pltpu.VMEM(block, F32),
            pltpu.VMEM((C,) + block, F32),
            pltpu.VMEM((nvec, 2 * nb), F32),
            pltpu.VMEM((R, nvec, 2 * nb), F32),
            pltpu.VMEM((steps + 1, nb, 2 * nb), F32),
            pltpu.VMEM((steps, nb, 2 * nb), F32),
            dma((2, share)),
            dma((2, share)),
            dma((R,)),
            dma((pieces,)),
            dma((C,)),
            dma((C,)),
            dma((C // per,)),
            dma((1,)),
            dma((R,)),
            dma((R,)),
            dma((steps,)),
            dma((steps,)),
            dma((share,)),
            dma((share,)),
            dma((C // per,)),
            dma((1,)),
            pltpu.SemaphoreType.REGULAR,
        ],
        compiler_params=pltpu.CompilerParams(collective_id=0, has_side_effects=True),
        name="krylov_step",
    )(factor, lower, upper, krylov, basis)


def local(R, C, factor, lower, upper, krylov, basis):
    tile, rows = lower.shape[1], lower.shape[2]
    share, per = tile // rows, tile // factor.shape[2]
    vmem = pl.BlockSpec(memory_space=pltpu.VMEM)
    paired = R == 2 * share and C == 2 * per and share == 4 and per == 2
    call = hub_call if paired else general_call
    projected, turned = call(R, C, factor, lower, upper, krylov, basis)
    if paired:
        projected, turned = [pltpu.with_memory_space_constraint(x, pltpu.VMEM) for x in (projected, turned)]
    projected, turned = pl.pallas_call(
        finish,
        out_shape=(jax.ShapeDtypeStruct(projected.shape, F32), jax.ShapeDtypeStruct(turned.shape, F32)),
        in_specs=[vmem] * 2,
        out_specs=[pl.BlockSpec(memory_space=pl.ANY)] * 2,
        scratch_shapes=[pltpu.SemaphoreType.DMA((2,))],
        name="finish",
    )(projected, turned)
    return projected, turned.transpose(0, 2, 1)


def solution(mesh):
    in_specs = (
        P(None, "row", "col"),
        P(None, None, "row"),
        P(None, None, "row"),
        P(None, None, "row"),
        P(None, None, "row"),
    )
    out_specs = (P(None, None, "row"), P())
    body = functools.partial(local, mesh.shape["row"], mesh.shape["col"])
    return jax.shard_map(body, mesh=mesh, in_specs=in_specs, out_specs=out_specs, check_vma=False)
```

```python
import functools

import jax
import jax.numpy as jnp
from jax import lax
from jax.experimental import pallas as pl
from jax.experimental.pallas import tpu as pltpu
from jax.sharding import PartitionSpec as P

MESH = pl.DeviceIdType.MESH
F32 = jnp.float32
BF16 = jnp.bfloat16


def split(value):
    high = value.astype(BF16)
    low = (value - high.astype(F32)).astype(BF16)
    return high, low


def dot_nt(left, right):
    return lax.dot_general(left, right, (((1,), (1,)), ((), ())), preferred_element_type=F32)


def dot_nn(left, right):
    return lax.dot_general(left, right, (((1,), (0,)), ((), ())), preferred_element_type=F32)


def product(left, high, low, dot):
    rows = left.shape[0]
    left_high, left_low = split(left)
    both = dot(jnp.concatenate([left_high, left_low], 0), high)
    return both[:rows] + (both[rows:] + dot(left_high, low))


def complex_left(pieces, nvec):
    re = [x[:nvec] for x in pieces]
    im = [x[nvec:] for x in pieces]
    top = jnp.concatenate(re + [-x for x in im], 1)
    bottom = jnp.concatenate(im + re, 1)
    return jnp.concatenate([top, bottom], 0)


def kernel(
    R, C, factor, lower, upper, krylov, basis, projected, coefficients,
    inv_hi, inv_lo, fac_hi, fac_lo, bas_hi, bas_lo,
    end_hi, end_lo, lead_hi, lead_lo, gather,
    psend, precv, ybuf, xbuf, bcast, vbuf, vrecv, fsend, frecv, gacc, grecv,
    psend_sem, precv_sem, bsend_sem, brecv_sem, vsend_sem, vrecv_sem, xsend_sem, xrecv_sem,
    fsend_sem, frecv_sem, gsend_sem, grecv_sem, tsend_sem, trecv_sem, ysend_sem, yrecv_sem,
    ready_sem,
):
    tile, rows = lower.shape[1], lower.shape[2]
    width = factor.shape[2]
    nvec = krylov.shape[1]
    nb = basis.shape[1]
    share = tile // rows
    per = tile // width
    pieces = width // rows
    steps = R.bit_length() - 1
    r = lax.axis_index("row")
    c = lax.axis_index("col")
    t, p = r // share, r % share
    j, h = c // per, c % per
    solver = j == t

    barrier = pltpu.get_barrier_semaphore()

    def greet_mate(i, carry):
        pl.semaphore_signal(barrier, inc=1, device_id=(t * share + (p + 1 + i) % share, c), device_id_type=MESH)
        return carry

    def greet_tile(i, carry):
        pl.semaphore_signal(barrier, inc=1, device_id=((r + (1 + i) * share) % R, c), device_id_type=MESH)
        return carry

    def greet_col(i, carry):
        pl.semaphore_signal(barrier, inc=1, device_id=(r, (c + 1 + i) % C), device_id_type=MESH)
        return carry

    lax.fori_loop(0, share - 1, greet_mate, 0)
    lax.fori_loop(0, R // share - 1, greet_tile, 0)
    lax.fori_loop(0, C - 1, greet_col, 0)

    def prepare(ref, slot):
        high, low = split(jnp.concatenate([ref[0], ref[1]], 1))
        inv_hi[slot] = high
        inv_lo[slot] = low

    @pl.when(solver)
    def _():
        prepare(lower, 0)

    @pl.when(jnp.logical_not(solver))
    def _():
        high, low = split(jnp.concatenate([factor[0], factor[1]], 1))
        fac_hi[...] = high
        fac_lo[...] = low

    def prepare_basis():
        top = jnp.concatenate([basis[0], basis[1]], 1)
        bottom = jnp.concatenate([-basis[1], basis[0]], 1)
        high, low = split(jnp.concatenate([top, bottom], 0))
        bas_hi[...] = high
        bas_lo[...] = low
        gacc[0] = product(top, high, low, dot_nt)

    def remote(src, dst, send, recv, dest):
        return pltpu.make_async_remote_copy(
            src_ref=src, dst_ref=dst, send_sem=send, recv_sem=recv, device_id=dest, device_id_type=MESH
        )

    def each(first_index, last_index, act):
        def body(i, carry):
            act(i)
            return carry

        lax.fori_loop(first_index, last_index, body, 0)

    def gram_copy(i):
        other = r + (1 << i) * (1 - 2 * ((r // (1 << i)) % 2))
        return remote(gacc.at[i], grecv.at[i], gsend_sem.at[i], grecv_sem.at[i], (other, c))

    def gram_all():
        for i in range(steps):
            copy = gram_copy(i)
            copy.start()
            copy.wait_recv()
            gacc[i + 1] = gacc[i] + grecv[i]
        top = gacc[steps]
        gram = jnp.concatenate([top, jnp.concatenate([-top[:, nb:], top[:, :nb]], 1)], 0)
        row_id = lax.broadcasted_iota(jnp.int32, gram.shape, 0)
        col_id = lax.broadcasted_iota(jnp.int32, gram.shape, 1)
        twice = jnp.where(row_id == col_id, 2.0, 0.0) - gram
        spread = product(twice, bas_hi[...], bas_lo[...], dot_nn)
        high, low = split(jnp.concatenate([twice, spread], 1))
        end_hi[...] = high
        end_lo[...] = low

    def t_copy(d):
        q = (p + d) % share
        return remote(basis, gather.at[p], tsend_sem.at[d], trecv_sem.at[p], (t * share + q, c))

    def lead_send():
        for d in range(1, share):
            t_copy(d).start()
        gather[p] = basis[...]

    def lead_all():
        for d in range(1, share):
            q = (p + d) % share
            remote(basis, gather.at[q], tsend_sem.at[d], trecv_sem.at[q], (t * share + q, c)).wait_recv()
        left = jnp.concatenate(
            [jnp.concatenate([gather[q, i] for q in range(share)], 1) for i in range(2)], 0
        )
        out = product(left, inv_hi[1], inv_lo[1], dot_nn)
        one = out[:nb, :rows] + out[nb:, rows:]
        two = out[nb:, :rows] - out[:nb, rows:]
        whole = jnp.concatenate([jnp.concatenate([one, two], 1), jnp.concatenate([-two, one], 1)], 0)
        high, low = split(whole)
        lead_hi[...] = high
        lead_lo[...] = low

    def side_work():
        gram_all()

        @pl.when(t == 0)
        def _():
            lead_send()
            lead_all()

    def part_copy(sweep, d):
        q = (p + d) % share
        return remote(
            psend.at[sweep, q], precv.at[sweep, p], psend_sem.at[sweep, q], precv_sem.at[sweep, p], (t * share + q, c)
        )

    def part_arrival(sweep, d):
        q = (p + d) % share
        return remote(
            psend.at[sweep, q], precv.at[sweep, q], psend_sem.at[sweep, q], precv_sem.at[sweep, q], (t * share + q, c)
        ), q

    def v_copy(cc):
        return remote(vbuf, vrecv.at[c], vsend_sem.at[cc], vrecv_sem.at[c], (r, cc))

    def v_each(act):
        @pl.when(t > 0)
        def _():
            for hh in range(per):
                act(v_copy(t * per + hh))

        @pl.when(t == 0)
        def _():
            each(1, C, lambda d: act(v_copy((c + d) % C)))

    def v_sum(first_col, last_col, value):
        def body(cc, total):
            @pl.when(cc != c)
            def _():
                remote(vbuf, vrecv.at[cc], vsend_sem.at[0], vrecv_sem.at[cc], (r, cc)).wait_recv()

            return total - vrecv[cc]

        return lax.fori_loop(first_col, last_col, body, value)

    def f_copy(d):
        return remote(fsend, frecv.at[r], fsend_sem.at[d], frecv_sem.at[r], ((r + d) % R, c))

    def send_first(value, high, low):
        wide_value = jnp.concatenate([value[:nvec], value[nvec:]], 1)
        fsend[...] = product(wide_value, high, low, dot_nt)
        each(1, R, lambda d: f_copy(d).start())

    def multiply(sweep, g):
        out = product(complex_left([g], nvec), inv_hi[sweep], inv_lo[sweep], dot_nt)
        for q in range(share):
            psend[sweep, q] = out[:, q * rows:(q + 1) * rows]

    def solve(sweep, g):
        multiply(sweep, g)
        return exchange(sweep)

    def exchange(sweep):
        for d in range(1, share):
            part_copy(sweep, d).start()
        total = psend[sweep, p]
        for d in range(1, share):
            arrival, q = part_arrival(sweep, d)
            arrival.wait_recv()
            total = total + precv[sweep, q]
        return total

    def b_copy(buf, rr):
        return remote(buf, bcast.at[p % pieces], bsend_sem.at[rr], brecv_sem.at[p % pieces], (rr, c))

    def x_copy(tt):
        cc = tt * per + h
        return remote(xbuf, xbuf, xsend_sem.at[tt], xrecv_sem.at[0], (r, cc))

    def y_copy(tt):
        return remote(ybuf, ybuf, ysend_sem.at[tt], yrecv_sem.at[0], (r, tt * per + h))

    speaks = p // pieces == h

    @pl.when(solver != (t == 0))
    def _():
        prepare(upper, 1)

    @pl.when(j > 0)
    def _():
        prepare_basis()

    @pl.when(jnp.logical_and(solver, t == 0))
    def _():
        multiply(0, jnp.concatenate([krylov[0], krylov[1]], 0))

    pl.semaphore_wait(barrier, share - 1 + R // share - 1 + C - 1)
    for d in range(1, share):
        pl.semaphore_signal(
            ready_sem, inc=1, device_id=(t * share + (p + d) % share, c), device_id_type=MESH
        )

    @pl.when(j > 0)
    def _():
        side_work()

    @pl.when(solver)
    def _():
        @pl.when(t > 0)
        def _():
            b = jnp.concatenate([krylov[0], krylov[1]], 0)
            multiply(0, v_sum(0, t * per, b))

        ybuf[...] = exchange(0)
        pl.semaphore_wait(ready_sem, share - 1)

        @pl.when(speaks)
        def _():
            each((t + 1) * share, R, lambda rr: b_copy(ybuf, rr).start())

        @pl.when(t == 0)
        def _():
            each(1, C // per, lambda tt: y_copy(tt).start())
            prepare(upper, 1)

    @pl.when(jnp.logical_not(solver))
    def _():
        pl.semaphore_wait(ready_sem, share - 1)
        got = []
        for i in range(pieces):
            remote(ybuf, bcast.at[i], bsend_sem.at[0], brecv_sem.at[i], (r, t * per)).wait_recv()
            got.append(bcast[i])
        value = product(complex_left(got, nvec), fac_hi[...], fac_lo[...], dot_nt)
        vbuf[...] = value
        v_each(lambda copy: copy.start())
        vrecv[c] = value

    @pl.when(j == 0)
    def _():
        prepare_basis()
        side_work()

    @pl.when(t == 0)
    def _():
        @pl.when(jnp.logical_not(solver))
        def _():
            remote(ybuf, ybuf, ysend_sem.at[0], yrecv_sem.at[0], (r, h)).wait_recv()

        g = v_sum(per, C, ybuf[...])
        send_first(g, lead_hi[...], lead_lo[...])
        xbuf[...] = solve(1, g)

    @pl.when(t > 0)
    def _():
        @pl.when(solver)
        def _():
            xbuf[...] = solve(1, v_sum((t + 1) * per, C, ybuf[...]))

            @pl.when(speaks)
            def _():
                each(0, t * share, lambda rr: b_copy(xbuf, rr).start())

            each(0, t, lambda tt: x_copy(tt).start())
            each(t + 1, C // per, lambda tt: x_copy(tt).start())

        @pl.when(jnp.logical_not(solver))
        def _():
            remote(ybuf, xbuf, xsend_sem.at[0], xrecv_sem.at[0], (r, t * per)).wait_recv()

        send_first(xbuf[...], bas_hi[...], bas_lo[...])

    frecv[r] = fsend[...]

    def f_wait(d):
        q = (r + d) % R
        remote(fsend, frecv.at[q], fsend_sem.at[d], frecv_sem.at[q], (q, c)).wait_recv()

    each(1, R, f_wait)
    first = frecv[0]
    for i in range(1, R):
        first = first + frecv[i]
    ends = product(first, end_hi[...], end_lo[...], dot_nn)
    coefficients[0] = ends[:, :nb]
    coefficients[1] = ends[:, nb:2 * nb]
    projected[0] = xbuf[:nvec] - ends[:, 2 * nb:2 * nb + rows]
    projected[1] = xbuf[nvec:] - ends[:, 2 * nb + rows:]

    each(1, R, lambda d: f_copy(d).wait_send())
    for i in range(steps):
        gram_copy(i).wait_send()

    def parts_sent(sweep):
        for d in range(1, share):
            part_copy(sweep, d).wait_send()

    @pl.when(t == 0)
    def _():
        parts_sent(1)
        for d in range(1, share):
            t_copy(d).wait_send()

    @pl.when(solver)
    def _():
        parts_sent(0)

        @pl.when(speaks)
        def _():
            each((t + 1) * share, R, lambda rr: b_copy(ybuf, rr).wait_send())

        @pl.when(t == 0)
        def _():
            each(1, C // per, lambda tt: y_copy(tt).wait_send())

        @pl.when(t > 0)
        def _():
            parts_sent(1)

            @pl.when(speaks)
            def _():
                each(0, t * share, lambda rr: b_copy(xbuf, rr).wait_send())

            each(0, t, lambda tt: x_copy(tt).wait_send())
            each(t + 1, C // per, lambda tt: x_copy(tt).wait_send())

    @pl.when(jnp.logical_not(solver))
    def _():
        v_each(lambda copy: copy.wait_send())


def hub_kernel(
    R, C, factor, lower, upper, krylov, basis, projected, coefficients,
    fac_in, f_first, up_in, bas_in, up_recv, f_recv,
    low_hi, low_lo, up_hi, up_lo, fac_hi, fac_lo, turn_hi, turn_lo,
    bas_hi, bas_lo, end_hi, end_lo, gather, gather_one,
    asend, arecv, ybuf, yrecv, dsend, drecv, esend, erecv, gsend, xrecv, gacc, grecv,
    load_sem, send_sem, recv_sem, next_sem, all_sem,
):
    tile, rows = lower.shape[1], lower.shape[2]
    width = factor.shape[2]
    nvec = krylov.shape[1]
    nb = basis.shape[1]
    share = tile // rows
    per = tile // width
    half = share // 2
    steps = R.bit_length() - 1
    r = lax.axis_index("row")
    c = lax.axis_index("col")
    me = r * C + c
    t, p = r // share, r % share
    y, z = p % half, p // half
    lead = per - 1
    main = c == lead
    hub = main & (z == 1 - t)
    side = c == 0

    def partner(i):
        return r + (1 << i) * (1 - 2 * ((r // (1 << i)) % 2))

    def remote(src, dst, send, recv, dest):
        return pltpu.make_async_remote_copy(
            src_ref=src, dst_ref=dst, send_sem=send, recv_sem=recv, device_id=dest, device_id_type=MESH
        )

    low_in, kry_in = f_first.at[:, pl.ds(0, tile)], f_first.at[:, pl.ds(tile, nvec)]

    def load(i, src, dst):
        return pltpu.make_async_copy(src, dst, load_sem.at[i])

    barrier = pltpu.get_barrier_semaphore()
    guide = (c == per) & (t == 1) & (z == 0)
    far = (c >= per) & (t == 0)
    parted = far & (z == 0) & (c == per)
    aid = (c == C - 1) & (t == 1) & (z == 1)

    def greet(rr, cc):
        pl.semaphore_signal(barrier, inc=1, device_id=(rr, cc), device_id_type=MESH)

    @pl.when(main)
    def _():
        @pl.when(hub)
        def _():
            for d in range(1, share):
                greet(t * share + (p + d) % share, c)

        greet(r, 0)

        @pl.when(t == 1)
        def _():
            for i in range(half):
                greet(half + i, 0)

        @pl.when(hub & (t == 0))
        def _():
            for cc in range(per, C):
                greet(r, cc)
                greet(y, cc)

        @pl.when(hub & (t == 1))
        def _():
            greet(share + half + y, C - 1)

        @pl.when((t == 0) & (z == 0))
        def _():
            greet(r, per)

    @pl.when(side)
    def _():
        for i in range(steps):
            greet(partner(i), c)

    @pl.when(c >= per)
    def _():
        greet(r, 0)

    for i in range(half):
        @pl.when(jnp.logical_not(guide & (y == i)))
        def _():
            greet(share + i, per)

    @pl.when(main)
    def _():
        load(0, lower, low_in).start()
        load(0, krylov, kry_in).start()

        @pl.when(t == 1)
        def _():
            load(1, factor, fac_in).start()

        @pl.when(hub)
        def _():
            load(2, upper, up_in).start()

    load(3, basis, bas_in).start()

    def arrive():
        count = jnp.where(main, jnp.where(hub, half - 1, half), jnp.where(
            side, steps + 1 + C - per + jnp.where((t == 0) & (z == 1), share, 0),
            jnp.where(guide, R * C - 1, jnp.where(parted, 2, 1)),
        ))
        @pl.when(main | side | far | guide | aid)
        def _():
            pl.semaphore_wait(barrier, count)

        @pl.when(side & (t == 0) & (z == 1))
        def _():
            pl.semaphore_signal(next_sem, inc=1, device_id=(r, lead), device_id_type=MESH)

        @pl.when(guide)
        def _():
            for i in range(2):
                pl.semaphore_signal(all_sem, inc=1, device_id=(half * (i + 1) + y, lead), device_id_type=MESH)

    def when(cond):
        return pl.when(cond)

    def pair(ref, axis=1):
        return jnp.concatenate([ref[0], ref[1]], axis)

    block, wave, bas, fac, ups, gram = 2 * nvec, 3 * nvec, 2 * nb, 2 * width, 2 * tile, 2 * nb * nb // rows
    AD, US, XS, YE, ES, TS, VS, OS, GS = range(9)
    MS = GS + 1

    def take(sem, count):
        if count > ups:
            ref = f_recv.at[:, :, :, pl.ds(0, count * rows // (4 * per * width))]
        else:
            ref = up_recv.at[:, pl.ds(0, count // 2)]
        remote(ref, ref, send_sem.at[0], sem, ((r + 1) % R, c)).wait_recv()

    def send(src, dst, recv, dest, way=0):
        return remote(src, dst, send_sem.at[way], recv_sem.at[recv], dest)

    def a_copy(i):
        i = (y + 1 + i) % half
        return send(asend.at[i], arecv.at[p], AD, (half + i, c))

    def y_copy(i):
        i = (1 - i // half) * half + (y + 1 + i) % half
        return send(ybuf, yrecv.at[y], YE, (share + i, c))

    def u_copy(first, count):
        at = pl.ds(first * (tile // 2), count * (tile // 2))
        return send(upper.at[:, at], up_recv.at[:, at], US, (t * share + (1 - z) * half + y, lead))

    def m_near():
        return send(factor, f_recv.at[0, 0], MS, (r, lead))

    def m_far():
        return send(factor, f_recv.at[z, c % per], MS + z * per + c % per, (half + y, lead))

    def m_part(i):
        return send(factor.at[i], f_recv.at[0, 0, i], MS, (half * (1 - i) + y, lead))

    def m_relay():
        return send(f_recv.at[0, 0, 1], f_recv.at[0, 0, 1], MS, (half + y, lead))

    def t_copy():
        return send(basis, gather.at[p], TS, (half + y, lead))

    def v_copy(i):
        if i == 0:
            return send(basis, gather.at[p], VS, (half + (y + 1) % half, lead))
        return send(gather.at[y], gather.at[y], VS, (half + (y + 1) % half, lead))

    def o_copy():
        return send(basis, gather_one.at[z], OS, (half + y, lead))

    def d_copy(i):
        i = (y + 1 + i) % half
        return send(dsend.at[i], drecv.at[p], AD, (share + i, c))

    def e_copy(i):
        h, k = i // half, (y + 1 + i) % half
        at = pl.ds(h * half, half)
        return send(esend.at[at], erecv.at[y, at], YE + h, (half + k, c))

    def x_copy(i):
        k, cc = i // C, i % C
        return send(esend.at[k], xrecv.at[y, pl.ds(0, block)], XS, (t * share + k, cc))

    def f_copy(i):
        at = pl.ds(block, nvec)
        return send(gsend.at[0, at], xrecv.at[y, at], XS, (i // C, i % C), 1)

    def z_copy(i):
        k, cc = i // C, i % C
        return send(gsend.at[k], xrecv.at[y], XS, (k, cc), 1)

    def g_copy(i):
        return send(gacc.at[i], grecv.at[i], MS + i, (partner(i), c))

    def h_copy(cc):
        return send(gacc.at[steps], grecv.at[steps], GS, (r, cc))

    def each(first_index, last_index, act, skip=None):
        def body(i, carry):
            if skip is None:
                act(i)
            else:
                @pl.when(i != skip)
                def _():
                    act(i)
            return carry

        lax.fori_loop(first_index, last_index, body, 0)

    def store(hi, lo, index, value):
        high, low = split(value)
        hi[index] = high
        lo[index] = low

    def wide(value):
        return jnp.concatenate([value[:nvec], value[nvec:]], 1)

    def start_sends():
        @when(side & (t == 1))
        def _():
            m_near().start()

        @when(far & jnp.logical_not(parted))
        def _():
            m_far().start()

        @when(parted)
        def _():
            for i in range(2):
                m_part(1 - i).start()

        @when(main & (t == 1) & (z == 1))
        def _():
            u_copy(0, 1).start()

        @when(aid)
        def _():
            u_copy(1, 1).start()

    def put_pairs(ref, out):
        for i in range(half):
            for k in range(2):
                ref[i, k] = out[:, (k * half + i) * rows:(k * half + i + 1) * rows]

    def times(values, high, low):
        left = jnp.concatenate([complex_left(v, nvec) for v in values], 1)
        return product(left, high, low, dot_nn)

    def turn(hi, lo, row, col, value):
        high, low = split(value.T)
        at = (slice(row, row + value.shape[1]), slice(col, col + value.shape[0]))
        hi[at] = high
        lo[at] = low

    def turn_pair(hi, lo, row, col, ref):
        for i in range(2):
            turn(hi, lo, row + i * ref.shape[2], col, ref[i])

    def turn_parts(row, ref):
        for i in range(2):
            for h in range(2):
                turn(up_hi, up_lo, row + i * rows, h * gap, ref[i, h * width:(h + 1) * width])

    def first_loads():
        at = pl.ds(0, tile + nvec)
        pltpu.make_async_copy(f_first.at[:, at], f_first.at[:, at], load_sem.at[0]).wait()

    span = 2 * rows
    gap = width + rows
    broad = 2 * width

    @when(main & (t == 0))
    def _():
        first_loads()
        store(low_hi, low_lo, ..., pair(low_in))
        left = complex_left([pair(kry_in, 0)], nvec)
        put_pairs(asend, product(left, low_hi[...], low_lo[...], dot_nt))

    arrive()

    @when(main & (t == 0))
    def _():
        each(0, jnp.where(hub, half - 1, half), lambda i: a_copy(i).start())

    start_sends()

    @when(main & (t == 0))
    def _():
        @when(hub)
        def _():
            arecv[p] = asend[y]
            take(recv_sem.at[AD], (share - 1) * 2 * block)
            parts = [arecv[q] for q in range(share)]
            ybuf[...] = (parts[0] + parts[1]) + (parts[2] + parts[3])
            pl.semaphore_wait(next_sem, 1)
            for i in range(share):
                y_copy(i).start()

        @when(hub)
        def _():
            v_copy(0).start()

        @when(jnp.logical_not(hub))
        def _():
            t_copy().start()
            u_copy(0, 2).start()
            take(recv_sem.at[MS], fac // 2)
            m_relay().start()

    load(3, basis, bas_in).wait()

    def prepare_basis():
        top = pair(bas_in)
        bottom = jnp.concatenate([-bas_in[1], bas_in[0]], 1)
        store(bas_hi, bas_lo, ..., jnp.concatenate([top, bottom], 0))
        return top

    def prepare_end(top):
        gram = jnp.concatenate([top, jnp.concatenate([-top[:, nb:], top[:, :nb]], 1)], 0)
        row_id = lax.broadcasted_iota(jnp.int32, gram.shape, 0)
        col_id = lax.broadcasted_iota(jnp.int32, gram.shape, 1)
        twice = jnp.where(row_id == col_id, 2.0, 0.0) - gram
        spread = product(twice, bas_hi[...], bas_lo[...], dot_nn)
        store(end_hi, end_lo, ..., jnp.concatenate([twice, spread], 1))

    def end_from_side():
        prepare_basis()
        take(recv_sem.at[GS], gram)
        prepare_end(grecv[steps])

    @when(side)
    def _():
        gacc[0] = product(prepare_basis(), bas_hi[...], bas_lo[...], dot_nt)
        for i in range(steps):
            g_copy(i).start()
            take(recv_sem.at[MS + i], gram)
            gacc[i + 1] = gacc[i] + grecv[i]
        each(1, C, lambda cc: h_copy(cc).start())
        prepare_end(gacc[steps])

    @when(c > lead)
    def _():
        end_from_side()

    @when(main & (t == 1))
    def _():
        first_loads()
        load(1, factor, fac_in).wait()
        turn_pair(turn_hi, turn_lo, 0, 0, low_in)
        turn_pair(fac_hi, fac_lo, broad, 0, fac_in)
        take(recv_sem.at[MS], fac)
        turn_pair(fac_hi, fac_lo, 0, 0, f_recv.at[0, 0])

        @when(hub)
        def _():
            load(2, upper, up_in).wait()
            turn_pair(up_hi, up_lo, 0, 0, up_in)

        take(recv_sem.at[YE], half * 2 * block)
        parts = [[yrecv[i, h] for i in range(half)] for h in range(per)]
        g = pair(kry_in, 0) - times(parts, fac_hi[:, :rows], fac_lo[:, :rows])
        ybuf[0] = g

        @when(main)
        def _():
            put_pairs(dsend, times([[ybuf[0]]], turn_hi[...], turn_lo[...]))

        each(0, jnp.where(hub, half - 1, half), lambda i: d_copy(i).start())
        o_copy().start()

        @when(hub)
        def _():
            drecv[p] = dsend[y]
            take(recv_sem.at[US], ups)
            turn_pair(up_hi, up_lo, span, 0, up_recv)

            take(recv_sem.at[AD], (share - 1) * 2 * block)
            parts = [drecv[q] for q in range(share)]
            total = (parts[0] + parts[1]) + (parts[2] + parts[3])
            out = times([[total[0]], [total[1]]], up_hi[:, :tile], up_lo[:, :tile])
            for h in range(per):
                for k in range(half):
                    esend[h * half + k] = out[:, (h * half + k) * rows:(h * half + k + 1) * rows]
                for k in range(half):
                    e_copy(h * half + k).start()
            pl.semaphore_wait(all_sem, 1)
            each(0, share * C, lambda i: x_copy(i).start(), p * C + c)
            xrecv[y, :block] = esend[p]

        end_from_side()

    @when(main & (t == 0))
    def _():
        @when(hub)
        def _():
            load(2, upper, up_in).wait()
            turn_parts(span, up_in)
            gather[p] = bas_in[...]
            take(recv_sem.at[TS], bas)
            v_copy(1).start()
            take(recv_sem.at[VS], 2 * bas)
            stacked = jnp.concatenate(
                [jnp.concatenate([gather[q, i] for q in range(share)], 1) for i in range(2)], 0
            )
            take(recv_sem.at[US], ups)
            turn_parts(0, up_recv)
            for k in range(2):
                at = slice(k * span, (k + 1) * span)
                high = jnp.concatenate([up_hi[at, :width], up_hi[at, gap:]], 1)
                low = jnp.concatenate([up_lo[at, :width], up_lo[at, gap:]], 1)
                out = product(stacked, high, low, dot_nt)
                turn(up_hi, up_lo, k * span, width, out[:nb, :rows] + out[nb:, rows:])
                turn(up_hi, up_lo, k * span + rows, width, out[:nb, rows:] - out[nb:, :rows])
            take(recv_sem.at[OS], 2 * bas)
            empty = jnp.zeros((nb, rows), F32)
            for h in range(per):
                one = gather_one[h]
                for i in range(2):
                    own = (1 - 2 * i) * one[i]
                    own = jnp.where(y == 0, jnp.concatenate([own, empty], 1), jnp.concatenate([empty, own], 1))
                    turn(fac_hi, fac_lo, h * broad + i * width, span, own)
            pl.semaphore_wait(all_sem, 1)
            for h in range(per):
                for k in range(2):
                    take(recv_sem.at[MS + k * per + h], fac)
                    turn_pair(fac_hi, fac_lo, h * broad, k * rows, f_recv.at[k, h])
            out = 0.0
            for h in range(per):
                take(recv_sem.at[YE + h], half * half * block)
                x = [erecv[0, h * half + k] + erecv[1, h * half + k] for k in range(half)]
                at = slice(h * broad, (h + 1) * broad)
                out = out + times([x], fac_hi[at], fac_lo[at])
            for k in range(2):
                yrecv[0, k] = ybuf[k] - out[:, k * rows:(k + 1) * rows]
            gsend[0, :, :nb] = jnp.concatenate([out[:, span:], out[:nvec, span:]], 0)

            @when(main)
            def _():
                w = [[yrecv[0, 0]], [yrecv[0, 1]]]
                more = times(w, up_hi[:, :width + nb], up_lo[:, :width + nb])
                first = wide(gsend[0, :block, :nb] + more[:, width:])
                for k in range(share):
                    if k == half:
                        more = times(w, up_hi[:, gap:], up_lo[:, gap:])
                    gsend[k, block:] = first
                    gsend[k, :block] = more[:, (k % half) * rows:(k % half + 1) * rows]
                    for cc in (range(C) if k != 1 else range(C - 1, -1, -1)):
                        if k < half or cc != lead:
                            z_copy(k * C + cc).start()
                        else:
                            @when(p != k)
                            def _():
                                z_copy(k * C + cc).start()

            each(share * C, R * C, lambda i: f_copy(i).start())
            xrecv[y] = gsend[p]
            end_from_side()

        @when(jnp.logical_not(hub))
        def _():
            end_from_side()

    @when(jnp.logical_not(hub))
    def _():
        take(recv_sem.at[XS], 2 * wave)

    for i in range(2):
        @when(hub & (t == i))
        def _():
            take(recv_sem.at[XS], wave + i * nvec)

    total = xrecv[0] + xrecv[1]
    ends = product(total[block:], end_hi[...], end_lo[...], dot_nn)
    coefficients[0] = ends[:, :nb]
    coefficients[1] = ends[:, nb:2 * nb]
    projected[0] = total[:nvec] - ends[:, 2 * nb:2 * nb + rows]
    projected[1] = total[nvec:block] - ends[:, 2 * nb + rows:]

    def sent(cond, count, way=0):
        @when(cond)
        def _():
            take(send_sem.at[way], count)

    others = share * C - 1
    sent(main & (t == 0) & (z == 0), half * 2 * block + bas + ups + fac // 2)
    sent(hub & (t == 0), (half - 1) * 2 * block + 2 * bas + share * 2 * block)
    sent(hub & (t == 0), others * wave + share * C * nvec, 1)
    sent(main & (t == 1) & (z == 1), half * 2 * block + bas + ups // 2)
    sent(hub & (t == 1), (half - 1) * 2 * block + bas + half * share * block + others * block)
    sent(side & (t == 0), (steps + C - 1) * gram)
    sent(side & (t == 1), (steps + C - 1) * gram + fac)
    sent(far, fac)
    sent(aid, ups // 2)


def hub_call(R, C, factor, lower, upper, krylov, basis):
    tile, rows = lower.shape[1], lower.shape[2]
    width = factor.shape[2]
    nvec, nb = krylov.shape[1], basis.shape[1]
    share, per = tile // rows, tile // width
    half = share // 2
    steps = R.bit_length() - 1
    dma = pltpu.SemaphoreType.DMA
    vmem = pl.BlockSpec(memory_space=pltpu.VMEM)
    block = (2 * nvec, rows)
    f32 = lambda *shape: pltpu.VMEM(shape, F32)
    bf16 = lambda *shape: [pltpu.VMEM(shape, BF16)] * 2
    return pl.pallas_call(
        functools.partial(hub_kernel, R, C),
        out_shape=(pltpu.VMEM(krylov.shape, F32), pltpu.VMEM((2, nvec, nb), F32)),
        in_specs=[pl.BlockSpec(memory_space=pl.ANY)] * 5,
        out_specs=(vmem, vmem),
        scratch_shapes=[
            f32(*factor.shape), f32(2, tile + nvec, rows), f32(*upper.shape), f32(*basis.shape),
            f32(*upper.shape), f32(2, per, *factor.shape),
            *bf16(tile, 2 * rows), *bf16(4 * rows, tile + rows), *bf16(2 * tile, 2 * rows + nb), *bf16(2 * rows, tile),
            *bf16(2 * nb, 2 * rows), *bf16(2 * nb, 2 * nb + 2 * rows),
            f32(share, *basis.shape), f32(2, *basis.shape),
            f32(half, 2, *block), f32(share, 2, *block), f32(2, *block), f32(half, 2, *block),
            f32(half, 2, *block), f32(share, 2, *block), f32(share, *block), f32(2, share, *block),
            f32(share, 3 * nvec, rows), f32(half, 3 * nvec, rows),
            f32(steps + 1, nb, 2 * nb), f32(steps + 1, nb, 2 * nb),
            dma((4,)), dma((2,)), dma((9 + max(steps, 2 * per),)),
            pltpu.SemaphoreType.REGULAR, pltpu.SemaphoreType.REGULAR,
        ],
        compiler_params=pltpu.CompilerParams(collective_id=0, has_side_effects=True),
        name="krylov_hubs",
    )(factor, lower, upper, krylov, basis)


def finish(projected, turned, projected_out, turned_out, sems):
    copies = [
        pltpu.make_async_copy(projected, projected_out, sems.at[0]),
        pltpu.make_async_copy(turned, turned_out, sems.at[1]),
    ]
    for copy in copies:
        copy.start()
    for copy in copies:
        copy.wait()


def general_call(R, C, factor, lower, upper, krylov, basis):
    tile, rows = lower.shape[1], lower.shape[2]
    width = factor.shape[2]
    nvec, nb = krylov.shape[1], basis.shape[1]
    share, per, pieces = tile // rows, tile // width, width // rows
    steps = R.bit_length() - 1
    dma = pltpu.SemaphoreType.DMA
    vmem = pl.BlockSpec(memory_space=pltpu.VMEM)
    block = (2 * nvec, rows)
    return pl.pallas_call(
        functools.partial(kernel, R, C),
        out_shape=(
            jax.ShapeDtypeStruct(krylov.shape, F32),
            jax.ShapeDtypeStruct((2, nvec, nb), F32),
        ),
        in_specs=[vmem] * 5,
        out_specs=(vmem, vmem),
        scratch_shapes=[
            pltpu.VMEM((2, tile, 2 * rows), BF16),
            pltpu.VMEM((2, tile, 2 * rows), BF16),
            pltpu.VMEM((rows, 2 * width), BF16),
            pltpu.VMEM((rows, 2 * width), BF16),
            pltpu.VMEM((2 * nb, 2 * rows), BF16),
            pltpu.VMEM((2 * nb, 2 * rows), BF16),
            pltpu.VMEM((2 * nb, 2 * nb + 2 * rows), BF16),
            pltpu.VMEM((2 * nb, 2 * nb + 2 * rows), BF16),
            pltpu.VMEM((2 * nb, 2 * rows), BF16),
            pltpu.VMEM((2 * nb, 2 * rows), BF16),
            pltpu.VMEM((share, 2, nb, rows), F32),
            pltpu.VMEM((2, share) + block, F32),
            pltpu.VMEM((2, share) + block, F32),
            pltpu.VMEM(block, F32),
            pltpu.VMEM(block, F32),
            pltpu.VMEM((pieces,) + block, F32),
            pltpu.VMEM(block, F32),
            pltpu.VMEM((C,) + block, F32),
            pltpu.VMEM((nvec, 2 * nb), F32),
            pltpu.VMEM((R, nvec, 2 * nb), F32),
            pltpu.VMEM((steps + 1, nb, 2 * nb), F32),
            pltpu.VMEM((steps, nb, 2 * nb), F32),
            dma((2, share)),
            dma((2, share)),
            dma((R,)),
            dma((pieces,)),
            dma((C,)),
            dma((C,)),
            dma((C // per,)),
            dma((1,)),
            dma((R,)),
            dma((R,)),
            dma((steps,)),
            dma((steps,)),
            dma((share,)),
            dma((share,)),
            dma((C // per,)),
            dma((1,)),
            pltpu.SemaphoreType.REGULAR,
        ],
        compiler_params=pltpu.CompilerParams(collective_id=0, has_side_effects=True),
        name="krylov_step",
    )(factor, lower, upper, krylov, basis)


def local(R, C, factor, lower, upper, krylov, basis):
    tile, rows = lower.shape[1], lower.shape[2]
    share, per = tile // rows, tile // factor.shape[2]
    vmem = pl.BlockSpec(memory_space=pltpu.VMEM)
    paired = R == 2 * share and C == 2 * per and share == 4 and per == 2
    call = hub_call if paired else general_call
    projected, turned = call(R, C, factor, lower, upper, krylov, basis)
    if paired:
        projected, turned = [pltpu.with_memory_space_constraint(x, pltpu.VMEM) for x in (projected, turned)]
    projected, turned = pl.pallas_call(
        finish,
        out_shape=(jax.ShapeDtypeStruct(projected.shape, F32), jax.ShapeDtypeStruct(turned.shape, F32)),
        in_specs=[vmem] * 2,
        out_specs=[pl.BlockSpec(memory_space=pl.ANY)] * 2,
        scratch_shapes=[pltpu.SemaphoreType.DMA((2,))],
        name="finish",
    )(projected, turned)
    return projected, turned.transpose(0, 2, 1)


def solution(mesh):
    in_specs = (
        P(None, "row", "col"),
        P(None, None, "row"),
        P(None, None, "row"),
        P(None, None, "row"),
        P(None, None, "row"),
    )
    out_specs = (P(None, None, "row"), P())
    body = functools.partial(local, mesh.shape["row"], mesh.shape["col"])
    return jax.shard_map(body, mesh=mesh, in_specs=in_specs, out_specs=out_specs, check_vma=False)
```

```python
import functools

import jax
import jax.numpy as jnp
from jax import lax
from jax.experimental import pallas as pl
from jax.experimental.pallas import tpu as pltpu
from jax.sharding import PartitionSpec as P

MESH = pl.DeviceIdType.MESH
F32 = jnp.float32
BF16 = jnp.bfloat16


def split(value):
    high = value.astype(BF16)
    low = (value - high.astype(F32)).astype(BF16)
    return high, low


def dot_nt(left, right):
    return lax.dot_general(left, right, (((1,), (1,)), ((), ())), preferred_element_type=F32)


def dot_nn(left, right):
    return lax.dot_general(left, right, (((1,), (0,)), ((), ())), preferred_element_type=F32)


def product(left, high, low, dot):
    rows = left.shape[0]
    left_high, left_low = split(left)
    both = dot(jnp.concatenate([left_high, left_low], 0), high)
    return both[:rows] + (both[rows:] + dot(left_high, low))


def complex_left(pieces, nvec):
    re = [x[:nvec] for x in pieces]
    im = [x[nvec:] for x in pieces]
    top = jnp.concatenate(re + [-x for x in im], 1)
    bottom = jnp.concatenate(im + re, 1)
    return jnp.concatenate([top, bottom], 0)


def kernel(
    R, C, factor, lower, upper, krylov, basis, projected, coefficients,
    inv_hi, inv_lo, fac_hi, fac_lo, bas_hi, bas_lo,
    end_hi, end_lo, lead_hi, lead_lo, gather,
    psend, precv, ybuf, xbuf, bcast, vbuf, vrecv, fsend, frecv, gacc, grecv,
    psend_sem, precv_sem, bsend_sem, brecv_sem, vsend_sem, vrecv_sem, xsend_sem, xrecv_sem,
    fsend_sem, frecv_sem, gsend_sem, grecv_sem, tsend_sem, trecv_sem, ysend_sem, yrecv_sem,
    ready_sem,
):
    tile, rows = lower.shape[1], lower.shape[2]
    width = factor.shape[2]
    nvec = krylov.shape[1]
    nb = basis.shape[1]
    share = tile // rows
    per = tile // width
    pieces = width // rows
    steps = R.bit_length() - 1
    r = lax.axis_index("row")
    c = lax.axis_index("col")
    t, p = r // share, r % share
    j, h = c // per, c % per
    solver = j == t

    barrier = pltpu.get_barrier_semaphore()

    def greet_mate(i, carry):
        pl.semaphore_signal(barrier, inc=1, device_id=(t * share + (p + 1 + i) % share, c), device_id_type=MESH)
        return carry

    def greet_tile(i, carry):
        pl.semaphore_signal(barrier, inc=1, device_id=((r + (1 + i) * share) % R, c), device_id_type=MESH)
        return carry

    def greet_col(i, carry):
        pl.semaphore_signal(barrier, inc=1, device_id=(r, (c + 1 + i) % C), device_id_type=MESH)
        return carry

    lax.fori_loop(0, share - 1, greet_mate, 0)
    lax.fori_loop(0, R // share - 1, greet_tile, 0)
    lax.fori_loop(0, C - 1, greet_col, 0)

    def prepare(ref, slot):
        high, low = split(jnp.concatenate([ref[0], ref[1]], 1))
        inv_hi[slot] = high
        inv_lo[slot] = low

    @pl.when(solver)
    def _():
        prepare(lower, 0)

    @pl.when(jnp.logical_not(solver))
    def _():
        high, low = split(jnp.concatenate([factor[0], factor[1]], 1))
        fac_hi[...] = high
        fac_lo[...] = low

    def prepare_basis():
        top = jnp.concatenate([basis[0], basis[1]], 1)
        bottom = jnp.concatenate([-basis[1], basis[0]], 1)
        high, low = split(jnp.concatenate([top, bottom], 0))
        bas_hi[...] = high
        bas_lo[...] = low
        gacc[0] = product(top, high, low, dot_nt)

    def remote(src, dst, send, recv, dest):
        return pltpu.make_async_remote_copy(
            src_ref=src, dst_ref=dst, send_sem=send, recv_sem=recv, device_id=dest, device_id_type=MESH
        )

    def each(first_index, last_index, act):
        def body(i, carry):
            act(i)
            return carry

        lax.fori_loop(first_index, last_index, body, 0)

    def gram_copy(i):
        other = r + (1 << i) * (1 - 2 * ((r // (1 << i)) % 2))
        return remote(gacc.at[i], grecv.at[i], gsend_sem.at[i], grecv_sem.at[i], (other, c))

    def gram_all():
        for i in range(steps):
            copy = gram_copy(i)
            copy.start()
            copy.wait_recv()
            gacc[i + 1] = gacc[i] + grecv[i]
        top = gacc[steps]
        gram = jnp.concatenate([top, jnp.concatenate([-top[:, nb:], top[:, :nb]], 1)], 0)
        row_id = lax.broadcasted_iota(jnp.int32, gram.shape, 0)
        col_id = lax.broadcasted_iota(jnp.int32, gram.shape, 1)
        twice = jnp.where(row_id == col_id, 2.0, 0.0) - gram
        spread = product(twice, bas_hi[...], bas_lo[...], dot_nn)
        high, low = split(jnp.concatenate([twice, spread], 1))
        end_hi[...] = high
        end_lo[...] = low

    def t_copy(d):
        q = (p + d) % share
        return remote(basis, gather.at[p], tsend_sem.at[d], trecv_sem.at[p], (t * share + q, c))

    def lead_send():
        for d in range(1, share):
            t_copy(d).start()
        gather[p] = basis[...]

    def lead_all():
        for d in range(1, share):
            q = (p + d) % share
            remote(basis, gather.at[q], tsend_sem.at[d], trecv_sem.at[q], (t * share + q, c)).wait_recv()
        left = jnp.concatenate(
            [jnp.concatenate([gather[q, i] for q in range(share)], 1) for i in range(2)], 0
        )
        out = product(left, inv_hi[1], inv_lo[1], dot_nn)
        one = out[:nb, :rows] + out[nb:, rows:]
        two = out[nb:, :rows] - out[:nb, rows:]
        whole = jnp.concatenate([jnp.concatenate([one, two], 1), jnp.concatenate([-two, one], 1)], 0)
        high, low = split(whole)
        lead_hi[...] = high
        lead_lo[...] = low

    def side_work():
        gram_all()

        @pl.when(t == 0)
        def _():
            lead_send()
            lead_all()

    def part_copy(sweep, d):
        q = (p + d) % share
        return remote(
            psend.at[sweep, q], precv.at[sweep, p], psend_sem.at[sweep, q], precv_sem.at[sweep, p], (t * share + q, c)
        )

    def part_arrival(sweep, d):
        q = (p + d) % share
        return remote(
            psend.at[sweep, q], precv.at[sweep, q], psend_sem.at[sweep, q], precv_sem.at[sweep, q], (t * share + q, c)
        ), q

    def v_copy(cc):
        return remote(vbuf, vrecv.at[c], vsend_sem.at[cc], vrecv_sem.at[c], (r, cc))

    def v_each(act):
        @pl.when(t > 0)
        def _():
            for hh in range(per):
                act(v_copy(t * per + hh))

        @pl.when(t == 0)
        def _():
            each(1, C, lambda d: act(v_copy((c + d) % C)))

    def v_sum(first_col, last_col, value):
        def body(cc, total):
            @pl.when(cc != c)
            def _():
                remote(vbuf, vrecv.at[cc], vsend_sem.at[0], vrecv_sem.at[cc], (r, cc)).wait_recv()

            return total - vrecv[cc]

        return lax.fori_loop(first_col, last_col, body, value)

    def f_copy(d):
        return remote(fsend, frecv.at[r], fsend_sem.at[d], frecv_sem.at[r], ((r + d) % R, c))

    def send_first(value, high, low):
        wide_value = jnp.concatenate([value[:nvec], value[nvec:]], 1)
        fsend[...] = product(wide_value, high, low, dot_nt)
        each(1, R, lambda d: f_copy(d).start())

    def multiply(sweep, g):
        out = product(complex_left([g], nvec), inv_hi[sweep], inv_lo[sweep], dot_nt)
        for q in range(share):
            psend[sweep, q] = out[:, q * rows:(q + 1) * rows]

    def solve(sweep, g):
        multiply(sweep, g)
        return exchange(sweep)

    def exchange(sweep):
        for d in range(1, share):
            part_copy(sweep, d).start()
        total = psend[sweep, p]
        for d in range(1, share):
            arrival, q = part_arrival(sweep, d)
            arrival.wait_recv()
            total = total + precv[sweep, q]
        return total

    def b_copy(buf, rr):
        return remote(buf, bcast.at[p % pieces], bsend_sem.at[rr], brecv_sem.at[p % pieces], (rr, c))

    def x_copy(tt):
        cc = tt * per + h
        return remote(xbuf, xbuf, xsend_sem.at[tt], xrecv_sem.at[0], (r, cc))

    def y_copy(tt):
        return remote(ybuf, ybuf, ysend_sem.at[tt], yrecv_sem.at[0], (r, tt * per + h))

    speaks = p // pieces == h

    @pl.when(solver != (t == 0))
    def _():
        prepare(upper, 1)

    @pl.when(j > 0)
    def _():
        prepare_basis()

    @pl.when(jnp.logical_and(solver, t == 0))
    def _():
        multiply(0, jnp.concatenate([krylov[0], krylov[1]], 0))

    pl.semaphore_wait(barrier, share - 1 + R // share - 1 + C - 1)
    for d in range(1, share):
        pl.semaphore_signal(
            ready_sem, inc=1, device_id=(t * share + (p + d) % share, c), device_id_type=MESH
        )

    @pl.when(j > 0)
    def _():
        side_work()

    @pl.when(solver)
    def _():
        @pl.when(t > 0)
        def _():
            b = jnp.concatenate([krylov[0], krylov[1]], 0)
            multiply(0, v_sum(0, t * per, b))

        ybuf[...] = exchange(0)
        pl.semaphore_wait(ready_sem, share - 1)

        @pl.when(speaks)
        def _():
            each((t + 1) * share, R, lambda rr: b_copy(ybuf, rr).start())

        @pl.when(t == 0)
        def _():
            each(1, C // per, lambda tt: y_copy(tt).start())
            prepare(upper, 1)

    @pl.when(jnp.logical_not(solver))
    def _():
        pl.semaphore_wait(ready_sem, share - 1)
        got = []
        for i in range(pieces):
            remote(ybuf, bcast.at[i], bsend_sem.at[0], brecv_sem.at[i], (r, t * per)).wait_recv()
            got.append(bcast[i])
        value = product(complex_left(got, nvec), fac_hi[...], fac_lo[...], dot_nt)
        vbuf[...] = value
        v_each(lambda copy: copy.start())
        vrecv[c] = value

    @pl.when(j == 0)
    def _():
        prepare_basis()
        side_work()

    @pl.when(t == 0)
    def _():
        @pl.when(jnp.logical_not(solver))
        def _():
            remote(ybuf, ybuf, ysend_sem.at[0], yrecv_sem.at[0], (r, h)).wait_recv()

        g = v_sum(per, C, ybuf[...])
        send_first(g, lead_hi[...], lead_lo[...])
        xbuf[...] = solve(1, g)

    @pl.when(t > 0)
    def _():
        @pl.when(solver)
        def _():
            xbuf[...] = solve(1, v_sum((t + 1) * per, C, ybuf[...]))

            @pl.when(speaks)
            def _():
                each(0, t * share, lambda rr: b_copy(xbuf, rr).start())

            each(0, t, lambda tt: x_copy(tt).start())
            each(t + 1, C // per, lambda tt: x_copy(tt).start())

        @pl.when(jnp.logical_not(solver))
        def _():
            remote(ybuf, xbuf, xsend_sem.at[0], xrecv_sem.at[0], (r, t * per)).wait_recv()

        send_first(xbuf[...], bas_hi[...], bas_lo[...])

    frecv[r] = fsend[...]

    def f_wait(d):
        q = (r + d) % R
        remote(fsend, frecv.at[q], fsend_sem.at[d], frecv_sem.at[q], (q, c)).wait_recv()

    each(1, R, f_wait)
    first = frecv[0]
    for i in range(1, R):
        first = first + frecv[i]
    ends = product(first, end_hi[...], end_lo[...], dot_nn)
    coefficients[0] = ends[:, :nb]
    coefficients[1] = ends[:, nb:2 * nb]
    projected[0] = xbuf[:nvec] - ends[:, 2 * nb:2 * nb + rows]
    projected[1] = xbuf[nvec:] - ends[:, 2 * nb + rows:]

    each(1, R, lambda d: f_copy(d).wait_send())
    for i in range(steps):
        gram_copy(i).wait_send()

    def parts_sent(sweep):
        for d in range(1, share):
            part_copy(sweep, d).wait_send()

    @pl.when(t == 0)
    def _():
        parts_sent(1)
        for d in range(1, share):
            t_copy(d).wait_send()

    @pl.when(solver)
    def _():
        parts_sent(0)

        @pl.when(speaks)
        def _():
            each((t + 1) * share, R, lambda rr: b_copy(ybuf, rr).wait_send())

        @pl.when(t == 0)
        def _():
            each(1, C // per, lambda tt: y_copy(tt).wait_send())

        @pl.when(t > 0)
        def _():
            parts_sent(1)

            @pl.when(speaks)
            def _():
                each(0, t * share, lambda rr: b_copy(xbuf, rr).wait_send())

            each(0, t, lambda tt: x_copy(tt).wait_send())
            each(t + 1, C // per, lambda tt: x_copy(tt).wait_send())

    @pl.when(jnp.logical_not(solver))
    def _():
        v_each(lambda copy: copy.wait_send())


def hub_kernel(
    R, C, factor, lower, upper, krylov, basis, projected, coefficients,
    fac_in, f_first, up_in, bas_in, up_recv, f_recv,
    low_hi, low_lo, up_hi, up_lo, fac_hi, fac_lo, turn_hi, turn_lo,
    bas_hi, bas_lo, end_hi, end_lo, gather, gather_one,
    asend, arecv, ybuf, yrecv, dsend, drecv, esend, erecv, gsend, xrecv, gacc, grecv,
    load_sem, send_sem, recv_sem, next_sem, all_sem,
):
    tile, rows = lower.shape[1], lower.shape[2]
    width = factor.shape[2]
    nvec = krylov.shape[1]
    nb = basis.shape[1]
    share = tile // rows
    per = tile // width
    half = share // 2
    steps = R.bit_length() - 1
    r = lax.axis_index("row")
    c = lax.axis_index("col")
    me = r * C + c
    t, p = r // share, r % share
    y, z = p % half, p // half
    lead = per - 1
    main = c == lead
    hub = main & (z == 1 - t)
    side = c == 0

    def partner(i):
        return r + (1 << i) * (1 - 2 * ((r // (1 << i)) % 2))

    def remote(src, dst, send, recv, dest):
        return pltpu.make_async_remote_copy(
            src_ref=src, dst_ref=dst, send_sem=send, recv_sem=recv, device_id=dest, device_id_type=MESH
        )

    low_in, kry_in = f_first.at[:, pl.ds(0, tile)], f_first.at[:, pl.ds(tile, nvec)]

    def load(i, src, dst):
        return pltpu.make_async_copy(src, dst, load_sem.at[i])

    barrier = pltpu.get_barrier_semaphore()
    guide = (c == per) & (t == 1) & (z == 0)
    far = (c >= per) & (t == 0)
    parted = far & (z == 0) & (c == per)
    aid = (c == C - 1) & (t == 1) & (z == 1)

    def greet(rr, cc):
        pl.semaphore_signal(barrier, inc=1, device_id=(rr, cc), device_id_type=MESH)

    @pl.when(main)
    def _():
        @pl.when(hub)
        def _():
            for d in range(1, share):
                greet(t * share + (p + d) % share, c)

        greet(r, 0)

        @pl.when(t == 1)
        def _():
            for i in range(half):
                greet(half + i, 0)

        @pl.when(hub & (t == 0))
        def _():
            for cc in range(per, C):
                greet(r, cc)
                greet(y, cc)

        @pl.when(hub & (t == 1))
        def _():
            greet(share + half + y, C - 1)

        @pl.when((t == 0) & (z == 0))
        def _():
            greet(r, per)

    @pl.when(side)
    def _():
        for i in range(steps):
            greet(partner(i), c)

    @pl.when(c >= per)
    def _():
        greet(r, 0)

    for i in range(half):
        @pl.when(jnp.logical_not(guide & (y == i)))
        def _():
            greet(share + i, per)

    @pl.when(main)
    def _():
        load(0, lower, low_in).start()
        load(0, krylov, kry_in).start()

        @pl.when(t == 1)
        def _():
            load(1, factor, fac_in).start()

        @pl.when(hub)
        def _():
            load(2, upper, up_in).start()

    load(3, basis, bas_in).start()

    def arrive():
        count = jnp.where(main, jnp.where(hub, half - 1, half), jnp.where(
            side, steps + 1 + C - per + jnp.where((t == 0) & (z == 1), share, 0),
            jnp.where(guide, R * C - 1, jnp.where(parted, 2, 1)),
        ))
        @pl.when(main | side | far | guide | aid)
        def _():
            pl.semaphore_wait(barrier, count)

        @pl.when(side & (t == 0) & (z == 1))
        def _():
            pl.semaphore_signal(next_sem, inc=1, device_id=(r, lead), device_id_type=MESH)

        @pl.when(guide)
        def _():
            for i in range(2):
                pl.semaphore_signal(all_sem, inc=1, device_id=(half * (i + 1) + y, lead), device_id_type=MESH)

    def when(cond):
        return pl.when(cond)

    def pair(ref, axis=1):
        return jnp.concatenate([ref[0], ref[1]], axis)

    block, wave, bas, fac, ups, gram = 2 * nvec, 3 * nvec, 2 * nb, 2 * width, 2 * tile, 2 * nb * nb // rows
    AD, US, XS, YE, ES, TS, VS, OS, GS = range(9)
    MS = GS + 1

    def take(sem, count):
        if count > ups:
            ref = f_recv.at[:, :, :, pl.ds(0, count * rows // (4 * per * width))]
        else:
            ref = up_recv.at[:, pl.ds(0, count // 2)]
        remote(ref, ref, send_sem.at[0], sem, ((r + 1) % R, c)).wait_recv()

    def send(src, dst, recv, dest, way=0):
        return remote(src, dst, send_sem.at[way], recv_sem.at[recv], dest)

    def a_copy(i):
        i = (y + 1 + i) % half
        return send(asend.at[i], arecv.at[p], AD, (half + i, c))

    def y_copy(i):
        i = (1 - i // half) * half + (y + 1 + i) % half
        return send(ybuf, yrecv.at[y], YE, (share + i, c))

    def u_copy(first, count):
        at = pl.ds(first * (tile // 2), count * (tile // 2))
        return send(upper.at[:, at], up_recv.at[:, at], US, (t * share + (1 - z) * half + y, lead))

    def m_near():
        return send(factor, f_recv.at[0, 0], MS, (r, lead))

    def m_far():
        return send(factor, f_recv.at[z, c % per], MS + z * per + c % per, (half + y, lead))

    def m_part(i):
        return send(factor.at[i], f_recv.at[0, 0, i], MS, (half * (1 - i) + y, lead))

    def m_relay():
        return send(f_recv.at[0, 0, 1], f_recv.at[0, 0, 1], MS, (half + y, lead))

    def t_copy():
        return send(basis, gather.at[p], TS, (half + y, lead))

    def v_copy(i):
        if i == 0:
            return send(basis, gather.at[p], VS, (half + (y + 1) % half, lead))
        return send(gather.at[y], gather.at[y], VS, (half + (y + 1) % half, lead))

    def o_copy():
        return send(basis, gather_one.at[z], OS, (half + y, lead))

    def d_copy(i):
        i = (y + 1 + i) % half
        return send(dsend.at[i], drecv.at[p], AD, (share + i, c))

    def e_copy(i):
        h, k = i // half, (y + 1 + i) % half
        at = pl.ds(h * half, half)
        return send(esend.at[at], erecv.at[y, at], YE + h, (half + k, c))

    def x_copy(i):
        k, cc = i // C, i % C
        return send(esend.at[k], xrecv.at[y, pl.ds(0, block)], XS, (t * share + k, cc))

    def f_copy(i):
        at = pl.ds(block, nvec)
        return send(gsend.at[0, at], xrecv.at[y, at], XS, (i // C, i % C), 1)

    def z_copy(i):
        k, cc = i // C, i % C
        return send(gsend.at[k], xrecv.at[y], XS, (k, cc), 1)

    def g_copy(i):
        return send(gacc.at[i], grecv.at[i], MS + i, (partner(i), c))

    def h_copy(cc):
        return send(gacc.at[steps], grecv.at[steps], GS, (r, cc))

    def each(first_index, last_index, act, skip=None):
        def body(i, carry):
            if skip is None:
                act(i)
            else:
                @pl.when(i != skip)
                def _():
                    act(i)
            return carry

        lax.fori_loop(first_index, last_index, body, 0)

    def store(hi, lo, index, value):
        high, low = split(value)
        hi[index] = high
        lo[index] = low

    def wide(value):
        return jnp.concatenate([value[:nvec], value[nvec:]], 1)

    def start_sends():
        @when(side & (t == 1))
        def _():
            m_near().start()

        @when(far & jnp.logical_not(parted))
        def _():
            m_far().start()

        @when(parted)
        def _():
            for i in range(2):
                m_part(1 - i).start()

        @when(main & (t == 1) & (z == 1))
        def _():
            u_copy(0, 1).start()

        @when(aid)
        def _():
            u_copy(1, 1).start()

    def put_pairs(ref, out):
        for i in range(half):
            for k in range(2):
                ref[i, k] = out[:, (k * half + i) * rows:(k * half + i + 1) * rows]

    def times(values, high, low):
        left = jnp.concatenate([complex_left(v, nvec) for v in values], 1)
        return product(left, high, low, dot_nn)

    def turn(hi, lo, row, col, value):
        high, low = split(value.T)
        at = (slice(row, row + value.shape[1]), slice(col, col + value.shape[0]))
        hi[at] = high
        lo[at] = low

    def turn_pair(hi, lo, row, col, ref):
        for i in range(2):
            turn(hi, lo, row + i * ref.shape[2], col, ref[i])

    def turn_parts(row, ref):
        for i in range(2):
            for h in range(2):
                turn(up_hi, up_lo, row + i * rows, h * gap, ref[i, h * width:(h + 1) * width])

    def first_loads():
        at = pl.ds(0, tile + nvec)
        pltpu.make_async_copy(f_first.at[:, at], f_first.at[:, at], load_sem.at[0]).wait()

    span = 2 * rows
    gap = width + rows
    broad = 2 * width

    @when(main & (t == 0))
    def _():
        first_loads()
        store(low_hi, low_lo, ..., pair(low_in))
        left = complex_left([pair(kry_in, 0)], nvec)
        put_pairs(asend, product(left, low_hi[...], low_lo[...], dot_nt))

    arrive()

    @when(main & (t == 0))
    def _():
        each(0, jnp.where(hub, half - 1, half), lambda i: a_copy(i).start())

    start_sends()

    @when(main & (t == 0))
    def _():
        @when(hub)
        def _():
            arecv[p] = asend[y]
            take(recv_sem.at[AD], (share - 1) * 2 * block)
            parts = [arecv[q] for q in range(share)]
            ybuf[...] = (parts[0] + parts[1]) + (parts[2] + parts[3])
            pl.semaphore_wait(next_sem, 1)
            for i in range(share):
                y_copy(i).start()

        @when(hub)
        def _():
            v_copy(0).start()

        @when(jnp.logical_not(hub))
        def _():
            t_copy().start()
            u_copy(0, 2).start()
            take(recv_sem.at[MS], fac // 2)
            m_relay().start()

    load(3, basis, bas_in).wait()

    def prepare_basis():
        top = pair(bas_in)
        bottom = jnp.concatenate([-bas_in[1], bas_in[0]], 1)
        store(bas_hi, bas_lo, ..., jnp.concatenate([top, bottom], 0))
        return top

    def prepare_end(top):
        gram = jnp.concatenate([top, jnp.concatenate([-top[:, nb:], top[:, :nb]], 1)], 0)
        row_id = lax.broadcasted_iota(jnp.int32, gram.shape, 0)
        col_id = lax.broadcasted_iota(jnp.int32, gram.shape, 1)
        twice = jnp.where(row_id == col_id, 2.0, 0.0) - gram
        spread = product(twice, bas_hi[...], bas_lo[...], dot_nn)
        store(end_hi, end_lo, ..., jnp.concatenate([twice, spread], 1))

    def end_from_side():
        prepare_basis()
        take(recv_sem.at[GS], gram)
        prepare_end(grecv[steps])

    @when(side)
    def _():
        gacc[0] = product(prepare_basis(), bas_hi[...], bas_lo[...], dot_nt)
        for i in range(steps):
            g_copy(i).start()
            take(recv_sem.at[MS + i], gram)
            gacc[i + 1] = gacc[i] + grecv[i]
        each(1, C, lambda cc: h_copy(cc).start())
        prepare_end(gacc[steps])

    @when(c > lead)
    def _():
        end_from_side()

    @when(main & (t == 1))
    def _():
        first_loads()
        load(1, factor, fac_in).wait()
        turn_pair(turn_hi, turn_lo, 0, 0, low_in)
        turn_pair(fac_hi, fac_lo, broad, 0, fac_in)
        take(recv_sem.at[MS], fac)
        turn_pair(fac_hi, fac_lo, 0, 0, f_recv.at[0, 0])

        @when(hub)
        def _():
            load(2, upper, up_in).wait()
            turn_pair(up_hi, up_lo, 0, 0, up_in)

        take(recv_sem.at[YE], half * 2 * block)
        parts = [[yrecv[i, h] for i in range(half)] for h in range(per)]
        g = pair(kry_in, 0) - times(parts, fac_hi[:, :rows], fac_lo[:, :rows])
        ybuf[0] = g

        @when(main)
        def _():
            out = times([[ybuf[0]]], turn_hi[...], turn_lo[...])
            cut = [out[:, k * rows:(k + 1) * rows] for k in range(share)]
            for j in range(half):
                for k in range(2):
                    dsend[(y + 1 + j) % half, k] = jnp.where(
                        y == 0, cut[k * half + (1 + j) % half], cut[k * half + j % half]
                    )
                if j < half - 1:
                    d_copy(j).start()
                else:
                    @when(jnp.logical_not(hub))
                    def _():
                        d_copy(j).start()

        o_copy().start()

        @when(hub)
        def _():
            drecv[p] = dsend[y]
            take(recv_sem.at[US], ups)
            turn_pair(up_hi, up_lo, span, 0, up_recv)

            take(recv_sem.at[AD], (share - 1) * 2 * block)
            parts = [drecv[q] for q in range(share)]
            total = (parts[0] + parts[1]) + (parts[2] + parts[3])
            out = times([[total[0]], [total[1]]], up_hi[:, :tile], up_lo[:, :tile])
            for h in range(per):
                for k in range(half):
                    esend[h * half + k] = out[:, (h * half + k) * rows:(h * half + k + 1) * rows]
                for k in range(half):
                    e_copy(h * half + k).start()
            pl.semaphore_wait(all_sem, 1)
            each(0, share * C, lambda i: x_copy(i).start(), p * C + c)
            xrecv[y, :block] = esend[p]

        end_from_side()

    @when(main & (t == 0))
    def _():
        @when(hub)
        def _():
            load(2, upper, up_in).wait()
            turn_parts(span, up_in)
            gather[p] = bas_in[...]
            take(recv_sem.at[TS], bas)
            v_copy(1).start()
            take(recv_sem.at[VS], 2 * bas)
            stacked = jnp.concatenate(
                [jnp.concatenate([gather[q, i] for q in range(share)], 1) for i in range(2)], 0
            )
            take(recv_sem.at[US], ups)
            turn_parts(0, up_recv)
            for k in range(2):
                at = slice(k * span, (k + 1) * span)
                high = jnp.concatenate([up_hi[at, :width], up_hi[at, gap:]], 1)
                low = jnp.concatenate([up_lo[at, :width], up_lo[at, gap:]], 1)
                out = product(stacked, high, low, dot_nt)
                turn(up_hi, up_lo, k * span, width, out[:nb, :rows] + out[nb:, rows:])
                turn(up_hi, up_lo, k * span + rows, width, out[:nb, rows:] - out[nb:, :rows])
            take(recv_sem.at[OS], 2 * bas)
            empty = jnp.zeros((nb, rows), F32)
            for h in range(per):
                one = gather_one[h]
                for i in range(2):
                    own = (1 - 2 * i) * one[i]
                    own = jnp.where(y == 0, jnp.concatenate([own, empty], 1), jnp.concatenate([empty, own], 1))
                    turn(fac_hi, fac_lo, h * broad + i * width, span, own)
            pl.semaphore_wait(all_sem, 1)
            for h in range(per):
                for k in range(2):
                    take(recv_sem.at[MS + k * per + h], fac)
                    turn_pair(fac_hi, fac_lo, h * broad, k * rows, f_recv.at[k, h])
            out = 0.0
            for h in range(per):
                take(recv_sem.at[YE + h], half * half * block)
                x = [erecv[0, h * half + k] + erecv[1, h * half + k] for k in range(half)]
                at = slice(h * broad, (h + 1) * broad)
                out = out + times([x], fac_hi[at], fac_lo[at])
            for k in range(2):
                yrecv[0, k] = ybuf[k] - out[:, k * rows:(k + 1) * rows]
            gsend[0, :, :nb] = jnp.concatenate([out[:, span:], out[:nvec, span:]], 0)

            @when(main)
            def _():
                w = [[yrecv[0, 0]], [yrecv[0, 1]]]
                more = times(w, up_hi[:, :width + nb], up_lo[:, :width + nb])
                first = wide(gsend[0, :block, :nb] + more[:, width:])
                for k in range(share):
                    if k == half:
                        more = times(w, up_hi[:, gap:], up_lo[:, gap:])
                    gsend[k, block:] = first
                    gsend[k, :block] = more[:, (k % half) * rows:(k % half + 1) * rows]
                    for cc in (range(C) if k != 1 else range(C - 1, -1, -1)):
                        if k < half or cc != lead:
                            z_copy(k * C + cc).start()
                        else:
                            @when(p != k)
                            def _():
                                z_copy(k * C + cc).start()

            each(share * C, R * C, lambda i: f_copy(i).start())
            xrecv[y] = gsend[p]
            end_from_side()

        @when(jnp.logical_not(hub))
        def _():
            end_from_side()

    @when(jnp.logical_not(hub))
    def _():
        take(recv_sem.at[XS], 2 * wave)

    for i in range(2):
        @when(hub & (t == i))
        def _():
            take(recv_sem.at[XS], wave + i * nvec)

    total = xrecv[0] + xrecv[1]
    ends = product(total[block:], end_hi[...], end_lo[...], dot_nn)
    coefficients[0] = ends[:, :nb]
    coefficients[1] = ends[:, nb:2 * nb]
    projected[0] = total[:nvec] - ends[:, 2 * nb:2 * nb + rows]
    projected[1] = total[nvec:block] - ends[:, 2 * nb + rows:]

    def sent(cond, count, way=0):
        @when(cond)
        def _():
            take(send_sem.at[way], count)

    others = share * C - 1
    sent(main & (t == 0) & (z == 0), half * 2 * block + bas + ups + fac // 2)
    sent(hub & (t == 0), (half - 1) * 2 * block + 2 * bas + share * 2 * block)
    sent(hub & (t == 0), others * wave + share * C * nvec, 1)
    sent(main & (t == 1) & (z == 1), half * 2 * block + bas + ups // 2)
    sent(hub & (t == 1), (half - 1) * 2 * block + bas + half * share * block + others * block)
    sent(side & (t == 0), (steps + C - 1) * gram)
    sent(side & (t == 1), (steps + C - 1) * gram + fac)
    sent(far, fac)
    sent(aid, ups // 2)


def hub_call(R, C, factor, lower, upper, krylov, basis):
    tile, rows = lower.shape[1], lower.shape[2]
    width = factor.shape[2]
    nvec, nb = krylov.shape[1], basis.shape[1]
    share, per = tile // rows, tile // width
    half = share // 2
    steps = R.bit_length() - 1
    dma = pltpu.SemaphoreType.DMA
    vmem = pl.BlockSpec(memory_space=pltpu.VMEM)
    block = (2 * nvec, rows)
    f32 = lambda *shape: pltpu.VMEM(shape, F32)
    bf16 = lambda *shape: [pltpu.VMEM(shape, BF16)] * 2
    return pl.pallas_call(
        functools.partial(hub_kernel, R, C),
        out_shape=(pltpu.VMEM(krylov.shape, F32), pltpu.VMEM((2, nvec, nb), F32)),
        in_specs=[pl.BlockSpec(memory_space=pl.ANY)] * 5,
        out_specs=(vmem, vmem),
        scratch_shapes=[
            f32(*factor.shape), f32(2, tile + nvec, rows), f32(*upper.shape), f32(*basis.shape),
            f32(*upper.shape), f32(2, per, *factor.shape),
            *bf16(tile, 2 * rows), *bf16(4 * rows, tile + rows), *bf16(2 * tile, 2 * rows + nb), *bf16(2 * rows, tile),
            *bf16(2 * nb, 2 * rows), *bf16(2 * nb, 2 * nb + 2 * rows),
            f32(share, *basis.shape), f32(2, *basis.shape),
            f32(half, 2, *block), f32(share, 2, *block), f32(2, *block), f32(half, 2, *block),
            f32(half, 2, *block), f32(share, 2, *block), f32(share, *block), f32(2, share, *block),
            f32(share, 3 * nvec, rows), f32(half, 3 * nvec, rows),
            f32(steps + 1, nb, 2 * nb), f32(steps + 1, nb, 2 * nb),
            dma((4,)), dma((2,)), dma((9 + max(steps, 2 * per),)),
            pltpu.SemaphoreType.REGULAR, pltpu.SemaphoreType.REGULAR,
        ],
        compiler_params=pltpu.CompilerParams(collective_id=0, has_side_effects=True),
        name="krylov_hubs",
    )(factor, lower, upper, krylov, basis)


def finish(projected, turned, projected_out, turned_out, sems):
    copies = [
        pltpu.make_async_copy(projected, projected_out, sems.at[0]),
        pltpu.make_async_copy(turned, turned_out, sems.at[1]),
    ]
    for copy in copies:
        copy.start()
    for copy in copies:
        copy.wait()


def general_call(R, C, factor, lower, upper, krylov, basis):
    tile, rows = lower.shape[1], lower.shape[2]
    width = factor.shape[2]
    nvec, nb = krylov.shape[1], basis.shape[1]
    share, per, pieces = tile // rows, tile // width, width // rows
    steps = R.bit_length() - 1
    dma = pltpu.SemaphoreType.DMA
    vmem = pl.BlockSpec(memory_space=pltpu.VMEM)
    block = (2 * nvec, rows)
    return pl.pallas_call(
        functools.partial(kernel, R, C),
        out_shape=(
            jax.ShapeDtypeStruct(krylov.shape, F32),
            jax.ShapeDtypeStruct((2, nvec, nb), F32),
        ),
        in_specs=[vmem] * 5,
        out_specs=(vmem, vmem),
        scratch_shapes=[
            pltpu.VMEM((2, tile, 2 * rows), BF16),
            pltpu.VMEM((2, tile, 2 * rows), BF16),
            pltpu.VMEM((rows, 2 * width), BF16),
            pltpu.VMEM((rows, 2 * width), BF16),
            pltpu.VMEM((2 * nb, 2 * rows), BF16),
            pltpu.VMEM((2 * nb, 2 * rows), BF16),
            pltpu.VMEM((2 * nb, 2 * nb + 2 * rows), BF16),
            pltpu.VMEM((2 * nb, 2 * nb + 2 * rows), BF16),
            pltpu.VMEM((2 * nb, 2 * rows), BF16),
            pltpu.VMEM((2 * nb, 2 * rows), BF16),
            pltpu.VMEM((share, 2, nb, rows), F32),
            pltpu.VMEM((2, share) + block, F32),
            pltpu.VMEM((2, share) + block, F32),
            pltpu.VMEM(block, F32),
            pltpu.VMEM(block, F32),
            pltpu.VMEM((pieces,) + block, F32),
            pltpu.VMEM(block, F32),
            pltpu.VMEM((C,) + block, F32),
            pltpu.VMEM((nvec, 2 * nb), F32),
            pltpu.VMEM((R, nvec, 2 * nb), F32),
            pltpu.VMEM((steps + 1, nb, 2 * nb), F32),
            pltpu.VMEM((steps, nb, 2 * nb), F32),
            dma((2, share)),
            dma((2, share)),
            dma((R,)),
            dma((pieces,)),
            dma((C,)),
            dma((C,)),
            dma((C // per,)),
            dma((1,)),
            dma((R,)),
            dma((R,)),
            dma((steps,)),
            dma((steps,)),
            dma((share,)),
            dma((share,)),
            dma((C // per,)),
            dma((1,)),
            pltpu.SemaphoreType.REGULAR,
        ],
        compiler_params=pltpu.CompilerParams(collective_id=0, has_side_effects=True),
        name="krylov_step",
    )(factor, lower, upper, krylov, basis)


def local(R, C, factor, lower, upper, krylov, basis):
    tile, rows = lower.shape[1], lower.shape[2]
    share, per = tile // rows, tile // factor.shape[2]
    vmem = pl.BlockSpec(memory_space=pltpu.VMEM)
    paired = R == 2 * share and C == 2 * per and share == 4 and per == 2
    call = hub_call if paired else general_call
    projected, turned = call(R, C, factor, lower, upper, krylov, basis)
    if paired:
        projected, turned = [pltpu.with_memory_space_constraint(x, pltpu.VMEM) for x in (projected, turned)]
    projected, turned = pl.pallas_call(
        finish,
        out_shape=(jax.ShapeDtypeStruct(projected.shape, F32), jax.ShapeDtypeStruct(turned.shape, F32)),
        in_specs=[vmem] * 2,
        out_specs=[pl.BlockSpec(memory_space=pl.ANY)] * 2,
        scratch_shapes=[pltpu.SemaphoreType.DMA((2,))],
        name="finish",
    )(projected, turned)
    return projected, turned.transpose(0, 2, 1)


def solution(mesh):
    in_specs = (
        P(None, "row", "col"),
        P(None, None, "row"),
        P(None, None, "row"),
        P(None, None, "row"),
        P(None, None, "row"),
    )
    out_specs = (P(None, None, "row"), P())
    body = functools.partial(local, mesh.shape["row"], mesh.shape["col"])
    return jax.shard_map(body, mesh=mesh, in_specs=in_specs, out_specs=out_specs, check_vma=False)
```
